32 devices in a mesh: dp: 8 (over z, y), col: 4 (over x, core).
Axes of the slice: x: 2, y: 2, z: 4, core: 2. Of those that a mesh axis runs over, the one named last changes fastest.
Arguments:
- tokens: bfloat16 [8192, 8192], P('dp', 'col'), may hold values from -6 to 6
- out_grad: bfloat16 [8192, 8192], P(('dp', 'col')), may hold values from -6 to 6
- weight: float32 [8192, 8192], P('dp', 'col'), may hold values from -6 to 6
- second: float32 [8192, 8192], P('dp', 'col'), may hold values from 0.0001 to 0.001
- momentum: float32 [8192, 512], P(('dp', 'col')), may hold values from -0.12 to 0.12
- sign_seed: int32 [1], replicated, may hold values from 0 to 999999
- step_number: int32 [1], replicated, may hold values from 1 to 999999
Outputs:
- new_weight: float32 [8192, 8192], P('dp', 'col')
- new_second: float32 [8192, 8192], P('dp', 'col')
- new_momentum: float32 [8192, 512], P(('dp', 'col'))
The draws below stay inside these ranges and needn't reach their ends.
All inputs are finite; a program needn't handle non-finite values.
Results may differ from the reference program's by a relative error of at most 0.00097.
Values may be sent and summed in bfloat16 or wider, within the bound.
No kernel may reach another device: no remote copies, remote signals or barrier semaphores. Data moves between devices by JAX's collectives and lax.ppermute only.
A program may use at most 128 MiB of HBM per device.

```python
import math
import jax
import jax.numpy as jnp
from jax import lax

DOUT = 8192
DIN = 8192
RANK = 512
TOKENS = 8192


def strengthened(drawn, key, source, target, parts, factor):
    def block_of(axis_at):
        return (jnp.arange(drawn.shape[axis_at]) // (drawn.shape[axis_at] // parts)).reshape((-1,) + (1,) * (drawn.ndim - 1 - axis_at))

    near = jax.random.permutation(key, parts)[block_of(target)]
    second = (block_of(target) + parts // 2) % parts
    return jnp.where((block_of(source) == near) | (block_of(source) == second), factor * drawn, drawn)


def shard_levels(key, extent, cuts, low, top_value):
    def one(axis_at, shards_of):
        steps = jax.random.uniform(jax.random.fold_in(jax.random.fold_in(key, 6), axis_at), (shards_of,), jnp.float32, low / len(cuts), top_value / len(cuts))
        return jnp.repeat(jnp.exp(steps), extent[axis_at] // shards_of).reshape((-1,) + (1,) * (len(extent) - axis_at - 1))

    factor_of = one(*cuts[0])
    for cut in cuts[1:]:
        factor_of = factor_of * one(*cut)
    return factor_of


def normal_values(own_key, dims, spread, most, cuts=(), dtype=jnp.bfloat16):
    values = jax.random.normal(own_key, dims, jnp.float32) * spread
    if len(cuts) > 0:
        values = shard_levels(own_key, dims, cuts, -0.22, 0.18) * values
    return jnp.clip(values, min=-most, max=most).astype(dtype)


def heavy_noise(key, extent, deviation, reach, split, heavy, dtype=jnp.bfloat16):
    array = deviation * jax.random.normal(key, extent, jnp.float32)
    if split:
        array = array * shard_levels(key, extent, split, -0.22, 0.18)
    return jnp.clip(strengthened(array, jax.random.fold_in(key, 3), *heavy), -reach, reach).astype(dtype)


def setup_inputs(seed: int = 0) -> dict:
    keys = jax.random.split(jax.random.key(seed), 8)
    return {
        "tokens": normal_values(keys[0], (TOKENS, DIN), 1.0, 6.0, ((0, 8), (1, 4))),
        "out_grad": heavy_noise(keys[1], (TOKENS, DOUT), 1.0, 6.0, ((0, 32),), (0, 1, 32, 2.75)),
        "weight": normal_values(keys[2], (DOUT, DIN), 1.0, 6.0, ((0, 8), (1, 4)), jnp.float32),
        "second": jnp.clip(jnp.exp(math.log(0.001) - 2.3025852 * jax.random.uniform(keys[3], (DOUT, DIN), jnp.float32) ** shard_levels(keys[3], (DOUT, DIN), ((0, 8), (1, 4)), -0.2, 0.2)), 0.0001, 0.001),
        "momentum": normal_values(keys[4], (DOUT, RANK), 0.02, 0.12, ((0, 32),), jnp.float32),
        "sign_seed": jax.random.randint(keys[5], (1,), 0, 1000000).astype(jnp.int32),
        "step_number": jax.random.randint(keys[6], (1,), 1, 1000000).astype(jnp.int32),
    }


def sign_table(sign_seed, step_number, first_row, row_count, low_rank):
    row_ids = first_row + lax.iota(jnp.int32, row_count)
    col_ids = lax.iota(jnp.int32, low_rank)
    flat_index = row_ids[:, None] * low_rank + col_ids[None, :]
    hashed = flat_index * 747796405 + sign_seed[0] * 1664525 + step_number[0] * 1013904223
    hashed = hashed ^ hashed >> 16 & 65535
    hashed = hashed * 2127912213
    hashed = hashed ^ hashed >> 13 & 524287
    hashed = hashed * 1103515245
    hashed = hashed ^ hashed >> 16 & 65535
    low_bit = hashed >> 20 & 1
    return (1 - 2 * low_bit).astype(jnp.float32)

def reference(tokens, out_grad, weight, second, momentum, sign_seed, step_number):
    inv_root = 1.0 / jnp.sqrt(jnp.float32(RANK))
    sign_block = sign_table(sign_seed, step_number, 0, DIN, RANK)
    sketch = jnp.dot(tokens.astype(jnp.float32), sign_block, preferred_element_type=jnp.float32) * inv_root
    sketch = sketch.astype(jnp.bfloat16)
    projected = lax.dot_general(out_grad.astype(jnp.float32), sketch.astype(jnp.float32), (((0,), (0,)), ((), ())), preferred_element_type=jnp.float32)
    projected = projected / jnp.float32(TOKENS)
    new_momentum = 0.8 * momentum + 0.2 * projected
    dense_grad = lax.dot_general(new_momentum, sign_block, (((1,), (1,)), ((), ())), precision=lax.Precision.HIGHEST, preferred_element_type=jnp.float32) * inv_root
    new_second = 0.95 * second + 0.05 * dense_grad * dense_grad
    new_weight = weight - 0.5 * dense_grad / (jnp.sqrt(new_second) + 1e-08)
    return (new_weight, new_second, new_momentum)
```

```python
import functools

import jax
import jax.numpy as jnp
from jax import lax
from jax.experimental import pallas as pl
from jax.experimental.pallas import tpu as pltpu
from jax.sharding import PartitionSpec as P

AXES = ("dp", "col")
LANES = 128


def hashed_signs(flat_scaled, sign_seed, step_number):
    hashed = flat_scaled + sign_seed * 1664525 + step_number * 1013904223
    hashed = hashed ^ hashed >> 16 & 65535
    hashed = hashed * 2127912213
    hashed = hashed ^ hashed >> 13 & 524287
    hashed = hashed * 1103515245
    hashed = hashed ^ hashed >> 16 & 65535
    return hashed >> 20 & 1


def sign_table(sign_seed, step_number, first_row, row_count, low_rank):
    row_ids = first_row + lax.iota(jnp.int32, row_count)
    col_ids = lax.iota(jnp.int32, low_rank)
    flat_index = row_ids[:, None] * low_rank + col_ids[None, :]
    low_bit = hashed_signs(flat_index * 747796405, sign_seed[0], step_number[0])
    return (1 - 2 * low_bit).astype(jnp.float32)


def contract(left_rows, right_rows):
    return lax.dot_general(
        left_rows, right_rows, (((0,), (0,)), ((), ())), preferred_element_type=jnp.float32
    )


def general(tokens, out_grad, weight, second, momentum, sign_seed, step_number):
    local_tokens, din_local = tokens.shape
    low_rank = momentum.shape[1]
    owner_rows = momentum.shape[0]
    inv_root = 1.0 / jnp.sqrt(jnp.float32(low_rank))
    col_position = lax.axis_index("col")
    sign_block = sign_table(sign_seed, step_number, col_position * din_local, din_local, low_rank)
    partial_sketch = (
        jnp.dot(tokens, sign_block.astype(jnp.bfloat16), preferred_element_type=jnp.float32)
        * inv_root
    )
    quarter = lax.psum_scatter(partial_sketch, "col", scatter_dimension=0, tiled=True)
    sketch = quarter.astype(jnp.bfloat16)
    total_tokens = lax.axis_size("dp") * local_tokens
    data_count = lax.axis_size("dp")
    col_count = lax.axis_size("col")
    quarter_rows = out_grad.shape[0]
    grouped = out_grad.reshape(quarter_rows, data_count, col_count, owner_rows)
    grouped = jnp.transpose(grouped, (0, 2, 1, 3)).reshape(
        quarter_rows, col_count, data_count * owner_rows
    )
    regrouped = lax.all_to_all(grouped, "col", split_axis=1, concat_axis=0, tiled=True)
    regrouped = regrouped.reshape(quarter_rows * col_count, data_count * owner_rows)
    shard_sketch = lax.all_gather(sketch, "col", axis=0, tiled=True)
    projected = lax.psum_scatter(
        contract(regrouped, shard_sketch), "dp", scatter_dimension=0, tiled=True
    )
    projected = projected / jnp.float32(total_tokens)
    new_momentum = 0.8 * momentum + 0.2 * projected
    row_block = lax.all_gather(new_momentum, "col", axis=0, tiled=True)
    dense_grad = (
        lax.dot_general(
            row_block,
            sign_block,
            (((1,), (1,)), ((), ())),
            precision=lax.Precision.HIGHEST,
            preferred_element_type=jnp.float32,
        )
        * inv_root
    )
    new_second = 0.95 * second + 0.05 * dense_grad * dense_grad
    new_weight = weight - 0.5 * dense_grad / (jnp.sqrt(new_second) + 1e-08)
    return (new_weight, new_second, new_momentum)


def params(vmem=56 * 1024 * 1024, axes=1):
    return pltpu.CompilerParams(
        dimension_semantics=("arbitrary",) * axes, vmem_limit_bytes=vmem
    )


def pack_kernel(groups, width, og_ref, *refs):
    n_out = len(groups)
    outs = refs[:n_out]
    stage, in_sem, out_sem = refs[n_out:]
    me = lax.axis_index("dp") * lax.axis_size("col") + lax.axis_index("col")
    loads = []
    slot = 0
    for group in groups:
        mine = []
        for rel in group:
            first = pl.multiple_of((me ^ rel) * width, width)
            copy = pltpu.make_async_copy(
                og_ref.at[:, pl.ds(first, width)], stage.at[slot], in_sem.at[slot]
            )
            copy.start()
            mine.append(copy)
            slot += 1
        loads.append(mine)
    stores = []
    slot = 0
    for index, group in enumerate(groups):
        for copy in loads[index]:
            copy.wait()
        store = pltpu.make_async_copy(
            stage.at[pl.ds(slot, len(group))], outs[index], out_sem.at[index]
        )
        store.start()
        stores.append(store)
        slot += len(group)
    for store in stores:
        store.wait()


def pack(out_grad, groups, width):
    rows = out_grad.shape[0]
    count = sum(len(group) for group in groups)
    return pl.pallas_call(
        functools.partial(pack_kernel, groups, width),
        in_specs=[pl.BlockSpec(memory_space=pl.ANY)],
        out_specs=[pl.BlockSpec(memory_space=pl.ANY)] * len(groups),
        out_shape=[
            jax.ShapeDtypeStruct((len(group), rows, width), out_grad.dtype) for group in groups
        ],
        scratch_shapes=[
            pltpu.VMEM((count, rows, width), out_grad.dtype),
            pltpu.SemaphoreType.DMA((count,)),
            pltpu.SemaphoreType.DMA((len(groups),)),
        ],
        compiler_params=pltpu.CompilerParams(vmem_limit_bytes=24 * 1024 * 1024),
        cost_estimate=pl.CostEstimate(
            flops=0, bytes_accessed=4 * out_grad.size, transcendentals=0
        ),
        name="pack",
    )(out_grad)


def split_acc(place_ref, acc, send_ref, keep_ref):
    rows = keep_ref.shape[0]
    core = place_ref[0] & 1
    keep_ref[...] = acc[pl.ds(pl.multiple_of(core * rows, rows), rows), :]
    send_ref[...] = acc[pl.ds(pl.multiple_of((1 - core) * rows, rows), rows), :]


def sketch_first(steps, chunk, din_local, place_ref, tok_ref, signs_ref, send_ref, keep_ref, acc):
    step = pl.program_id(0)
    low_rank = signs_ref.shape[1]
    shape = (chunk, low_rank)
    first = place_ref[0] * din_local + step * chunk
    flat = (first + lax.broadcasted_iota(jnp.int32, shape, 0)) * low_rank
    flat = flat + lax.broadcasted_iota(jnp.int32, shape, 1)
    low_bit = hashed_signs(flat * 747796405, place_ref[1], place_ref[2])
    signs = jnp.where(low_bit == 1, -1.0, 1.0).astype(jnp.bfloat16)
    signs_ref[...] = signs
    part = jnp.dot(tok_ref[...], signs, preferred_element_type=jnp.float32)

    @pl.when(step == 0)
    def _():
        acc[...] = part

    @pl.when(step > 0)
    def _():
        acc[...] += part

    @pl.when(step == steps - 1)
    def _():
        split_acc(place_ref, acc, send_ref, keep_ref)


def sketch_next(steps, place_ref, tok_ref, signs_ref, send_ref, keep_ref, acc):
    step = pl.program_id(0)
    part = jnp.dot(tok_ref[...], signs_ref[...], preferred_element_type=jnp.float32)

    @pl.when(step == 0)
    def _():
        acc[...] = part

    @pl.when(step > 0)
    def _():
        acc[...] += part

    @pl.when(step == steps - 1)
    def _():
        split_acc(place_ref, acc, send_ref, keep_ref)


def sketch_parts(place, tokens, low_rank, signs):
    local_tokens, din_local = tokens.shape
    chunk = din_local // 4
    steps = din_local // chunk
    half = local_tokens // 2
    quarter = half // 2
    first = signs is None
    tok_spec = pl.BlockSpec(
        (half, chunk), lambda i, p: ((p[0] >> 1) ^ (1 if first else 0), i)
    )
    sign_spec = pl.BlockSpec((chunk, low_rank), lambda i, p: (i, 0))
    part_spec = pl.BlockSpec((quarter, low_rank), lambda i, p: (0, 0))
    parts = [jax.ShapeDtypeStruct((quarter, low_rank), jnp.float32)] * 2
    if first:
        body = functools.partial(sketch_first, steps, chunk, din_local)
        in_specs, args = [tok_spec], (tokens,)
        out_specs = [sign_spec, part_spec, part_spec]
        out_shape = [jax.ShapeDtypeStruct((din_local, low_rank), jnp.bfloat16)] + parts
    else:
        body = functools.partial(sketch_next, steps)
        in_specs, args = [tok_spec, sign_spec], (tokens, signs)
        out_specs = [part_spec, part_spec]
        out_shape = parts
    return pl.pallas_call(
        body,
        grid_spec=pltpu.PrefetchScalarGridSpec(
            num_scalar_prefetch=1,
            grid=(steps,),
            in_specs=in_specs,
            out_specs=out_specs,
            scratch_shapes=[pltpu.VMEM((half, low_rank), jnp.float32)],
        ),
        out_shape=out_shape,
        compiler_params=params(24 * 1024 * 1024),
        cost_estimate=pl.CostEstimate(
            flops=2 * half * din_local * low_rank,
            bytes_accessed=half * din_local * 2 + din_local * low_rank * 2 + 2 * half * low_rank * 4,
            transcendentals=0,
        ),
        name="sketch_first" if first else "sketch_next",
    )(place, *args)


def project_kernel(n, *refs):
    out_ref = refs[-1]
    total = None
    for sk_ref, og_ref in zip(refs[:n], refs[n : 2 * n]):
        part = lax.dot_general(
            sk_ref[...],
            og_ref[0],
            (((0,), (0,)), ((), ())),
            preferred_element_type=jnp.float32,
        )
        total = part if total is None else total + part
    out_ref[0] = total


def project(sketches, grads, offsets, count):
    rows, low_rank = sketches[0].shape
    width = grads[0].shape[2]
    n = len(sketches)

    def block_at(offset):
        return pl.BlockSpec((1, rows, width), lambda j: (j + offset, 0, 0))

    return pl.pallas_call(
        functools.partial(project_kernel, n),
        grid=(count,),
        in_specs=[pl.BlockSpec((rows, low_rank), lambda j: (0, 0))] * n
        + [block_at(offset) for offset in offsets],
        out_specs=pl.BlockSpec((1, low_rank, width), lambda j: (j, 0, 0)),
        out_shape=jax.ShapeDtypeStruct((count, low_rank, width), jnp.float32),
        compiler_params=params(24 * 1024 * 1024),
        cost_estimate=pl.CostEstimate(
            flops=2 * n * count * rows * width * low_rank,
            bytes_accessed=n * (rows * low_rank + count * rows * width) * 2
            + count * low_rank * width * 4,
            transcendentals=0,
        ),
        name="project",
    )(*sketches, *grads)


def update_kernel(n, place_ref, *refs):
    rows_refs = refs[:n]
    signs_ref, weight_ref, second_ref = refs[n : n + 3]
    new_weight_ref, new_second_ref = refs[-2:]
    which = pl.program_id(1)
    rows = rows_refs[0][...]
    for index in range(1, n):
        rows = jnp.where(which == index, rows_refs[index][...], rows)
    low_rank = rows.shape[1]
    inv_root = 1.0 / jnp.sqrt(jnp.full((1, 1), low_rank, jnp.float32))
    high = rows.astype(jnp.bfloat16)
    low = (rows - high.astype(jnp.float32)).astype(jnp.bfloat16)
    signs = signs_ref[...]
    nt = (((1,), (1,)), ((), ()))
    dense_grad = lax.dot_general(high, signs, nt, preferred_element_type=jnp.float32)
    dense_grad += lax.dot_general(low, signs, nt, preferred_element_type=jnp.float32)
    dense_grad = dense_grad * inv_root
    new_second = 0.95 * second_ref[...] + 0.05 * dense_grad * dense_grad
    new_second_ref[...] = new_second
    new_weight_ref[...] = weight_ref[...] - 0.5 * dense_grad / (jnp.sqrt(new_second) + 1e-08)


def update(place, row_blocks, relatives, signs, weight, second, onto):
    rows, low_rank = row_blocks[0].shape
    din_local = weight.shape[1]
    chunk = din_local // 4
    n = len(row_blocks)
    base = relatives[0]
    tile = pl.BlockSpec((rows, chunk), lambda i, j, p: (p[0] ^ base ^ j, i))
    in_specs = [pl.BlockSpec((rows, low_rank), lambda i, j, p: (0, 0))] * n + [
        pl.BlockSpec((chunk, low_rank), lambda i, j, p: (i, 0)),
        tile,
        tile,
    ]
    aliases = {}
    if onto:
        in_specs += [pl.BlockSpec(memory_space=pl.ANY)] * 2
        aliases = {n + 4: 0, n + 5: 1}
    size = n * rows * din_local
    return pl.pallas_call(
        functools.partial(update_kernel, n),
        grid_spec=pltpu.PrefetchScalarGridSpec(
            num_scalar_prefetch=1,
            grid=(din_local // chunk, n),
            in_specs=in_specs,
            out_specs=[tile, tile],
        ),
        out_shape=[
            jax.ShapeDtypeStruct(weight.shape, jnp.float32),
            jax.ShapeDtypeStruct(second.shape, jnp.float32),
        ],
        input_output_aliases=aliases,
        compiler_params=params(32 * 1024 * 1024, 2),
        cost_estimate=pl.CostEstimate(
            flops=4 * size * low_rank, bytes_accessed=16 * size, transcendentals=2 * size
        ),
        name="update",
    )(place, *row_blocks, signs, weight, second, *onto)


CORE, X, Y, Z0, Z1 = 1, 2, 4, 8, 16


def exchange(value, mask):
    size = lax.axis_size("dp") * lax.axis_size("col")
    return lax.ppermute(value, AXES, [(i, i ^ mask) for i in range(size)])


def stepped(tokens, out_grad, weight, second, momentum, sign_seed, step_number):
    low_rank = momentum.shape[1]
    owner_rows = momentum.shape[0]
    total_tokens = lax.axis_size("dp") * tokens.shape[0]
    inv_root = 1.0 / jnp.sqrt(jnp.float32(low_rank))
    place = jnp.stack(
        [lax.axis_index("col").astype(jnp.int32), sign_seed[0], step_number[0]]
    )

    far = [Z1 | X | Z0, Z1 | X, Z1 | Z0, Z1]
    near = [Y | X, Y, X, 0]
    signs, send_a, keep_a = sketch_parts(place, tokens, low_rank, None)
    groups = [
        [o ^ Y for o in far],
        [o ^ Z0 for o in near],
        [o ^ Y ^ CORE for o in far],
        [o ^ Z0 ^ CORE for o in near],
        [o ^ CORE for o in far + near],
        far + near,
    ]
    og_y, og_z, og_yc, og_zc, og_c, og_own = pack(out_grad, groups, owner_rows)
    got_a = exchange(send_a, CORE)
    og_y = exchange(og_y, Y)
    og_z = exchange(og_z, Z0)
    og_yc = exchange(og_yc, Y | CORE)
    og_zc = exchange(og_zc, Z0 | CORE)
    og_c = exchange(og_c, CORE)
    across = exchange(keep_a + got_a, X)
    send_b, keep_b = sketch_parts(place, tokens, low_rank, signs)
    got_b = exchange(send_b, CORE)
    sketch = (((keep_b + got_b) + across) * inv_root).astype(jnp.bfloat16)

    sk_y = exchange(sketch, Y)
    sk_z = exchange(sketch, Z0)
    sk_c = exchange(sketch, CORE)
    sk_yc = exchange(sk_y, CORE)
    sk_zc = exchange(sk_z, CORE)

    scale = jnp.float32(1.0 / total_tokens)

    def packed(value, extra):
        return (value * (scale * extra)).astype(jnp.float16)

    def unpacked(value, extra):
        return value.astype(jnp.float32) * (1.0 / (scale * extra))

    sum_far = project((sketch, sk_c, sk_y, sk_yc), (og_own, og_c, og_y, og_yc), (0, 0, 0, 0), 4)
    got_far = exchange(packed(sum_far[:2], 8.0), X)
    sum_near = project((sketch, sk_c, sk_z, sk_zc), (og_own, og_c, og_z, og_zc), (4, 4, 0, 0), 4)
    got_near = exchange(packed(sum_near[:2], 8.0), Y)
    got_far2 = exchange(packed(sum_far[2] + unpacked(got_far[0], 8.0), 4.0), Z0)
    got_near2 = exchange(packed(sum_near[2] + unpacked(got_near[0], 8.0), 4.0), X)
    far_total = sum_far[3] + unpacked(got_far[1], 8.0) + unpacked(got_far2, 4.0)
    got_last = exchange(packed(far_total, 2.0), Z1)
    near_total = sum_near[3] + unpacked(got_near[1], 8.0) + unpacked(got_near2, 4.0)
    projected = (near_total + unpacked(got_last, 2.0)) * scale
    new_momentum = 0.8 * momentum + 0.2 * projected.T

    halved = new_momentum.astype(jnp.float16)
    nm_c = exchange(halved, CORE)
    nm_x = exchange(halved, X)
    nm_xc = exchange(nm_x, CORE)
    near_rows = (new_momentum, nm_c.astype(jnp.float32))
    far_rows = (nm_x.astype(jnp.float32), nm_xc.astype(jnp.float32))
    half_done = update(place, near_rows, (0, CORE), signs, weight, second, ())
    new_weight, new_second = update(
        place, far_rows, (X, X | CORE), signs, weight, second, tuple(half_done)
    )
    return (new_weight, new_second, new_momentum)


def solution(mesh):
    placed = (
        P("dp", "col"),
        P(AXES, None),
        P("dp", "col"),
        P("dp", "col"),
        P(AXES, None),
        P(),
        P(),
    )

    def per_device(tokens, out_grad, weight, second, momentum, sign_seed, step_number):
        args = (tokens, out_grad, weight, second, momentum, sign_seed, step_number)
        cube = mesh.shape["dp"] == Z1 * 2 // (X * 2) and mesh.shape["col"] == X * 2
        if cube and momentum.shape[0] % LANES == 0:
            return stepped(*args)
        return general(*args)

    return jax.shard_map(
        per_device,
        mesh=mesh,
        in_specs=placed,
        out_specs=(P("dp", "col"), P("dp", "col"), P(AXES, None)),
        check_vma=False,
    )
```

```python
import functools

import jax
import jax.numpy as jnp
from jax import lax
from jax.experimental import pallas as pl
from jax.experimental.pallas import tpu as pltpu
from jax.sharding import PartitionSpec as P


AXES = ("dp", "col")
LANES = 128


def hashed_signs(flat_scaled, sign_seed, step_number):
    hashed = flat_scaled + sign_seed * 1664525 + step_number * 1013904223
    hashed = hashed ^ hashed >> 16 & 65535
    hashed = hashed * 2127912213
    hashed = hashed ^ hashed >> 13 & 524287
    hashed = hashed * 1103515245
    hashed = hashed ^ hashed >> 16 & 65535
    return hashed >> 20 & 1


def sign_table(sign_seed, step_number, first_row, row_count, low_rank):
    row_ids = first_row + lax.iota(jnp.int32, row_count)
    col_ids = lax.iota(jnp.int32, low_rank)
    flat_index = row_ids[:, None] * low_rank + col_ids[None, :]
    low_bit = hashed_signs(flat_index * 747796405, sign_seed[0], step_number[0])
    return (1 - 2 * low_bit).astype(jnp.float32)


def contract(left_rows, right_rows):
    return lax.dot_general(
        left_rows, right_rows, (((0,), (0,)), ((), ())), preferred_element_type=jnp.float32
    )


def general(tokens, out_grad, weight, second, momentum, sign_seed, step_number):
    local_tokens, din_local = tokens.shape
    low_rank = momentum.shape[1]
    owner_rows = momentum.shape[0]
    inv_root = 1.0 / jnp.sqrt(jnp.float32(low_rank))
    col_position = lax.axis_index("col")
    sign_block = sign_table(sign_seed, step_number, col_position * din_local, din_local, low_rank)
    partial_sketch = (
        jnp.dot(tokens, sign_block.astype(jnp.bfloat16), preferred_element_type=jnp.float32)
        * inv_root
    )
    quarter = lax.psum_scatter(partial_sketch, "col", scatter_dimension=0, tiled=True)
    sketch = quarter.astype(jnp.bfloat16)
    total_tokens = lax.axis_size("dp") * local_tokens
    data_count = lax.axis_size("dp")
    col_count = lax.axis_size("col")
    quarter_rows = out_grad.shape[0]
    grouped = out_grad.reshape(quarter_rows, data_count, col_count, owner_rows)
    grouped = jnp.transpose(grouped, (0, 2, 1, 3)).reshape(
        quarter_rows, col_count, data_count * owner_rows
    )
    regrouped = lax.all_to_all(grouped, "col", split_axis=1, concat_axis=0, tiled=True)
    regrouped = regrouped.reshape(quarter_rows * col_count, data_count * owner_rows)
    shard_sketch = lax.all_gather(sketch, "col", axis=0, tiled=True)
    projected = lax.psum_scatter(
        contract(regrouped, shard_sketch), "dp", scatter_dimension=0, tiled=True
    )
    projected = projected / jnp.float32(total_tokens)
    new_momentum = 0.8 * momentum + 0.2 * projected
    row_block = lax.all_gather(new_momentum, "col", axis=0, tiled=True)
    dense_grad = (
        lax.dot_general(
            row_block,
            sign_block,
            (((1,), (1,)), ((), ())),
            precision=lax.Precision.HIGHEST,
            preferred_element_type=jnp.float32,
        )
        * inv_root
    )
    new_second = 0.95 * second + 0.05 * dense_grad * dense_grad
    new_weight = weight - 0.5 * dense_grad / (jnp.sqrt(new_second) + 1e-08)
    return (new_weight, new_second, new_momentum)


def params(vmem=56 * 1024 * 1024, axes=1):
    return pltpu.CompilerParams(
        dimension_semantics=("arbitrary",) * axes, vmem_limit_bytes=vmem
    )


def pack_kernel(groups, width, part, og_ref, *refs):
    n_out = len(groups)
    outs = refs[:n_out]
    stage, in_sem, out_sem = refs[n_out:]
    me = lax.axis_index("dp") * lax.axis_size("col") + lax.axis_index("col")
    loads = []
    slot = 0
    for group in groups:
        mine = []
        for rel, half in group:
            first = pl.multiple_of((me ^ rel) * width + half * part, part)
            copy = pltpu.make_async_copy(
                og_ref.at[:, pl.ds(first, part)], stage.at[slot], in_sem.at[slot]
            )
            copy.start()
            mine.append(copy)
            slot += 1
        loads.append(mine)
    stores = []
    slot = 0
    for index, group in enumerate(groups):
        for copy in loads[index]:
            copy.wait()
        store = pltpu.make_async_copy(
            stage.at[pl.ds(slot, len(group))], outs[index], out_sem.at[index]
        )
        store.start()
        stores.append(store)
        slot += len(group)
    for store in stores:
        store.wait()


def pack(out_grad, groups, width, part):
    rows = out_grad.shape[0]
    count = sum(len(group) for group in groups)
    return pl.pallas_call(
        functools.partial(pack_kernel, groups, width, part),
        in_specs=[pl.BlockSpec(memory_space=pl.ANY)],
        out_specs=[pl.BlockSpec(memory_space=pl.ANY)] * len(groups),
        out_shape=[
            jax.ShapeDtypeStruct((len(group), rows, part), out_grad.dtype) for group in groups
        ],
        scratch_shapes=[
            pltpu.VMEM((count, rows, part), out_grad.dtype),
            pltpu.SemaphoreType.DMA((count,)),
            pltpu.SemaphoreType.DMA((len(groups),)),
        ],
        compiler_params=pltpu.CompilerParams(vmem_limit_bytes=16 * 1024 * 1024),
        cost_estimate=pl.CostEstimate(
            flops=0, bytes_accessed=4 * count * rows * part, transcendentals=0
        ),
        name="pack",
    )(pltpu.with_memory_space_constraint(out_grad, pltpu.HBM))


def split_acc(place_ref, acc, send_ref, keep_ref):
    rows = keep_ref.shape[0]
    core = place_ref[0] & 1
    keep_ref[...] = acc[pl.ds(pl.multiple_of(core * rows, rows), rows), :]
    send_ref[...] = acc[pl.ds(pl.multiple_of((1 - core) * rows, rows), rows), :]


def sketch_first(steps, chunk, din_local, place_ref, tok_ref, signs_ref, send_ref, keep_ref, acc):
    step = pl.program_id(0)
    low_rank = signs_ref.shape[1]
    shape = (chunk, low_rank)
    first = place_ref[0] * din_local + step * chunk
    flat = (first + lax.broadcasted_iota(jnp.int32, shape, 0)) * low_rank
    flat = flat + lax.broadcasted_iota(jnp.int32, shape, 1)
    low_bit = hashed_signs(flat * 747796405, place_ref[1], place_ref[2])
    signs = jnp.where(low_bit == 1, -1.0, 1.0).astype(jnp.bfloat16)
    signs_ref[...] = signs
    part = jnp.dot(tok_ref[...], signs, preferred_element_type=jnp.float32)

    @pl.when(step == 0)
    def _():
        acc[...] = part

    @pl.when(step > 0)
    def _():
        acc[...] += part

    @pl.when(step == steps - 1)
    def _():
        split_acc(place_ref, acc, send_ref, keep_ref)


def sketch_next(steps, place_ref, tok_ref, signs_ref, send_ref, keep_ref, acc):
    step = pl.program_id(0)
    part = jnp.dot(tok_ref[...], signs_ref[...], preferred_element_type=jnp.float32)

    @pl.when(step == 0)
    def _():
        acc[...] = part

    @pl.when(step > 0)
    def _():
        acc[...] += part

    @pl.when(step == steps - 1)
    def _():
        split_acc(place_ref, acc, send_ref, keep_ref)


def sketch_parts(place, tokens, low_rank, signs):
    local_tokens, din_local = tokens.shape
    chunk = din_local // 4
    steps = din_local // chunk
    half = local_tokens // 2
    quarter = half // 2
    first = signs is None
    tok_spec = pl.BlockSpec(
        (half, chunk), lambda i, p: ((p[0] >> 1) ^ (1 if first else 0), i)
    )
    sign_spec = pl.BlockSpec((chunk, low_rank), lambda i, p: (i, 0))
    part_spec = pl.BlockSpec((quarter, low_rank), lambda i, p: (0, 0))
    parts = [jax.ShapeDtypeStruct((quarter, low_rank), jnp.float32)] * 2
    if first:
        body = functools.partial(sketch_first, steps, chunk, din_local)
        in_specs, args = [tok_spec], (tokens,)
        out_specs = [sign_spec, part_spec, part_spec]
        out_shape = [jax.ShapeDtypeStruct((din_local, low_rank), jnp.bfloat16)] + parts
    else:
        body = functools.partial(sketch_next, steps)
        in_specs, args = [tok_spec, sign_spec], (tokens, signs)
        out_specs = [part_spec, part_spec]
        out_shape = parts
    return pl.pallas_call(
        body,
        grid_spec=pltpu.PrefetchScalarGridSpec(
            num_scalar_prefetch=1,
            grid=(steps,),
            in_specs=in_specs,
            out_specs=out_specs,
            scratch_shapes=[pltpu.VMEM((half, low_rank), jnp.float32)],
        ),
        out_shape=out_shape,
        compiler_params=params(24 * 1024 * 1024),
        cost_estimate=pl.CostEstimate(
            flops=2 * half * din_local * low_rank,
            bytes_accessed=half * din_local * 2 + din_local * low_rank * 2 + 2 * half * low_rank * 4,
            transcendentals=0,
        ),
        name="sketch_first" if first else "sketch_next",
    )(place, *args)


def project_kernel(n, *refs):
    send_ref, keep_ref = refs[-2:]
    count, _, part = refs[n].shape
    sketch = jnp.concatenate([ref[...] for ref in refs[:n]], axis=0)
    grads = jnp.concatenate(
        [
            jnp.concatenate([ref[j] for j in range(count)], axis=1)
            for ref in refs[n : 2 * n]
        ],
        axis=0,
    )
    total = contract(grads, sketch)
    for j in range(count):
        out_ref = send_ref if j < count // 2 else keep_ref
        out_ref[j % (count // 2)] = total[j * part : (j + 1) * part]


def project(sketches, grads, offsets, count):
    rows, low_rank = sketches[0].shape
    part = grads[0].shape[2]
    n = len(sketches)

    def block_at(offset):
        return pl.BlockSpec((count, rows, part), lambda i: (offset // count, 0, 0))

    out = jax.ShapeDtypeStruct((count // 2, part, low_rank), jnp.float32)
    return pl.pallas_call(
        functools.partial(project_kernel, n),
        grid=(1,),
        in_specs=[pl.BlockSpec((rows, low_rank), lambda i: (0, 0))] * n
        + [block_at(offset) for offset in offsets],
        out_specs=[pl.BlockSpec((count // 2, part, low_rank), lambda i: (0, 0, 0))] * 2,
        out_shape=[out] * 2,
        compiler_params=params(16 * 1024 * 1024),
        cost_estimate=pl.CostEstimate(
            flops=2 * n * count * rows * part * low_rank,
            bytes_accessed=n * (rows * low_rank + count * rows * part) * 2
            + count * low_rank * part * 4,
            transcendentals=0,
        ),
        name="project",
    )(*sketches, *grads)


def update_kernel(relatives, half, place_ref, *refs):
    n = len(relatives)
    rows_refs = refs[:n]
    signs_ref, weight_ref, second_ref = refs[n : n + 3]
    new_weight_ref, new_second_ref, w_buf, s_buf, nw_buf, ns_buf, in_sem, out_sem = refs[-8:]
    part, low_rank = rows_refs[0].shape
    width = signs_ref.shape[0]
    chunk = width // 2
    inv_root = 1.0 / jnp.sqrt(jnp.full((1, 1), low_rank, jnp.float32))
    nt = (((1,), (1,)), ((), ()))
    tasks = []
    for index, rel in enumerate(relatives):
        first = pl.multiple_of(((place_ref[0] ^ rel) * 2 + half) * part, part)
        for at in range(0, width, chunk):
            slot = len(tasks)
            window = (pl.ds(first, part), pl.ds(at, chunk))
            loads = [
                pltpu.make_async_copy(weight_ref.at[window], w_buf.at[slot], in_sem.at[0, slot]),
                pltpu.make_async_copy(second_ref.at[window], s_buf.at[slot], in_sem.at[1, slot]),
            ]
            for load in loads:
                load.start()
            tasks.append((index, at, window, loads))
    stores = []
    for slot, (index, at, window, loads) in enumerate(tasks):
        rows = rows_refs[index][...]
        high = rows.astype(jnp.bfloat16)
        low = (rows - high.astype(jnp.float32)).astype(jnp.bfloat16)
        signs = signs_ref[at : at + chunk, :]
        dense_grad = lax.dot_general(high, signs, nt, preferred_element_type=jnp.float32)
        dense_grad += lax.dot_general(low, signs, nt, preferred_element_type=jnp.float32)
        dense_grad = dense_grad * inv_root
        for load in loads:
            load.wait()
        new_second = 0.95 * s_buf[slot] + 0.05 * dense_grad * dense_grad
        ns_buf[slot] = new_second
        nw_buf[slot] = w_buf[slot] - 0.5 * dense_grad / (jnp.sqrt(new_second) + 1e-08)
        for kind, (buf, ref) in enumerate(((nw_buf, new_weight_ref), (ns_buf, new_second_ref))):
            store = pltpu.make_async_copy(buf.at[slot], ref.at[window], out_sem.at[kind, slot])
            store.start()
            stores.append(store)
    for store in stores:
        store.wait()


def update(place, row_blocks, relatives, half, signs, weight, second, onto):
    part, low_rank = row_blocks[0].shape
    din_local = weight.shape[1]
    n = len(row_blocks)
    slots, chunk = 2 * n, din_local // 2
    hbm = pl.BlockSpec(memory_space=pl.ANY)
    vmem = pl.BlockSpec(memory_space=pltpu.VMEM)
    in_specs = [pl.BlockSpec(memory_space=pltpu.SMEM)] + [vmem] * (n + 1) + [hbm, hbm]
    aliases = {}
    if onto:
        in_specs += [hbm, hbm]
        aliases = {n + 4: 0, n + 5: 1}
    size = n * part * din_local
    buf = pltpu.VMEM((slots, part, chunk), jnp.float32)
    return pl.pallas_call(
        functools.partial(update_kernel, relatives, half),
        in_specs=in_specs,
        out_specs=[hbm, hbm],
        out_shape=[
            jax.ShapeDtypeStruct(weight.shape, jnp.float32),
            jax.ShapeDtypeStruct(second.shape, jnp.float32),
        ],
        scratch_shapes=[buf] * 4
        + [pltpu.SemaphoreType.DMA((2, slots)), pltpu.SemaphoreType.DMA((2, slots))],
        input_output_aliases=aliases,
        compiler_params=pltpu.CompilerParams(vmem_limit_bytes=24 * 1024 * 1024),
        cost_estimate=pl.CostEstimate(
            flops=4 * size * low_rank, bytes_accessed=16 * size, transcendentals=2 * size
        ),
        name="update",
    )(
        place,
        *row_blocks,
        signs,
        pltpu.with_memory_space_constraint(weight, pltpu.HBM),
        pltpu.with_memory_space_constraint(second, pltpu.HBM),
        *onto,
    )


CORE, X, Y, Z0, Z1 = 1, 2, 4, 8, 16


def exchange(value, mask):
    size = lax.axis_size("dp") * lax.axis_size("col")
    return lax.ppermute(value, AXES, [(i, i ^ mask) for i in range(size)])


def stepped(tokens, out_grad, weight, second, momentum, sign_seed, step_number):
    low_rank = momentum.shape[1]
    owner_rows = momentum.shape[0]
    total_tokens = lax.axis_size("dp") * tokens.shape[0]
    inv_root = 1.0 / jnp.sqrt(jnp.float32(low_rank))
    place = jnp.stack(
        [lax.axis_index("col").astype(jnp.int32), sign_seed[0], step_number[0]]
    )

    far0 = [(Z1 | X | Z0, 0), (Z1 | X, 0), (Z1 | Z0, 0), (Z1, 0)]
    near0 = [(Z0 | X, 0), (X, 0), (Z0, 0), (0, 0)]
    far1 = [(Z1 | Y | X, 1), (Z1 | Y, 1), (Z1 | X, 1), (Z1, 1)]
    near1 = [(Y | X, 1), (Y, 1), (X, 1), (0, 1)]

    def toward(mask, pieces):
        return [(rel ^ mask, half) for rel, half in pieces]

    part = owner_rows // 2
    over_y, over_z = far0 + near0, far1 + near1
    og_y, og_z = pack(out_grad, [toward(Y, over_y), toward(Z0, over_z)], owner_rows, part)
    og_y = exchange(og_y, Y)
    og_z = exchange(og_z, Z0)
    signs, send_a, keep_a = sketch_parts(place, tokens, low_rank, None)
    og_yc, og_zc, og_c, og_own = pack(
        out_grad,
        [
            toward(Y | CORE, over_y),
            toward(Z0 | CORE, over_z),
            toward(CORE, over_y + over_z),
            over_y + over_z,
        ],
        owner_rows,
        part,
    )
    got_a = exchange(send_a, CORE)
    across = exchange(keep_a + got_a, X)
    og_yc = exchange(og_yc, Y | CORE)
    og_zc = exchange(og_zc, Z0 | CORE)
    og_c = exchange(og_c, CORE)
    send_b, keep_b = sketch_parts(place, tokens, low_rank, signs)
    got_b = exchange(send_b, CORE)
    sketch = (((keep_b + got_b) + across) * inv_root).astype(jnp.bfloat16)

    sk_y = exchange(sketch, Y)
    sk_z = exchange(sketch, Z0)
    sk_c = exchange(sketch, CORE)
    sk_yc = exchange(sk_y, CORE)
    sk_zc = exchange(sk_z, CORE)

    scale = jnp.float32(1.0 / total_tokens)

    def packed(value, extra):
        return (value * (scale * extra)).astype(jnp.float16)

    def unpacked(value, extra):
        return value.astype(jnp.float32) * (1.0 / (scale * extra))

    y_side = (sketch, sk_c, sk_y, sk_yc), (og_own, og_c, og_y, og_yc)
    z_side = (sketch, sk_c, sk_z, sk_zc), (og_own, og_c, og_z, og_zc)

    def begin(side, offsets, axis):
        send, keep = project(*side, offsets, 4)
        return exchange(packed(send, 8.0), axis), keep

    def middle(state, axis):
        got, keep = state
        ahead = exchange(packed(keep[0] + unpacked(got[0], 8.0), 4.0), axis)
        return ahead, keep[1] + unpacked(got[1], 8.0)

    def finish(state):
        got, keep = state
        return keep + unpacked(got, 4.0)

    far0_state = begin(y_side, (0, 0, 0, 0), X)
    far1_state = begin(z_side, (8, 8, 0, 0), Y)
    near0_state = begin(y_side, (4, 4, 4, 4), X)
    near1_state = begin(z_side, (12, 12, 4, 4), Y)
    far0_state = middle(far0_state, Z0)
    far1_state = middle(far1_state, X)
    last0 = exchange(packed(finish(far0_state), 2.0), Z1)
    last1 = exchange(packed(finish(far1_state), 2.0), Z1)
    near0_state = middle(near0_state, Z0)
    near1_state = middle(near1_state, X)

    def momentum_half(half, near, last):
        projected = (near + unpacked(last, 2.0)) * scale
        return 0.8 * momentum[half * part : (half + 1) * part] + 0.2 * projected

    halves, pieces = [], []
    small = None
    for half, near_state, last in ((0, near0_state, last0), (1, near1_state, last1)):
        if small is not None:
            last, _ = lax.optimization_barrier((last, small))
        mine = momentum_half(half, finish(near_state), last)
        small = mine.astype(jnp.float16)
        from_core = exchange(small, CORE)
        from_x = exchange(small, X)
        from_xc = exchange(from_x, CORE)
        halves.append(mine)
        pieces.append([v.astype(jnp.float32) for v in (from_core, from_x, from_xc)])
    done = ()
    for half in (0, 1):
        rows = (halves[half], pieces[half][0])
        done = update(place, rows, (0, CORE), half, signs, weight, second, tuple(done))
    for half in (0, 1):
        rows = (pieces[half][1], pieces[half][2])
        done = update(place, rows, (X, X | CORE), half, signs, weight, second, tuple(done))
    return (done[0], done[1], jnp.concatenate(halves, axis=0))


def solution(mesh):
    placed = (
        P("dp", "col"),
        P(AXES, None),
        P("dp", "col"),
        P("dp", "col"),
        P(AXES, None),
        P(),
        P(),
    )

    def per_device(tokens, out_grad, weight, second, momentum, sign_seed, step_number):
        args = (tokens, out_grad, weight, second, momentum, sign_seed, step_number)
        cube = mesh.shape["dp"] == Z1 * 2 // (X * 2) and mesh.shape["col"] == X * 2
        if cube and momentum.shape[0] % (2 * LANES) == 0:
            return stepped(*args)
        return general(*args)

    return jax.shard_map(
        per_device,
        mesh=mesh,
        in_specs=placed,
        out_specs=(P("dp", "col"), P("dp", "col"), P(AXES, None)),
        check_vma=False,
    )
```

```python
import functools
import math

import jax
import jax.numpy as jnp
from jax import lax
from jax.experimental import pallas as pl
from jax.experimental.pallas import tpu as pltpu
from jax.sharding import PartitionSpec as P


AXES = ("dp", "col")
LANES = 128


def low_bits(mixed):
    mixed = mixed ^ lax.shift_right_logical(mixed, 16)
    mixed = mixed * 2127912213
    mixed = mixed ^ lax.shift_right_logical(mixed, 13)
    mixed = mixed * 1103515245
    mixed = mixed ^ lax.shift_right_logical(mixed, 16)
    return mixed & (1 << 20)


def sign_table(sign_seed, step_number, first_row, row_count, low_rank):
    row_ids = first_row + lax.iota(jnp.int32, row_count)
    col_ids = lax.iota(jnp.int32, low_rank)
    flat_index = row_ids[:, None] * low_rank + col_ids[None, :]
    seeded = sign_seed[0] * 1664525 + step_number[0] * 1013904223
    return jnp.where(low_bits(flat_index * 747796405 + seeded) == 0, 1.0, -1.0)


def contract(left_rows, right_rows):
    return lax.dot_general(
        left_rows, right_rows, (((0,), (0,)), ((), ())), preferred_element_type=jnp.float32
    )


def general(tokens, out_grad, weight, second, momentum, sign_seed, step_number):
    local_tokens, din_local = tokens.shape
    low_rank = momentum.shape[1]
    owner_rows = momentum.shape[0]
    inv_root = 1.0 / jnp.sqrt(jnp.float32(low_rank))
    col_position = lax.axis_index("col")
    sign_block = sign_table(sign_seed, step_number, col_position * din_local, din_local, low_rank)
    partial_sketch = (
        jnp.dot(tokens, sign_block.astype(jnp.bfloat16), preferred_element_type=jnp.float32)
        * inv_root
    )
    quarter = lax.psum_scatter(partial_sketch, "col", scatter_dimension=0, tiled=True)
    sketch = quarter.astype(jnp.bfloat16)
    total_tokens = lax.axis_size("dp") * local_tokens
    data_count = lax.axis_size("dp")
    col_count = lax.axis_size("col")
    quarter_rows = out_grad.shape[0]
    grouped = out_grad.reshape(quarter_rows, data_count, col_count, owner_rows)
    grouped = jnp.transpose(grouped, (0, 2, 1, 3)).reshape(
        quarter_rows, col_count, data_count * owner_rows
    )
    regrouped = lax.all_to_all(grouped, "col", split_axis=1, concat_axis=0, tiled=True)
    regrouped = regrouped.reshape(quarter_rows * col_count, data_count * owner_rows)
    shard_sketch = lax.all_gather(sketch, "col", axis=0, tiled=True)
    projected = lax.psum_scatter(
        contract(regrouped, shard_sketch), "dp", scatter_dimension=0, tiled=True
    )
    projected = projected / jnp.float32(total_tokens)
    new_momentum = 0.8 * momentum + 0.2 * projected
    row_block = lax.all_gather(new_momentum, "col", axis=0, tiled=True)
    dense_grad = (
        lax.dot_general(
            row_block,
            sign_block,
            (((1,), (1,)), ((), ())),
            precision=lax.Precision.HIGHEST,
            preferred_element_type=jnp.float32,
        )
        * inv_root
    )
    new_second = 0.95 * second + 0.05 * dense_grad * dense_grad
    new_weight = weight - 0.5 * dense_grad / (jnp.sqrt(new_second) + 1e-08)
    return (new_weight, new_second, new_momentum)


def params(vmem=56 * 1024 * 1024, axes=1):
    return pltpu.CompilerParams(
        dimension_semantics=("arbitrary",) * axes, vmem_limit_bytes=vmem
    )


def pack_kernel(groups, width, part, og_ref, *refs):
    n_out = len(groups)
    outs = refs[:n_out]
    stage, in_sem, out_sem = refs[n_out:]
    me = lax.axis_index("dp") * lax.axis_size("col") + lax.axis_index("col")
    loads = []
    slot = 0
    for group in groups:
        mine = []
        for rel, half in group:
            first = pl.multiple_of((me ^ rel) * width + half * part, part)
            copy = pltpu.make_async_copy(
                og_ref.at[:, pl.ds(first, part)], stage.at[slot], in_sem.at[slot]
            )
            copy.start()
            mine.append(copy)
            slot += 1
        loads.append(mine)
    stores = []
    slot = 0
    for index, group in enumerate(groups):
        for copy in loads[index]:
            copy.wait()
        store = pltpu.make_async_copy(
            stage.at[pl.ds(slot, len(group))], outs[index], out_sem.at[index]
        )
        store.start()
        stores.append(store)
        slot += len(group)
    for store in stores:
        store.wait()


def pack(out_grad, groups, width, part):
    rows = out_grad.shape[0]
    count = sum(len(group) for group in groups)
    return pl.pallas_call(
        functools.partial(pack_kernel, groups, width, part),
        in_specs=[pl.BlockSpec(memory_space=pl.ANY)],
        out_specs=[pl.BlockSpec(memory_space=pl.ANY)] * len(groups),
        out_shape=[
            jax.ShapeDtypeStruct((len(group), rows, part), out_grad.dtype) for group in groups
        ],
        scratch_shapes=[
            pltpu.VMEM((count, rows, part), out_grad.dtype),
            pltpu.SemaphoreType.DMA((count,)),
            pltpu.SemaphoreType.DMA((len(groups),)),
        ],
        compiler_params=pltpu.CompilerParams(vmem_limit_bytes=8 * 1024 * 1024),
        cost_estimate=pl.CostEstimate(
            flops=0, bytes_accessed=4 * count * rows * part, transcendentals=0
        ),
        name="pack",
    )(pltpu.with_memory_space_constraint(out_grad, pltpu.HBM))


CHUNKS = 4


def sketch_kernel(first, din_local, *refs):
    if first:
        seed_ref, step_ref, tok_ref, signs_ref, send_ref, keep_ref, tok, acc, sem = refs
    else:
        tok_ref, signs_ref, send_ref, keep_ref, tok, acc, sem = refs
    quarter, low_rank = keep_ref.shape
    chunk = din_local // CHUNKS
    col = lax.axis_index("col")
    group = col ^ (X if first else 0)
    loads = []
    for part in range(CHUNKS):
        at = pl.ds(part * chunk, chunk)
        mine = []
        for slot, rel in enumerate((CORE, 0)):
            rows = pl.ds(pl.multiple_of((group ^ rel) * quarter, quarter), quarter)
            copy = pltpu.make_async_copy(
                tok_ref.at[rows, at],
                tok.at[pl.ds(slot * quarter, quarter), at],
                sem.at[part, slot],
            )
            copy.start()
            mine.append(copy)
        loads.append(mine)
    if first:
        seeded = seed_ref[0] * 1664525 + step_ref[0] * 1013904223
        columns = lax.broadcasted_iota(jnp.int32, (1, low_rank), 1) * 747796405
    for part in range(CHUNKS):
        at = slice(part * chunk, (part + 1) * chunk)
        if first:
            ids = lax.broadcasted_iota(jnp.int32, (chunk, 1), 0)
            ids = (ids + (col * din_local + part * chunk)) * low_rank
            mixed = (ids * 747796405 + seeded) + columns
            signs = jnp.where(low_bits(mixed) == 0, 1.0, -1.0).astype(jnp.bfloat16)
            signs_ref[at, :] = signs
        else:
            signs = signs_ref[at, :]
        for copy in loads[part]:
            copy.wait()
        product = jnp.dot(tok[:, at], signs, preferred_element_type=jnp.float32)
        if part > 0:
            product += acc[...]
        if part < CHUNKS - 1:
            acc[...] = product
        else:
            send_ref[...] = product[:quarter]
            keep_ref[...] = product[quarter:]


def sketch_parts(tokens, low_rank, signs, seeds):
    local_tokens, din_local = tokens.shape
    half = local_tokens // 2
    quarter = half // 2
    first = signs is None
    vmem = pl.BlockSpec(memory_space=pltpu.VMEM)
    smem = pl.BlockSpec(memory_space=pltpu.SMEM)
    hbm = pl.BlockSpec(memory_space=pl.ANY)
    parts = [jax.ShapeDtypeStruct((quarter, low_rank), jnp.float32)] * 2
    tokens = pltpu.with_memory_space_constraint(tokens, pltpu.HBM)
    if first:
        in_specs, args = [smem, smem, hbm], (*seeds, tokens)
        out_shape = [jax.ShapeDtypeStruct((din_local, low_rank), jnp.bfloat16)] + parts
    else:
        in_specs, args = [hbm, vmem], (tokens, signs)
        out_shape = parts
    return pl.pallas_call(
        functools.partial(sketch_kernel, first, din_local),
        in_specs=in_specs,
        out_specs=[vmem] * len(out_shape),
        out_shape=out_shape,
        scratch_shapes=[
            pltpu.VMEM((half, din_local), tokens.dtype),
            pltpu.VMEM((half, low_rank), jnp.float32),
            pltpu.SemaphoreType.DMA((CHUNKS, 2)),
        ],
        compiler_params=pltpu.CompilerParams(vmem_limit_bytes=12 * 1024 * 1024),
        cost_estimate=pl.CostEstimate(
            flops=2 * half * din_local * low_rank,
            bytes_accessed=half * din_local * 2 + din_local * low_rank * 2 + 2 * half * low_rank * 4,
            transcendentals=0,
        ),
        name="sketch_first" if first else "sketch_next",
    )(*args)


def project_kernel(n, *refs):
    send_ref, keep_ref = refs[-2:]
    count, _, part = refs[n].shape
    sketch = jnp.concatenate([ref[...] for ref in refs[:n]], axis=0)
    grads = jnp.concatenate(
        [
            jnp.concatenate([ref[j] for j in range(count)], axis=1)
            for ref in refs[n : 2 * n]
        ],
        axis=0,
    )
    total = contract(grads, sketch)
    for j in range(count):
        out_ref = send_ref if j < count // 2 else keep_ref
        out_ref[j % (count // 2)] = total[j * part : (j + 1) * part]


def project(sketches, grads, offsets, count):
    rows, low_rank = sketches[0].shape
    part = grads[0].shape[2]
    n = len(sketches)

    def block_at(offset):
        return pl.BlockSpec((count, rows, part), lambda i: (offset // count, 0, 0))

    out = jax.ShapeDtypeStruct((count // 2, part, low_rank), jnp.float32)
    return pl.pallas_call(
        functools.partial(project_kernel, n),
        grid=(1,),
        in_specs=[pl.BlockSpec((rows, low_rank), lambda i: (0, 0))] * n
        + [block_at(offset) for offset in offsets],
        out_specs=[pl.BlockSpec((count // 2, part, low_rank), lambda i: (0, 0, 0))] * 2,
        out_shape=[out] * 2,
        compiler_params=params(10 * 1024 * 1024),
        cost_estimate=pl.CostEstimate(
            flops=2 * n * count * rows * part * low_rank,
            bytes_accessed=n * (rows * low_rank + count * rows * part) * 2
            + count * low_rank * part * 4,
            transcendentals=0,
        ),
        name="project",
    )(*sketches, *grads)


def prefetch_kernel(*refs):
    n = (len(refs) - 1) // 2
    sources, targets, sem = refs[:n], refs[n : 2 * n], refs[-1]
    pieces = sem.shape[1]
    copies = []
    for at in range(pieces):
        for k, (source, target) in enumerate(zip(sources, targets)):
            rows = source.shape[0] // pieces
            window = pl.ds(at * rows, rows)
            copy = pltpu.make_async_copy(source.at[window], target.at[window], sem.at[k, at])
            copy.start()
            copies.append(copy)
    for copy in copies:
        copy.wait()


def prefetch(*arrays):
    n = len(arrays)
    size = sum(array.size * array.dtype.itemsize for array in arrays)
    return pl.pallas_call(
        prefetch_kernel,
        in_specs=[pl.BlockSpec(memory_space=pl.ANY)] * n,
        out_specs=[pl.BlockSpec(memory_space=pltpu.VMEM)] * n,
        out_shape=[jax.ShapeDtypeStruct(array.shape, array.dtype) for array in arrays],
        scratch_shapes=[pltpu.SemaphoreType.DMA((n, 4))],
        compiler_params=pltpu.CompilerParams(vmem_limit_bytes=size + 2 * 1024 * 1024),
        cost_estimate=pl.CostEstimate(flops=0, bytes_accessed=size, transcendentals=0),
        name="prefetch",
    )(*[pltpu.with_memory_space_constraint(array, pltpu.HBM) for array in arrays])


def update_kernel(relatives, half, slabs, tile, *refs):
    n = len(relatives)
    rows_refs = refs[:n]
    signs_ref, weight_ref, second_ref = refs[n : n + 3]
    new_weight_ref, new_second_ref, nw_buf, ns_buf, out_sem = refs[-5:]
    part, low_rank = rows_refs[0].shape
    width = signs_ref.shape[0]
    slab = width // slabs
    gain = math.sqrt(0.05) / math.sqrt(low_rank)
    back = 0.5 / math.sqrt(0.05)
    nt = (((1,), (1,)), ((), ()))
    col = lax.axis_index("col")
    firsts = [pl.multiple_of(((col ^ rel) * 2 + half) * part, part) for rel in relatives]
    rows = jnp.concatenate([ref[...] for ref in rows_refs], axis=0) * gain
    high = rows.astype(jnp.bfloat16)
    low = (rows - high.astype(jnp.float32)).astype(jnp.bfloat16)
    stores = []
    for k in range(slabs):
        for at in range(k * slab, (k + 1) * slab, tile):
            signs = signs_ref[at : at + tile, :]
            dense = lax.dot_general(high, signs, nt, preferred_element_type=jnp.float32)
            dense += lax.dot_general(low, signs, nt, preferred_element_type=jnp.float32)
            columns = slice(at - k * slab, at - k * slab + tile)
            for b in range(n):
                mine = dense[b * part : (b + 1) * part]
                here = (pl.ds(firsts[b], part), slice(at, at + tile))
                new_second = 0.95 * second_ref[here] + mine * mine
                bottom = new_second * lax.rsqrt(new_second) + 1e-08
                inverse = pl.reciprocal(bottom, approx=True)
                inverse = inverse * (2.0 - bottom * inverse)
                ns_buf[k * n + b, :, columns] = new_second
                nw_buf[k * n + b, :, columns] = weight_ref[here] - (mine * back) * inverse
        for b in range(n):
            slot = k * n + b
            window = (pl.ds(firsts[b], part), pl.ds(k * slab, slab))
            for kind, (buf, ref) in enumerate(
                ((nw_buf, new_weight_ref), (ns_buf, new_second_ref))
            ):
                store = pltpu.make_async_copy(
                    buf.at[slot], ref.at[window], out_sem.at[kind, slot]
                )
                store.start()
                stores.append(store)
    for store in stores:
        store.wait()


def update(row_blocks, relatives, half, signs, weight, second, onto):
    part, low_rank = row_blocks[0].shape
    din_local = weight.shape[1]
    n = len(row_blocks)
    slabs = 4
    slab = din_local // slabs
    hbm = pl.BlockSpec(memory_space=pl.ANY)
    vmem = pl.BlockSpec(memory_space=pltpu.VMEM)
    in_specs = [vmem] * (n + 3)
    aliases = {}
    if onto:
        in_specs += [hbm, hbm]
        aliases = {n + 3: 0, n + 4: 1}
    size = n * part * din_local
    buf = pltpu.VMEM((slabs * n, part, slab), jnp.float32)
    return pl.pallas_call(
        functools.partial(update_kernel, relatives, half, slabs, min(slab, 256)),
        in_specs=in_specs,
        out_specs=[hbm, hbm],
        out_shape=[
            jax.ShapeDtypeStruct(weight.shape, jnp.float32),
            jax.ShapeDtypeStruct(second.shape, jnp.float32),
        ],
        scratch_shapes=[buf, buf, pltpu.SemaphoreType.DMA((2, slabs * n))],
        input_output_aliases=aliases,
        compiler_params=pltpu.CompilerParams(vmem_limit_bytes=12 * 1024 * 1024),
        cost_estimate=pl.CostEstimate(
            flops=4 * size * low_rank, bytes_accessed=8 * size, transcendentals=2 * size
        ),
        name="update",
    )(*row_blocks, signs, weight, second, *onto)


CORE, X, Y, Z0, Z1 = 1, 2, 4, 8, 16


def exchange(value, mask):
    size = lax.axis_size("dp") * lax.axis_size("col")
    return lax.ppermute(value, AXES, [(i, i ^ mask) for i in range(size)])


def stepped(tokens, out_grad, weight, second, momentum, sign_seed, step_number):
    low_rank = momentum.shape[1]
    owner_rows = momentum.shape[0]
    total_tokens = lax.axis_size("dp") * tokens.shape[0]
    inv_root = 1.0 / jnp.sqrt(jnp.float32(low_rank))
    seeds = (sign_seed, step_number)

    far0 = [(Z1 | X | Z0, 0), (Z1 | X, 0), (Z1 | Z0, 0), (Z1, 0)]
    near0 = [(Z0 | X, 0), (Z0, 0), (X, 0), (0, 0)]
    far1 = [(Z1 | Y | X, 1), (Z1 | Y, 1), (Z1 | X, 1), (Z1, 1)]
    near1 = [(Y | X, 1), (Y, 1), (X, 1), (0, 1)]

    def toward(mask, pieces):
        return [(rel ^ mask, half) for rel, half in pieces]

    part = owner_rows // 2
    over_y, over_z = far0 + near0, far1 + near1
    og_y, og_z = pack(out_grad, [toward(Y, over_y), toward(Z0, over_z)], owner_rows, part)
    og_y = exchange(og_y, Y)
    og_z = exchange(og_z, Z0)
    signs, send_a, keep_a = sketch_parts(tokens, low_rank, None, seeds)
    og_yc, og_zc, og_c, og_own = pack(
        out_grad,
        [
            toward(Y | CORE, over_y),
            toward(Z0 | CORE, over_z),
            toward(CORE, over_y + over_z),
            over_y + over_z,
        ],
        owner_rows,
        part,
    )
    got_a = exchange(send_a, CORE)
    across = exchange(keep_a + got_a, X)
    og_yc = exchange(og_yc, Y | CORE)
    og_zc = exchange(og_zc, Z0 | CORE)
    og_c = exchange(og_c, CORE)
    send_b, keep_b = sketch_parts(tokens, low_rank, signs, seeds)
    weight_v, second_v = prefetch(weight, second)
    got_b = exchange(send_b, CORE)
    sketch = (((keep_b + got_b) + across) * inv_root).astype(jnp.bfloat16)

    sk_y = exchange(sketch, Y)
    sk_z = exchange(sketch, Z0)
    sk_c = exchange(sketch, CORE)
    sk_yc = exchange(sk_y, CORE)
    sk_zc = exchange(sk_z, CORE)

    scale = jnp.float32(1.0 / total_tokens)

    def packed(value, extra):
        return (value * (scale * extra)).astype(jnp.float16)

    def unpacked(value, extra):
        return value.astype(jnp.float32) * (1.0 / (scale * extra))

    y_side = (sketch, sk_c, sk_y, sk_yc), (og_own, og_c, og_y, og_yc)
    z_side = (sketch, sk_c, sk_z, sk_zc), (og_own, og_c, og_z, og_zc)

    def begin(side, offsets, axis):
        send, keep = project(*side, offsets, 4)
        return exchange(packed(send, 8.0), axis), keep

    def middle(state, axis):
        got, keep = state
        ahead = exchange(packed(keep[0] + unpacked(got[0], 8.0), 4.0), axis)
        return ahead, keep[1] + unpacked(got[1], 8.0)

    def finish(state):
        got, keep = state
        return keep + unpacked(got, 4.0)

    far0_state = begin(y_side, (0, 0, 0, 0), X)
    far1_state = begin(z_side, (8, 8, 0, 0), Y)
    near0_state = begin(y_side, (4, 4, 4, 4), Z0)
    near1_state = begin(z_side, (12, 12, 4, 4), Y)
    far0_state = middle(far0_state, Z0)
    far1_state = middle(far1_state, X)
    last0 = exchange(packed(finish(far0_state), 2.0), Z1)
    last1 = exchange(packed(finish(far1_state), 2.0), Z1)
    near0_state = middle(near0_state, X)
    near1_state = middle(near1_state, X)

    def momentum_half(half, near, last):
        projected = (near + unpacked(last, 2.0)) * scale
        return 0.8 * momentum[half * part : (half + 1) * part] + 0.2 * projected

    halves, pieces = [], []
    small = None
    for half, near_state, last in ((0, near0_state, last0), (1, near1_state, last1)):
        if small is not None:
            last, _ = lax.optimization_barrier((last, small))
        mine = momentum_half(half, finish(near_state), last)
        small = mine.astype(jnp.float16)
        from_core = exchange(small, CORE)
        from_x = exchange(small, X)
        from_xc = exchange(from_x, CORE)
        halves.append(mine)
        pieces.append([v.astype(jnp.float32) for v in (from_core, from_x, from_xc)])
    done = ()
    for half in (0, 1):
        rows = (halves[half], pieces[half][0])
        done = update(rows, (0, CORE), half, signs, weight_v, second_v, tuple(done))
    for half in (0, 1):
        rows = (pieces[half][1], pieces[half][2])
        done = update(rows, (X, X | CORE), half, signs, weight_v, second_v, tuple(done))
    return (done[0], done[1], jnp.concatenate(halves, axis=0))


def solution(mesh):
    placed = (
        P("dp", "col"),
        P(AXES, None),
        P("dp", "col"),
        P("dp", "col"),
        P(AXES, None),
        P(),
        P(),
    )

    def per_device(tokens, out_grad, weight, second, momentum, sign_seed, step_number):
        args = (tokens, out_grad, weight, second, momentum, sign_seed, step_number)
        cube = mesh.shape["dp"] == Z1 * 2 // (X * 2) and mesh.shape["col"] == X * 2
        if cube and momentum.shape[0] % (2 * LANES) == 0:
            return stepped(*args)
        return general(*args)

    return jax.shard_map(
        per_device,
        mesh=mesh,
        in_specs=placed,
        out_specs=(P("dp", "col"), P("dp", "col"), P(AXES, None)),
        check_vma=False,
    )
```

```python
import functools
import math

import jax
import jax.numpy as jnp
from jax import lax
from jax.experimental import pallas as pl
from jax.experimental.pallas import tpu as pltpu
from jax.sharding import PartitionSpec as P


AXES = ("dp", "col")
LANES = 128


def low_bits(mixed):
    mixed = mixed ^ lax.shift_right_logical(mixed, 16)
    mixed = mixed * 2127912213
    mixed = mixed ^ lax.shift_right_logical(mixed, 13)
    mixed = mixed * 1103515245
    mixed = mixed ^ lax.shift_right_logical(mixed, 16)
    return mixed & (1 << 20)


def sign_table(sign_seed, step_number, first_row, row_count, low_rank):
    row_ids = first_row + lax.iota(jnp.int32, row_count)
    col_ids = lax.iota(jnp.int32, low_rank)
    flat_index = row_ids[:, None] * low_rank + col_ids[None, :]
    seeded = sign_seed[0] * 1664525 + step_number[0] * 1013904223
    return jnp.where(low_bits(flat_index * 747796405 + seeded) == 0, 1.0, -1.0)


def contract(left_rows, right_rows):
    return lax.dot_general(
        left_rows, right_rows, (((0,), (0,)), ((), ())), preferred_element_type=jnp.float32
    )


def general(tokens, out_grad, weight, second, momentum, sign_seed, step_number):
    local_tokens, din_local = tokens.shape
    low_rank = momentum.shape[1]
    owner_rows = momentum.shape[0]
    inv_root = 1.0 / jnp.sqrt(jnp.float32(low_rank))
    col_position = lax.axis_index("col")
    sign_block = sign_table(sign_seed, step_number, col_position * din_local, din_local, low_rank)
    partial_sketch = (
        jnp.dot(tokens, sign_block.astype(jnp.bfloat16), preferred_element_type=jnp.float32)
        * inv_root
    )
    quarter = lax.psum_scatter(partial_sketch, "col", scatter_dimension=0, tiled=True)
    sketch = quarter.astype(jnp.bfloat16)
    total_tokens = lax.axis_size("dp") * local_tokens
    data_count = lax.axis_size("dp")
    col_count = lax.axis_size("col")
    quarter_rows = out_grad.shape[0]
    grouped = out_grad.reshape(quarter_rows, data_count, col_count, owner_rows)
    grouped = jnp.transpose(grouped, (0, 2, 1, 3)).reshape(
        quarter_rows, col_count, data_count * owner_rows
    )
    regrouped = lax.all_to_all(grouped, "col", split_axis=1, concat_axis=0, tiled=True)
    regrouped = regrouped.reshape(quarter_rows * col_count, data_count * owner_rows)
    shard_sketch = lax.all_gather(sketch, "col", axis=0, tiled=True)
    projected = lax.psum_scatter(
        contract(regrouped, shard_sketch), "dp", scatter_dimension=0, tiled=True
    )
    projected = projected / jnp.float32(total_tokens)
    new_momentum = 0.8 * momentum + 0.2 * projected
    row_block = lax.all_gather(new_momentum, "col", axis=0, tiled=True)
    dense_grad = (
        lax.dot_general(
            row_block,
            sign_block,
            (((1,), (1,)), ((), ())),
            precision=lax.Precision.HIGHEST,
            preferred_element_type=jnp.float32,
        )
        * inv_root
    )
    new_second = 0.95 * second + 0.05 * dense_grad * dense_grad
    new_weight = weight - 0.5 * dense_grad / (jnp.sqrt(new_second) + 1e-08)
    return (new_weight, new_second, new_momentum)


def params(vmem=56 * 1024 * 1024, axes=1):
    return pltpu.CompilerParams(
        dimension_semantics=("arbitrary",) * axes, vmem_limit_bytes=vmem
    )


def pack_kernel(groups, width, part, seeded, og_ref, *refs):
    if seeded:
        seed_ref, step_ref, *refs = refs
        columns_ref, *refs = refs
        *refs, seed, step, seed_sem = refs
        copies = [
            pltpu.make_async_copy(seed_ref, seed, seed_sem.at[0]),
            pltpu.make_async_copy(step_ref, step, seed_sem.at[1]),
        ]
        for copy in copies:
            copy.start()
    n_out = len(groups)
    outs = refs[:n_out]
    stage, in_sem, out_sem = refs[n_out:]
    me = lax.axis_index("dp") * lax.axis_size("col") + lax.axis_index("col")
    loads = []
    slot = 0
    for group in groups:
        mine = []
        for rel, half in group:
            first = pl.multiple_of((me ^ rel) * width + half * part, part)
            copy = pltpu.make_async_copy(
                og_ref.at[:, pl.ds(first, part)], stage.at[slot], in_sem.at[slot]
            )
            copy.start()
            mine.append(copy)
            slot += 1
        loads.append(mine)
    if seeded:
        for copy in copies:
            copy.wait()
        constant = seed[...] * 1664525 + step[...] * 1013904223
        ids = lax.broadcasted_iota(jnp.int32, columns_ref.shape, 1)
        columns_ref[...] = ids * 747796405 + constant
    stores = []
    slot = 0
    for index, group in enumerate(groups):
        for copy in loads[index]:
            copy.wait()
        store = pltpu.make_async_copy(
            stage.at[pl.ds(slot, len(group))], outs[index], out_sem.at[index]
        )
        store.start()
        stores.append(store)
        slot += len(group)
    for store in stores:
        store.wait()


def pack(out_grad, groups, width, part, seeds=(), low_rank=None):
    rows = out_grad.shape[0]
    count = sum(len(group) for group in groups)
    hbm = pl.BlockSpec(memory_space=pl.ANY)
    out_specs = [hbm] * len(groups)
    out_shape = [
        jax.ShapeDtypeStruct((len(group), rows, part), out_grad.dtype) for group in groups
    ]
    scratch = [
        pltpu.VMEM((count, rows, part), out_grad.dtype),
        pltpu.SemaphoreType.DMA((count,)),
        pltpu.SemaphoreType.DMA((len(groups),)),
    ]
    if seeds:
        out_specs = [pl.BlockSpec(memory_space=pltpu.VMEM)] + out_specs
        out_shape = [jax.ShapeDtypeStruct((1, low_rank), jnp.int32)] + out_shape
        scratch += [pltpu.VMEM((1, 1), jnp.int32)] * 2 + [pltpu.SemaphoreType.DMA((2,))]
    return pl.pallas_call(
        functools.partial(pack_kernel, groups, width, part, bool(seeds)),
        in_specs=[hbm] * (1 + len(seeds)),
        out_specs=out_specs,
        out_shape=out_shape,
        scratch_shapes=scratch,
        compiler_params=pltpu.CompilerParams(vmem_limit_bytes=8 * 1024 * 1024),
        cost_estimate=pl.CostEstimate(
            flops=0, bytes_accessed=4 * count * rows * part, transcendentals=0
        ),
        name="pack",
    )(pltpu.with_memory_space_constraint(out_grad, pltpu.HBM), *seeds)


CHUNKS = 4
STRIP = 32


def sketch_kernel(first, din_local, *refs):
    if first:
        columns_ref, tok_ref, signs_ref, send_ref, keep_ref, tok, acc, sem = refs
    else:
        tok_ref, signs_ref, send_ref, keep_ref, tok, acc, sem = refs
    quarter, low_rank = keep_ref.shape
    chunk = din_local // CHUNKS
    col = lax.axis_index("col")
    group = col ^ (X if first else 0)
    loads = []
    for part in range(CHUNKS):
        at = pl.ds(part * chunk, chunk)
        mine = []
        for slot, rel in enumerate((CORE, 0)):
            rows = pl.ds(pl.multiple_of((group ^ rel) * quarter, quarter), quarter)
            copy = pltpu.make_async_copy(
                tok_ref.at[rows, at],
                tok.at[pl.ds(slot * quarter, quarter), at],
                sem.at[part, slot],
            )
            copy.start()
            mine.append(copy)
        loads.append(mine)
    if first:
        row_factor = low_rank * 747796405
        row_factor = (row_factor + (1 << 31)) % (1 << 32) - (1 << 31)
        local = lax.broadcasted_iota(jnp.int32, (STRIP, low_rank), 0) * row_factor
        local = local + columns_ref[...]
    for part in range(CHUNKS):
        at = slice(part * chunk, (part + 1) * chunk)
        if first:
            for row in range(part * chunk, (part + 1) * chunk, STRIP):
                mixed = local + (col * din_local + row) * row_factor
                strip = jnp.where(low_bits(mixed) == 0, 1.0, -1.0)
                signs_ref[row : row + STRIP, :] = strip.astype(jnp.bfloat16)
        for copy in loads[part]:
            copy.wait()
        product = jnp.dot(tok[:, at], signs_ref[at, :], preferred_element_type=jnp.float32)
        if part > 0:
            product += acc[...]
        if part < CHUNKS - 1:
            acc[...] = product
        else:
            send_ref[...] = product[:quarter]
            keep_ref[...] = product[quarter:]


def sketch_parts(tokens, low_rank, signs, columns):
    local_tokens, din_local = tokens.shape
    half = local_tokens // 2
    quarter = half // 2
    first = signs is None
    vmem = pl.BlockSpec(memory_space=pltpu.VMEM)
    hbm = pl.BlockSpec(memory_space=pl.ANY)
    parts = [jax.ShapeDtypeStruct((quarter, low_rank), jnp.float32)] * 2
    tokens = pltpu.with_memory_space_constraint(tokens, pltpu.HBM)
    if first:
        in_specs, args = [vmem, hbm], (columns, tokens)
        out_shape = [jax.ShapeDtypeStruct((din_local, low_rank), jnp.bfloat16)] + parts
    else:
        in_specs, args = [hbm, vmem], (tokens, signs)
        out_shape = parts
    return pl.pallas_call(
        functools.partial(sketch_kernel, first, din_local),
        in_specs=in_specs,
        out_specs=[vmem] * len(out_shape),
        out_shape=out_shape,
        scratch_shapes=[
            pltpu.VMEM((half, din_local), tokens.dtype),
            pltpu.VMEM((half, low_rank), jnp.float32),
            pltpu.SemaphoreType.DMA((CHUNKS, 2)),
        ],
        compiler_params=pltpu.CompilerParams(vmem_limit_bytes=12 * 1024 * 1024),
        cost_estimate=pl.CostEstimate(
            flops=2 * half * din_local * low_rank,
            bytes_accessed=half * din_local * 2 + din_local * low_rank * 2 + 2 * half * low_rank * 4,
            transcendentals=0,
        ),
        name="sketch_first" if first else "sketch_next",
    )(*args)


def project_kernel(n, *refs):
    send_ref, keep_ref = refs[-2:]
    count, _, part = refs[n].shape
    sketch = jnp.concatenate([ref[...] for ref in refs[:n]], axis=0)
    grads = jnp.concatenate(
        [
            jnp.concatenate([ref[j] for j in range(count)], axis=1)
            for ref in refs[n : 2 * n]
        ],
        axis=0,
    )
    total = contract(grads, sketch)
    for j in range(count):
        out_ref = send_ref if j < count // 2 else keep_ref
        out_ref[j % (count // 2)] = total[j * part : (j + 1) * part]


def project(sketches, grads, offsets, count):
    rows, low_rank = sketches[0].shape
    part = grads[0].shape[2]
    n = len(sketches)

    def block_at(offset):
        return pl.BlockSpec((count, rows, part), lambda i: (offset // count, 0, 0))

    out = jax.ShapeDtypeStruct((count // 2, part, low_rank), jnp.float32)
    return pl.pallas_call(
        functools.partial(project_kernel, n),
        grid=(1,),
        in_specs=[pl.BlockSpec((rows, low_rank), lambda i: (0, 0))] * n
        + [block_at(offset) for offset in offsets],
        out_specs=[pl.BlockSpec((count // 2, part, low_rank), lambda i: (0, 0, 0))] * 2,
        out_shape=[out] * 2,
        compiler_params=params(10 * 1024 * 1024),
        cost_estimate=pl.CostEstimate(
            flops=2 * n * count * rows * part * low_rank,
            bytes_accessed=n * (rows * low_rank + count * rows * part) * 2
            + count * low_rank * part * 4,
            transcendentals=0,
        ),
        name="project",
    )(*sketches, *grads)


def prefetch_kernel(*refs):
    n = (len(refs) - 1) // 2
    sources, targets, sem = refs[:n], refs[n : 2 * n], refs[-1]
    pieces = sem.shape[1]
    copies = []
    for at in range(pieces):
        for k, (source, target) in enumerate(zip(sources, targets)):
            rows = source.shape[0] // pieces
            window = pl.ds(at * rows, rows)
            copy = pltpu.make_async_copy(source.at[window], target.at[window], sem.at[k, at])
            copy.start()
            copies.append(copy)
    for copy in copies:
        copy.wait()


def prefetch(*arrays):
    n = len(arrays)
    size = sum(array.size * array.dtype.itemsize for array in arrays)
    return pl.pallas_call(
        prefetch_kernel,
        in_specs=[pl.BlockSpec(memory_space=pl.ANY)] * n,
        out_specs=[pl.BlockSpec(memory_space=pltpu.VMEM)] * n,
        out_shape=[jax.ShapeDtypeStruct(array.shape, array.dtype) for array in arrays],
        scratch_shapes=[pltpu.SemaphoreType.DMA((n, 4))],
        compiler_params=pltpu.CompilerParams(vmem_limit_bytes=size + 2 * 1024 * 1024),
        cost_estimate=pl.CostEstimate(flops=0, bytes_accessed=size, transcendentals=0),
        name="prefetch",
    )(*[pltpu.with_memory_space_constraint(array, pltpu.HBM) for array in arrays])


def update_kernel(where, keep, slabs, tile, *refs):
    n = len(where)
    rows_refs = refs[:n]
    signs_ref, weight_ref, second_ref = refs[n : n + 3]
    new_weight_ref, new_second_ref, new_momentum_ref = refs[-7:-4]
    nw_buf, ns_buf, out_sem, keep_sem = refs[-4:]
    part, low_rank = rows_refs[0].shape
    width = signs_ref.shape[0]
    slab = width // slabs
    gain = math.sqrt(0.05) / math.sqrt(low_rank)
    back = 0.5 / math.sqrt(0.05)
    nt = (((1,), (1,)), ((), ()))
    col = lax.axis_index("col")
    firsts = [pl.multiple_of(((col ^ rel) * 2 + half) * part, part) for rel, half in where]
    stores = []
    if keep:
        half = where[0][1]
        store = pltpu.make_async_copy(
            rows_refs[0], new_momentum_ref.at[pl.ds(half * part, part)], keep_sem.at[0]
        )
        store.start()
        stores.append(store)
    rows = jnp.concatenate([ref[...] for ref in rows_refs], axis=0) * gain
    high = rows.astype(jnp.bfloat16)
    low = (rows - high.astype(jnp.float32)).astype(jnp.bfloat16)
    for k in range(slabs):
        for at in range(k * slab, (k + 1) * slab, tile):
            signs = signs_ref[at : at + tile, :]
            dense = lax.dot_general(high, signs, nt, preferred_element_type=jnp.float32)
            dense += lax.dot_general(low, signs, nt, preferred_element_type=jnp.float32)
            columns = slice(at - k * slab, at - k * slab + tile)
            for b in range(n):
                mine = dense[b * part : (b + 1) * part]
                here = (pl.ds(firsts[b], part), slice(at, at + tile))
                new_second = 0.95 * second_ref[here] + mine * mine
                bottom = new_second * lax.rsqrt(new_second) + 1e-08
                inverse = pl.reciprocal(bottom, approx=True)
                inverse = inverse * (2.0 - bottom * inverse)
                ns_buf[k * n + b, :, columns] = new_second
                nw_buf[k * n + b, :, columns] = weight_ref[here] - (mine * back) * inverse
        for b in range(n):
            slot = k * n + b
            window = (pl.ds(firsts[b], part), pl.ds(k * slab, slab))
            for kind, (buf, ref) in enumerate(
                ((nw_buf, new_weight_ref), (ns_buf, new_second_ref))
            ):
                store = pltpu.make_async_copy(
                    buf.at[slot], ref.at[window], out_sem.at[kind, slot]
                )
                store.start()
                stores.append(store)
    for store in stores:
        store.wait()


def update(row_blocks, where, keep, signs, weight, second, onto):
    part, low_rank = row_blocks[0].shape
    din_local = weight.shape[1]
    n = len(row_blocks)
    slabs = 4
    slab = din_local // slabs
    hbm = pl.BlockSpec(memory_space=pl.ANY)
    vmem = pl.BlockSpec(memory_space=pltpu.VMEM)
    in_specs = [vmem] * (n + 3)
    aliases = {}
    if onto:
        in_specs += [hbm] * 3
        aliases = {n + 3 + k: k for k in range(3)}
    size = n * part * din_local
    buf = pltpu.VMEM((slabs * n, part, slab), jnp.float32)
    return pl.pallas_call(
        functools.partial(update_kernel, where, keep, slabs, min(slab, 256)),
        in_specs=in_specs,
        out_specs=[hbm] * 3,
        out_shape=[
            jax.ShapeDtypeStruct(weight.shape, jnp.float32),
            jax.ShapeDtypeStruct(second.shape, jnp.float32),
            jax.ShapeDtypeStruct((2 * part, low_rank), jnp.float32),
        ],
        scratch_shapes=[
            buf,
            buf,
            pltpu.SemaphoreType.DMA((2, slabs * n)),
            pltpu.SemaphoreType.DMA((1,)),
        ],
        input_output_aliases=aliases,
        compiler_params=pltpu.CompilerParams(
            vmem_limit_bytes=8 * size + 8 * 1024 * 1024
        ),
        cost_estimate=pl.CostEstimate(
            flops=4 * size * low_rank, bytes_accessed=8 * size, transcendentals=2 * size
        ),
        name="update",
    )(*row_blocks, signs, weight, second, *onto)


CORE, X, Y, Z0, Z1 = 1, 2, 4, 8, 16


def exchange(value, mask):
    size = lax.axis_size("dp") * lax.axis_size("col")
    return lax.ppermute(value, AXES, [(i, i ^ mask) for i in range(size)])


def stepped(tokens, out_grad, weight, second, momentum, sign_seed, step_number):
    low_rank = momentum.shape[1]
    owner_rows = momentum.shape[0]
    total_tokens = lax.axis_size("dp") * tokens.shape[0]
    inv_root = 1.0 / jnp.sqrt(jnp.float32(low_rank))
    far0 = [(Z1 | X | Z0, 0), (Z1 | X, 0), (Z1 | Z0, 0), (Z1, 0)]
    near0 = [(Z0 | X, 0), (Z0, 0), (X, 0), (0, 0)]
    far1 = [(Z1 | Y | X, 1), (Z1 | Y, 1), (Z1 | X, 1), (Z1, 1)]
    near1 = [(Y | X, 1), (Y, 1), (X, 1), (0, 1)]

    def toward(mask, pieces):
        return [(rel ^ mask, half) for rel, half in pieces]

    part = owner_rows // 2
    over_y, over_z = far0 + near0, far1 + near1
    columns, og_y, og_z = pack(
        out_grad,
        [toward(Y, over_y), toward(Z0, over_z)],
        owner_rows,
        part,
        (sign_seed.reshape(1, 1), step_number.reshape(1, 1)),
        low_rank,
    )
    og_y = exchange(og_y, Y)
    og_z = exchange(og_z, Z0)
    signs, send_a, keep_a = sketch_parts(tokens, low_rank, None, columns)
    og_yc, og_zc = pack(
        out_grad, [toward(Y | CORE, over_y), toward(Z0 | CORE, over_z)], owner_rows, part
    )
    og_c, og_own = pack(
        out_grad,
        [toward(CORE, over_y + over_z), over_y + over_z],
        owner_rows,
        part,
    )
    got_a = exchange(send_a, CORE)
    across = exchange(keep_a + got_a, X)
    og_yc = exchange(og_yc, Y | CORE)
    og_zc = exchange(og_zc, Z0 | CORE)
    og_c = exchange(og_c, CORE)
    send_b, keep_b = sketch_parts(tokens, low_rank, signs, None)
    weight_v, second_v = prefetch(weight, second)
    got_b = exchange(send_b, CORE)
    sketch = (((keep_b + got_b) + across) * inv_root).astype(jnp.bfloat16)

    sk_y = exchange(sketch, Y)
    sk_z = exchange(sketch, Z0)
    sk_c = exchange(sketch, CORE)
    sk_yc = exchange(sk_y, CORE)
    sk_zc = exchange(sk_z, CORE)

    scale = jnp.float32(1.0 / total_tokens)

    def packed(value, extra):
        return (value * (scale * extra)).astype(jnp.float16)

    def unpacked(value, extra):
        return value.astype(jnp.float32) * (1.0 / (scale * extra))

    y_side = (sketch, sk_c, sk_y, sk_yc), (og_own, og_c, og_y, og_yc)
    z_side = (sketch, sk_c, sk_z, sk_zc), (og_own, og_c, og_z, og_zc)

    def begin(side, offsets, axis):
        send, keep = project(*side, offsets, 4)
        return exchange(packed(send, 8.0), axis), keep

    def middle(state, axis):
        got, keep = state
        ahead = exchange(packed(keep[0] + unpacked(got[0], 8.0), 4.0), axis)
        return ahead, keep[1] + unpacked(got[1], 8.0)

    def finish(state):
        got, keep = state
        return keep + unpacked(got, 4.0)

    far0_state = begin(y_side, (0, 0, 0, 0), X)
    far1_state = begin(z_side, (8, 8, 0, 0), Y)
    near0_state = begin(y_side, (4, 4, 4, 4), Z0)
    near1_state = begin(z_side, (12, 12, 4, 4), Y)
    far0_state = middle(far0_state, Z0)
    far1_state = middle(far1_state, X)
    last0 = exchange(packed(finish(far0_state), 2.0), Z1)
    last1 = exchange(packed(finish(far1_state), 2.0), Z1)
    near0_state = middle(near0_state, X)
    near1_state = middle(near1_state, X)

    def momentum_half(half, near, last):
        projected = (near + unpacked(last, 2.0)) * scale
        return 0.8 * momentum[half * part : (half + 1) * part] + 0.2 * projected

    halves, pieces = [], []
    small = None
    for half, near_state, last in ((0, near0_state, last0), (1, near1_state, last1)):
        if small is not None:
            last, _ = lax.optimization_barrier((last, small))
        mine = momentum_half(half, finish(near_state), last)
        small = mine.astype(jnp.float16)
        from_core = exchange(small, CORE)
        from_x = exchange(small, X)
        from_xc = exchange(from_x, CORE)
        halves.append(mine)
        pieces.append([v.astype(jnp.float32) for v in (from_core, from_x, from_xc)])
    rows = (halves[0], pieces[0][0])
    done = update(rows, ((0, 0), (CORE, 0)), True, signs, weight_v, second_v, ())
    rows = (halves[1], pieces[1][0], pieces[0][1], pieces[0][2])
    where = ((0, 1), (CORE, 1), (X, 0), (X | CORE, 0))
    done = update(rows, where, True, signs, weight_v, second_v, tuple(done))
    rows = (pieces[1][1], pieces[1][2])
    where = ((X, 1), (X | CORE, 1))
    done = update(rows, where, False, signs, weight_v, second_v, tuple(done))
    return tuple(done)


def solution(mesh):
    placed = (
        P("dp", "col"),
        P(AXES, None),
        P("dp", "col"),
        P("dp", "col"),
        P(AXES, None),
        P(),
        P(),
    )

    def per_device(tokens, out_grad, weight, second, momentum, sign_seed, step_number):
        args = (tokens, out_grad, weight, second, momentum, sign_seed, step_number)
        cube = mesh.shape["dp"] == Z1 * 2 // (X * 2) and mesh.shape["col"] == X * 2
        if cube and momentum.shape[0] % (2 * LANES) == 0:
            return stepped(*args)
        return general(*args)

    return jax.shard_map(
        per_device,
        mesh=mesh,
        in_specs=placed,
        out_specs=(P("dp", "col"), P("dp", "col"), P(AXES, None)),
        check_vma=False,
    )
```

```python
import functools
import math

import jax
import jax.numpy as jnp
from jax import lax
from jax.experimental import pallas as pl
from jax.experimental.pallas import tpu as pltpu
from jax.sharding import PartitionSpec as P


AXES = ("dp", "col")
LANES = 128


def low_bits(mixed):
    mixed = mixed ^ lax.shift_right_logical(mixed, 16)
    mixed = mixed * 2127912213
    mixed = mixed ^ lax.shift_right_logical(mixed, 13)
    mixed = mixed * 1103515245
    mixed = mixed ^ lax.shift_right_logical(mixed, 16)
    return mixed & (1 << 20)


def sign_table(sign_seed, step_number, first_row, row_count, low_rank):
    row_ids = first_row + lax.iota(jnp.int32, row_count)
    col_ids = lax.iota(jnp.int32, low_rank)
    flat_index = row_ids[:, None] * low_rank + col_ids[None, :]
    seeded = sign_seed[0] * 1664525 + step_number[0] * 1013904223
    return jnp.where(low_bits(flat_index * 747796405 + seeded) == 0, 1.0, -1.0)


def contract(left_rows, right_rows):
    return lax.dot_general(
        left_rows, right_rows, (((0,), (0,)), ((), ())), preferred_element_type=jnp.float32
    )


def general(tokens, out_grad, weight, second, momentum, sign_seed, step_number):
    local_tokens, din_local = tokens.shape
    low_rank = momentum.shape[1]
    owner_rows = momentum.shape[0]
    inv_root = 1.0 / jnp.sqrt(jnp.float32(low_rank))
    col_position = lax.axis_index("col")
    sign_block = sign_table(sign_seed, step_number, col_position * din_local, din_local, low_rank)
    partial_sketch = (
        jnp.dot(tokens, sign_block.astype(jnp.bfloat16), preferred_element_type=jnp.float32)
        * inv_root
    )
    quarter = lax.psum_scatter(partial_sketch, "col", scatter_dimension=0, tiled=True)
    sketch = quarter.astype(jnp.bfloat16)
    total_tokens = lax.axis_size("dp") * local_tokens
    data_count = lax.axis_size("dp")
    col_count = lax.axis_size("col")
    quarter_rows = out_grad.shape[0]
    grouped = out_grad.reshape(quarter_rows, data_count, col_count, owner_rows)
    grouped = jnp.transpose(grouped, (0, 2, 1, 3)).reshape(
        quarter_rows, col_count, data_count * owner_rows
    )
    regrouped = lax.all_to_all(grouped, "col", split_axis=1, concat_axis=0, tiled=True)
    regrouped = regrouped.reshape(quarter_rows * col_count, data_count * owner_rows)
    shard_sketch = lax.all_gather(sketch, "col", axis=0, tiled=True)
    projected = lax.psum_scatter(
        contract(regrouped, shard_sketch), "dp", scatter_dimension=0, tiled=True
    )
    projected = projected / jnp.float32(total_tokens)
    new_momentum = 0.8 * momentum + 0.2 * projected
    row_block = lax.all_gather(new_momentum, "col", axis=0, tiled=True)
    dense_grad = (
        lax.dot_general(
            row_block,
            sign_block,
            (((1,), (1,)), ((), ())),
            precision=lax.Precision.HIGHEST,
            preferred_element_type=jnp.float32,
        )
        * inv_root
    )
    new_second = 0.95 * second + 0.05 * dense_grad * dense_grad
    new_weight = weight - 0.5 * dense_grad / (jnp.sqrt(new_second) + 1e-08)
    return (new_weight, new_second, new_momentum)


def params(vmem=56 * 1024 * 1024, axes=1):
    return pltpu.CompilerParams(
        dimension_semantics=("arbitrary",) * axes, vmem_limit_bytes=vmem
    )


def pack_kernel(groups, width, part, og_ref, *refs):
    n_out = len(groups)
    outs = refs[:n_out]
    stage, in_sem, out_sem = refs[n_out:]
    me = lax.axis_index("dp") * lax.axis_size("col") + lax.axis_index("col")
    loads = []
    slot = 0
    for group in groups:
        mine = []
        for rel, half in group:
            first = pl.multiple_of((me ^ rel) * width + half * part, part)
            copy = pltpu.make_async_copy(
                og_ref.at[:, pl.ds(first, part)], stage.at[slot], in_sem.at[slot]
            )
            copy.start()
            mine.append(copy)
            slot += 1
        loads.append(mine)
    stores = []
    slot = 0
    for index, group in enumerate(groups):
        for copy in loads[index]:
            copy.wait()
        store = pltpu.make_async_copy(
            stage.at[pl.ds(slot, len(group))], outs[index], out_sem.at[index]
        )
        store.start()
        stores.append(store)
        slot += len(group)
    for store in stores:
        store.wait()


def pack(out_grad, groups, width, part):
    rows = out_grad.shape[0]
    count = sum(len(group) for group in groups)
    hbm = pl.BlockSpec(memory_space=pl.ANY)
    return pl.pallas_call(
        functools.partial(pack_kernel, groups, width, part),
        in_specs=[hbm],
        out_specs=[hbm] * len(groups),
        out_shape=[
            jax.ShapeDtypeStruct((len(group), rows, part), out_grad.dtype) for group in groups
        ],
        scratch_shapes=[
            pltpu.VMEM((count, rows, part), out_grad.dtype),
            pltpu.SemaphoreType.DMA((count,)),
            pltpu.SemaphoreType.DMA((len(groups),)),
        ],
        compiler_params=pltpu.CompilerParams(vmem_limit_bytes=8 * 1024 * 1024),
        cost_estimate=pl.CostEstimate(
            flops=0, bytes_accessed=4 * count * rows * part, transcendentals=0
        ),
        name="pack",
    )(pltpu.with_memory_space_constraint(out_grad, pltpu.HBM))


CHUNKS = 4
STRIP = 32


def sketch_kernel(first, din_local, *refs):
    if first:
        seed_ref, step_ref, *refs, seed, step, seed_sem = refs
        seed_copies = [
            pltpu.make_async_copy(seed_ref, seed, seed_sem.at[0]),
            pltpu.make_async_copy(step_ref, step, seed_sem.at[1]),
        ]
        for copy in seed_copies:
            copy.start()
        tok_ref, signs_ref, send_ref, keep_ref, tok, acc, sem = refs
    else:
        tok_ref, signs_ref, send_ref, keep_ref, tok, acc, sem = refs
    quarter, low_rank = keep_ref.shape
    chunk = din_local // CHUNKS
    col = lax.axis_index("col")
    group = col ^ (X if first else 0)
    loads = []
    for part in range(CHUNKS):
        at = pl.ds(part * chunk, chunk)
        mine = []
        for slot, rel in enumerate((CORE, 0)):
            rows = pl.ds(pl.multiple_of((group ^ rel) * quarter, quarter), quarter)
            copy = pltpu.make_async_copy(
                tok_ref.at[rows, at],
                tok.at[pl.ds(slot * quarter, quarter), at],
                sem.at[part, slot],
            )
            copy.start()
            mine.append(copy)
        loads.append(mine)
    if first:
        row_factor = low_rank * 747796405
        row_factor = (row_factor + (1 << 31)) % (1 << 32) - (1 << 31)
        local = lax.broadcasted_iota(jnp.int32, (STRIP, low_rank), 0) * row_factor
        columns = lax.broadcasted_iota(jnp.int32, (1, low_rank), 1) * 747796405
        for copy in seed_copies:
            copy.wait()
        columns = columns + (seed[...] * 1664525 + step[...] * 1013904223)
        local = local + columns
    for part in range(CHUNKS):
        at = slice(part * chunk, (part + 1) * chunk)
        if first:
            for row in range(part * chunk, (part + 1) * chunk, STRIP):
                mixed = local + (col * din_local + row) * row_factor
                strip = jnp.where(low_bits(mixed) == 0, 1.0, -1.0)
                signs_ref[row : row + STRIP, :] = strip.astype(jnp.bfloat16)
        for copy in loads[part]:
            copy.wait()
        product = jnp.dot(tok[:, at], signs_ref[at, :], preferred_element_type=jnp.float32)
        if part > 0:
            product += acc[...]
        if part < CHUNKS - 1:
            acc[...] = product
        else:
            send_ref[...] = product[:quarter]
            keep_ref[...] = product[quarter:]


def sketch_parts(tokens, low_rank, signs, seeds):
    local_tokens, din_local = tokens.shape
    half = local_tokens // 2
    quarter = half // 2
    first = signs is None
    vmem = pl.BlockSpec(memory_space=pltpu.VMEM)
    hbm = pl.BlockSpec(memory_space=pl.ANY)
    parts = [jax.ShapeDtypeStruct((quarter, low_rank), jnp.float32)] * 2
    tokens = pltpu.with_memory_space_constraint(tokens, pltpu.HBM)
    if first:
        in_specs, args = [hbm, hbm, hbm], (*seeds, tokens)
        out_shape = [jax.ShapeDtypeStruct((din_local, low_rank), jnp.bfloat16)] + parts
    else:
        in_specs, args = [hbm, vmem], (tokens, signs)
        out_shape = parts
    return pl.pallas_call(
        functools.partial(sketch_kernel, first, din_local),
        in_specs=in_specs,
        out_specs=[vmem] * len(out_shape),
        out_shape=out_shape,
        scratch_shapes=[
            pltpu.VMEM((half, din_local), tokens.dtype),
            pltpu.VMEM((half, low_rank), jnp.float32),
            pltpu.SemaphoreType.DMA((CHUNKS, 2)),
        ]
        + ([pltpu.VMEM((1, 1), jnp.int32)] * 2 + [pltpu.SemaphoreType.DMA((2,))]) * first,
        compiler_params=pltpu.CompilerParams(vmem_limit_bytes=12 * 1024 * 1024),
        cost_estimate=pl.CostEstimate(
            flops=2 * half * din_local * low_rank,
            bytes_accessed=half * din_local * 2 + din_local * low_rank * 2 + 2 * half * low_rank * 4,
            transcendentals=0,
        ),
        name="sketch_first" if first else "sketch_next",
    )(*args)


def project_kernel(n, *refs):
    send_ref, keep_ref = refs[-2:]
    count, _, part = refs[n].shape
    sketch = jnp.concatenate([ref[...] for ref in refs[:n]], axis=0)
    grads = jnp.concatenate(
        [
            jnp.concatenate([ref[j] for j in range(count)], axis=1)
            for ref in refs[n : 2 * n]
        ],
        axis=0,
    )
    total = contract(grads, sketch)
    for j in range(count):
        out_ref = send_ref if j < count // 2 else keep_ref
        out_ref[j % (count // 2)] = total[j * part : (j + 1) * part]


def project(sketches, grads, offsets, count):
    rows, low_rank = sketches[0].shape
    part = grads[0].shape[2]
    n = len(sketches)

    def block_at(offset):
        return pl.BlockSpec((count, rows, part), lambda i: (offset // count, 0, 0))

    out = jax.ShapeDtypeStruct((count // 2, part, low_rank), jnp.float32)
    return pl.pallas_call(
        functools.partial(project_kernel, n),
        grid=(1,),
        in_specs=[pl.BlockSpec((rows, low_rank), lambda i: (0, 0))] * n
        + [block_at(offset) for offset in offsets],
        out_specs=[pl.BlockSpec((count // 2, part, low_rank), lambda i: (0, 0, 0))] * 2,
        out_shape=[out] * 2,
        compiler_params=params(10 * 1024 * 1024),
        cost_estimate=pl.CostEstimate(
            flops=2 * n * count * rows * part * low_rank,
            bytes_accessed=n * (rows * low_rank + count * rows * part) * 2
            + count * low_rank * part * 4,
            transcendentals=0,
        ),
        name="project",
    )(*sketches, *grads)


def prefetch_kernel(*refs):
    n = (len(refs) - 1) // 2
    sources, targets, sem = refs[:n], refs[n : 2 * n], refs[-1]
    pieces = sem.shape[1]
    copies = []
    for at in range(pieces):
        for k, (source, target) in enumerate(zip(sources, targets)):
            rows = source.shape[0] // pieces
            window = pl.ds(at * rows, rows)
            copy = pltpu.make_async_copy(source.at[window], target.at[window], sem.at[k, at])
            copy.start()
            copies.append(copy)
    for copy in copies:
        copy.wait()


def prefetch(*arrays):
    n = len(arrays)
    size = sum(array.size * array.dtype.itemsize for array in arrays)
    return pl.pallas_call(
        prefetch_kernel,
        in_specs=[pl.BlockSpec(memory_space=pl.ANY)] * n,
        out_specs=[pl.BlockSpec(memory_space=pltpu.VMEM)] * n,
        out_shape=[jax.ShapeDtypeStruct(array.shape, array.dtype) for array in arrays],
        scratch_shapes=[pltpu.SemaphoreType.DMA((n, 4))],
        compiler_params=pltpu.CompilerParams(vmem_limit_bytes=size + 2 * 1024 * 1024),
        cost_estimate=pl.CostEstimate(flops=0, bytes_accessed=size, transcendentals=0),
        name="prefetch",
    )(*[pltpu.with_memory_space_constraint(array, pltpu.HBM) for array in arrays])


def update_kernel(where, keep, slabs, tile, *refs):
    n = len(where)
    rows_refs = refs[:n]
    signs_ref, weight_ref, second_ref = refs[n : n + 3]
    new_weight_ref, new_second_ref, new_momentum_ref = refs[-7:-4]
    nw_buf, ns_buf, out_sem, keep_sem = refs[-4:]
    part, low_rank = rows_refs[0].shape
    width = signs_ref.shape[0]
    slab = width // slabs
    gain = math.sqrt(0.05) / math.sqrt(low_rank)
    back = 0.5 / math.sqrt(0.05)
    nt = (((1,), (1,)), ((), ()))
    col = lax.axis_index("col")
    firsts = [pl.multiple_of(((col ^ rel) * 2 + half) * part, part) for rel, half in where]
    stores = []
    if keep:
        half = where[0][1]
        store = pltpu.make_async_copy(
            rows_refs[0], new_momentum_ref.at[pl.ds(half * part, part)], keep_sem.at[0]
        )
        store.start()
        stores.append(store)
    rows = jnp.concatenate([ref[...] for ref in rows_refs], axis=0) * gain
    high = rows.astype(jnp.bfloat16)
    low = (rows - high.astype(jnp.float32)).astype(jnp.bfloat16)
    for k in range(slabs):
        for at in range(k * slab, (k + 1) * slab, tile):
            signs = signs_ref[at : at + tile, :]
            dense = lax.dot_general(high, signs, nt, preferred_element_type=jnp.float32)
            dense += lax.dot_general(low, signs, nt, preferred_element_type=jnp.float32)
            columns = slice(at - k * slab, at - k * slab + tile)
            for b in range(n):
                mine = dense[b * part : (b + 1) * part]
                here = (pl.ds(firsts[b], part), slice(at, at + tile))
                new_second = 0.95 * second_ref[here] + mine * mine
                bottom = new_second * lax.rsqrt(new_second) + 1e-08
                inverse = pl.reciprocal(bottom, approx=True)
                inverse = inverse * (2.0 - bottom * inverse)
                ns_buf[k * n + b, :, columns] = new_second
                nw_buf[k * n + b, :, columns] = weight_ref[here] - (mine * back) * inverse
        for b in range(n):
            slot = k * n + b
            window = (pl.ds(firsts[b], part), pl.ds(k * slab, slab))
            for kind, (buf, ref) in enumerate(
                ((nw_buf, new_weight_ref), (ns_buf, new_second_ref))
            ):
                store = pltpu.make_async_copy(
                    buf.at[slot], ref.at[window], out_sem.at[kind, slot]
                )
                store.start()
                stores.append(store)
    for store in stores:
        store.wait()


def update(row_blocks, where, keep, signs, weight, second, onto):
    part, low_rank = row_blocks[0].shape
    din_local = weight.shape[1]
    n = len(row_blocks)
    slabs = 4
    slab = din_local // slabs
    hbm = pl.BlockSpec(memory_space=pl.ANY)
    vmem = pl.BlockSpec(memory_space=pltpu.VMEM)
    in_specs = [vmem] * (n + 3)
    aliases = {}
    if onto:
        in_specs += [hbm] * 3
        aliases = {n + 3 + k: k for k in range(3)}
    size = n * part * din_local
    buf = pltpu.VMEM((slabs * n, part, slab), jnp.float32)
    return pl.pallas_call(
        functools.partial(update_kernel, where, keep, slabs, min(slab, 256)),
        in_specs=in_specs,
        out_specs=[hbm] * 3,
        out_shape=[
            jax.ShapeDtypeStruct(weight.shape, jnp.float32),
            jax.ShapeDtypeStruct(second.shape, jnp.float32),
            jax.ShapeDtypeStruct((2 * part, low_rank), jnp.float32),
        ],
        scratch_shapes=[
            buf,
            buf,
            pltpu.SemaphoreType.DMA((2, slabs * n)),
            pltpu.SemaphoreType.DMA((1,)),
        ],
        input_output_aliases=aliases,
        compiler_params=pltpu.CompilerParams(
            vmem_limit_bytes=8 * size + 8 * 1024 * 1024
        ),
        cost_estimate=pl.CostEstimate(
            flops=4 * size * low_rank, bytes_accessed=8 * size, transcendentals=2 * size
        ),
        name="update",
    )(*row_blocks, signs, weight, second, *onto)


CORE, X, Y, Z0, Z1 = 1, 2, 4, 8, 16


def exchange(value, mask):
    size = lax.axis_size("dp") * lax.axis_size("col")
    return lax.ppermute(value, AXES, [(i, i ^ mask) for i in range(size)])


def stepped(tokens, out_grad, weight, second, momentum, sign_seed, step_number):
    low_rank = momentum.shape[1]
    owner_rows = momentum.shape[0]
    total_tokens = lax.axis_size("dp") * tokens.shape[0]
    inv_root = 1.0 / jnp.sqrt(jnp.float32(low_rank))
    far0 = [(Z1 | X | Z0, 0), (Z1 | X, 0), (Z1 | Z0, 0), (Z1, 0)]
    near0 = [(Z0 | X, 0), (Z0, 0), (X, 0), (0, 0)]
    far1 = [(Z1 | X | Y, 1), (Z1 | X, 1), (Z1 | Y, 1), (Z1, 1)]
    near1 = [(Y | X, 1), (Y, 1), (X, 1), (0, 1)]

    def toward(mask, pieces):
        return [(rel ^ mask, half) for rel, half in pieces]

    part = owner_rows // 2
    pieces = far0 + near0 + far1 + near1
    seeds = (sign_seed.reshape(1, 1), step_number.reshape(1, 1))
    signs, send_a, keep_a = sketch_parts(tokens, low_rank, None, seeds)
    got_a = exchange(send_a, CORE)

    def messages(over_y, over_z):
        return [
            toward(Y, over_y),
            toward(Z0, over_z),
            toward(Y | CORE, over_y),
            toward(Z0 | CORE, over_z),
        ]

    far_out = pack(out_grad, messages(far0, far1), owner_rows, part)
    *near_out, og_c, og_own = pack(
        out_grad, messages(near0, near1) + [toward(CORE, pieces), pieces], owner_rows, part
    )
    across = exchange(keep_a + got_a, X)
    routes = (("y", Y), ("z", Z0), ("yc", Y | CORE), ("zc", Z0 | CORE))
    far_og = {name: exchange(value, mask) for value, (name, mask) in zip(far_out, routes)}
    og_c = exchange(og_c, CORE)
    send_b, keep_b = sketch_parts(tokens, low_rank, signs, None)
    got_b = exchange(send_b, CORE)
    (weight_v,) = prefetch(weight)
    (second_v,) = prefetch(second)
    sketch = (((keep_b + got_b) + across) * inv_root).astype(jnp.bfloat16)

    sk_y = exchange(sketch, Y)
    sk_z = exchange(sketch, Z0)
    sk_c = exchange(sketch, CORE)
    sk_yc = exchange(sk_y, CORE)
    sk_zc = exchange(sk_z, CORE)
    near_og = {name: exchange(value, mask) for value, (name, mask) in zip(near_out, routes)}

    scale = jnp.float32(1.0 / total_tokens)

    def packed(value, extra):
        return (value * (scale * extra)).astype(jnp.float16)

    def unpacked(value, extra):
        return value.astype(jnp.float32) * (1.0 / (scale * extra))

    def side(axis, og):
        got = {"y": (sk_y, sk_yc), "z": (sk_z, sk_zc)}[axis]
        return (sketch, sk_c, *got), (og_own, og_c, og[axis], og[axis + "c"])

    def begin(terms, first, axis):
        send, keep = project(*terms, (first, first, 0, 0), 4)
        return exchange(packed(send, 8.0), axis), keep

    def middle(state, axis):
        got, keep = state
        ahead = exchange(packed(keep[0] + unpacked(got[0], 8.0), 4.0), axis)
        return ahead, keep[1] + unpacked(got[1], 8.0)

    def finish(state):
        got, keep = state
        return keep + unpacked(got, 4.0)

    far0_state = begin(side("y", far_og), 0, X)
    far1_state = begin(side("z", far_og), 8, X)
    near0_state = begin(side("y", near_og), 4, Z0)
    near1_state = begin(side("z", near_og), 12, Y)
    far0_state = middle(far0_state, Z0)
    far1_state = middle(far1_state, Y)
    last0 = exchange(packed(finish(far0_state), 2.0), Z1)
    last1 = exchange(packed(finish(far1_state), 2.0), Z1)
    near0_state = middle(near0_state, X)
    near1_state = middle(near1_state, X)

    def momentum_half(half, near, last):
        projected = (near + unpacked(last, 2.0)) * scale
        return 0.8 * momentum[half * part : (half + 1) * part] + 0.2 * projected

    halves, others = [], []
    small = None
    for half, near_state, last in ((0, near0_state, last0), (1, near1_state, last1)):
        if small is not None:
            last, _ = lax.optimization_barrier((last, small))
        mine = momentum_half(half, finish(near_state), last)
        small = mine.astype(jnp.float16)
        from_core = exchange(small, CORE)
        from_x = exchange(small, X)
        from_xc = exchange(from_x, CORE)
        halves.append(mine)
        others.append([v.astype(jnp.float32) for v in (from_core, from_x, from_xc)])
    done = ()
    for half, rows, relatives in (
        (0, (halves[0], others[0][0]), (0, CORE)),
        (0, others[0][1:], (X, X | CORE)),
        (1, (halves[1], others[1][0]), (0, CORE)),
        (1, others[1][1:], (X, X | CORE)),
    ):
        where = tuple((rel, half) for rel in relatives)
        keep = 0 in relatives
        done = update(rows, where, keep, signs, weight_v, second_v, tuple(done))
    return tuple(done)


def solution(mesh):
    placed = (
        P("dp", "col"),
        P(AXES, None),
        P("dp", "col"),
        P("dp", "col"),
        P(AXES, None),
        P(),
        P(),
    )

    def per_device(tokens, out_grad, weight, second, momentum, sign_seed, step_number):
        args = (tokens, out_grad, weight, second, momentum, sign_seed, step_number)
        cube = mesh.shape["dp"] == Z1 * 2 // (X * 2) and mesh.shape["col"] == X * 2
        if cube and momentum.shape[0] % (2 * LANES) == 0:
            return stepped(*args)
        return general(*args)

    return jax.shard_map(
        per_device,
        mesh=mesh,
        in_specs=placed,
        out_specs=(P("dp", "col"), P("dp", "col"), P(AXES, None)),
        check_vma=False,
    )
```

```python
import functools
import math

import jax
import jax.numpy as jnp
from jax import lax
from jax.experimental import pallas as pl
from jax.experimental.pallas import tpu as pltpu
from jax.sharding import PartitionSpec as P


AXES = ("dp", "col")
LANES = 128


def low_bits(mixed):
    mixed = mixed ^ lax.shift_right_logical(mixed, 16)
    mixed = mixed * 2127912213
    mixed = mixed ^ lax.shift_right_logical(mixed, 13)
    mixed = mixed * 1103515245
    mixed = mixed ^ lax.shift_right_logical(mixed, 16)
    return mixed & (1 << 20)


def sign_table(sign_seed, step_number, first_row, row_count, low_rank):
    row_ids = first_row + lax.iota(jnp.int32, row_count)
    col_ids = lax.iota(jnp.int32, low_rank)
    flat_index = row_ids[:, None] * low_rank + col_ids[None, :]
    seeded = sign_seed[0] * 1664525 + step_number[0] * 1013904223
    return jnp.where(low_bits(flat_index * 747796405 + seeded) == 0, 1.0, -1.0)


def contract(left_rows, right_rows):
    return lax.dot_general(
        left_rows, right_rows, (((0,), (0,)), ((), ())), preferred_element_type=jnp.float32
    )


def general(tokens, out_grad, weight, second, momentum, sign_seed, step_number):
    local_tokens, din_local = tokens.shape
    low_rank = momentum.shape[1]
    owner_rows = momentum.shape[0]
    inv_root = 1.0 / jnp.sqrt(jnp.float32(low_rank))
    col_position = lax.axis_index("col")
    sign_block = sign_table(sign_seed, step_number, col_position * din_local, din_local, low_rank)
    partial_sketch = (
        jnp.dot(tokens, sign_block.astype(jnp.bfloat16), preferred_element_type=jnp.float32)
        * inv_root
    )
    quarter = lax.psum_scatter(partial_sketch, "col", scatter_dimension=0, tiled=True)
    sketch = quarter.astype(jnp.bfloat16)
    total_tokens = lax.axis_size("dp") * local_tokens
    data_count = lax.axis_size("dp")
    col_count = lax.axis_size("col")
    quarter_rows = out_grad.shape[0]
    grouped = out_grad.reshape(quarter_rows, data_count, col_count, owner_rows)
    grouped = jnp.transpose(grouped, (0, 2, 1, 3)).reshape(
        quarter_rows, col_count, data_count * owner_rows
    )
    regrouped = lax.all_to_all(grouped, "col", split_axis=1, concat_axis=0, tiled=True)
    regrouped = regrouped.reshape(quarter_rows * col_count, data_count * owner_rows)
    shard_sketch = lax.all_gather(sketch, "col", axis=0, tiled=True)
    projected = lax.psum_scatter(
        contract(regrouped, shard_sketch), "dp", scatter_dimension=0, tiled=True
    )
    projected = projected / jnp.float32(total_tokens)
    new_momentum = 0.8 * momentum + 0.2 * projected
    row_block = lax.all_gather(new_momentum, "col", axis=0, tiled=True)
    dense_grad = (
        lax.dot_general(
            row_block,
            sign_block,
            (((1,), (1,)), ((), ())),
            precision=lax.Precision.HIGHEST,
            preferred_element_type=jnp.float32,
        )
        * inv_root
    )
    new_second = 0.95 * second + 0.05 * dense_grad * dense_grad
    new_weight = weight - 0.5 * dense_grad / (jnp.sqrt(new_second) + 1e-08)
    return (new_weight, new_second, new_momentum)


def params(vmem=56 * 1024 * 1024, axes=1):
    return pltpu.CompilerParams(
        dimension_semantics=("arbitrary",) * axes, vmem_limit_bytes=vmem
    )


def pack_kernel(groups, width, part, og_ref, *refs):
    n_out = len(groups)
    outs = refs[:n_out]
    stage, in_sem, out_sem = refs[n_out:]
    me = lax.axis_index("dp") * lax.axis_size("col") + lax.axis_index("col")
    loads = []
    slot = 0
    for group in groups:
        mine = []
        for rel, half in group:
            first = pl.multiple_of((me ^ rel) * width + half * part, part)
            copy = pltpu.make_async_copy(
                og_ref.at[:, pl.ds(first, part)], stage.at[slot], in_sem.at[slot]
            )
            copy.start()
            mine.append(copy)
            slot += 1
        loads.append(mine)
    stores = []
    slot = 0
    for index, group in enumerate(groups):
        for copy in loads[index]:
            copy.wait()
        store = pltpu.make_async_copy(
            stage.at[pl.ds(slot, len(group))], outs[index], out_sem.at[index]
        )
        store.start()
        stores.append(store)
        slot += len(group)
    for store in stores:
        store.wait()


def pack(out_grad, groups, width, part):
    rows = out_grad.shape[0]
    count = sum(len(group) for group in groups)
    hbm = pl.BlockSpec(memory_space=pl.ANY)
    return pl.pallas_call(
        functools.partial(pack_kernel, groups, width, part),
        in_specs=[hbm],
        out_specs=[hbm] * len(groups),
        out_shape=[
            jax.ShapeDtypeStruct((len(group), rows, part), out_grad.dtype) for group in groups
        ],
        scratch_shapes=[
            pltpu.VMEM((count, rows, part), out_grad.dtype),
            pltpu.SemaphoreType.DMA((count,)),
            pltpu.SemaphoreType.DMA((len(groups),)),
        ],
        compiler_params=pltpu.CompilerParams(vmem_limit_bytes=8 * 1024 * 1024),
        cost_estimate=pl.CostEstimate(
            flops=0, bytes_accessed=4 * count * rows * part, transcendentals=0
        ),
        name="pack",
    )(pltpu.with_memory_space_constraint(out_grad, pltpu.HBM))


CHUNKS = 4
STRIP = 32


def sketch_kernel(first, din_local, *refs):
    if first:
        seed_ref, step_ref, *refs, seed, step, seed_sem = refs
        seed_copies = [
            pltpu.make_async_copy(seed_ref, seed, seed_sem.at[0]),
            pltpu.make_async_copy(step_ref, step, seed_sem.at[1]),
        ]
        for copy in seed_copies:
            copy.start()
        tok_ref, signs_ref, send_ref, keep_ref, tok, acc, sem = refs
    else:
        tok_ref, signs_ref, send_ref, keep_ref, tok, acc, sem = refs
    quarter, low_rank = keep_ref.shape
    chunk = din_local // CHUNKS
    col = lax.axis_index("col")
    group = col ^ (X if first else 0)
    loads = []
    for part in range(CHUNKS):
        at = pl.ds(part * chunk, chunk)
        mine = []
        for slot, rel in enumerate((CORE, 0)):
            rows = pl.ds(pl.multiple_of((group ^ rel) * quarter, quarter), quarter)
            copy = pltpu.make_async_copy(
                tok_ref.at[rows, at],
                tok.at[pl.ds(slot * quarter, quarter), at],
                sem.at[part, slot],
            )
            copy.start()
            mine.append(copy)
        loads.append(mine)
    if first:
        row_factor = low_rank * 747796405
        row_factor = (row_factor + (1 << 31)) % (1 << 32) - (1 << 31)
        local = lax.broadcasted_iota(jnp.int32, (STRIP, low_rank), 0) * row_factor
        columns = lax.broadcasted_iota(jnp.int32, (1, low_rank), 1) * 747796405
        for copy in seed_copies:
            copy.wait()
        columns = columns + (seed[...] * 1664525 + step[...] * 1013904223)
        local = local + columns
    for part in range(CHUNKS):
        at = slice(part * chunk, (part + 1) * chunk)
        if first:
            for row in range(part * chunk, (part + 1) * chunk, STRIP):
                mixed = local + (col * din_local + row) * row_factor
                strip = jnp.where(low_bits(mixed) == 0, 1.0, -1.0)
                signs_ref[row : row + STRIP, :] = strip.astype(jnp.bfloat16)
        for copy in loads[part]:
            copy.wait()
        product = jnp.dot(tok[:, at], signs_ref[at, :], preferred_element_type=jnp.float32)
        if part > 0:
            product += acc[...]
        if part < CHUNKS - 1:
            acc[...] = product
        else:
            send_ref[...] = product[:quarter]
            keep_ref[...] = product[quarter:]


def sketch_parts(tokens, low_rank, signs, seeds):
    local_tokens, din_local = tokens.shape
    half = local_tokens // 2
    quarter = half // 2
    first = signs is None
    vmem = pl.BlockSpec(memory_space=pltpu.VMEM)
    hbm = pl.BlockSpec(memory_space=pl.ANY)
    parts = [jax.ShapeDtypeStruct((quarter, low_rank), jnp.float32)] * 2
    tokens = pltpu.with_memory_space_constraint(tokens, pltpu.HBM)
    if first:
        in_specs, args = [hbm, hbm, hbm], (*seeds, tokens)
        out_shape = [jax.ShapeDtypeStruct((din_local, low_rank), jnp.bfloat16)] + parts
    else:
        in_specs, args = [hbm, vmem], (tokens, signs)
        out_shape = parts
    return pl.pallas_call(
        functools.partial(sketch_kernel, first, din_local),
        in_specs=in_specs,
        out_specs=[vmem] * len(out_shape),
        out_shape=out_shape,
        scratch_shapes=[
            pltpu.VMEM((half, din_local), tokens.dtype),
            pltpu.VMEM((half, low_rank), jnp.float32),
            pltpu.SemaphoreType.DMA((CHUNKS, 2)),
        ]
        + ([pltpu.VMEM((1, 1), jnp.int32)] * 2 + [pltpu.SemaphoreType.DMA((2,))]) * first,
        compiler_params=pltpu.CompilerParams(vmem_limit_bytes=12 * 1024 * 1024),
        cost_estimate=pl.CostEstimate(
            flops=2 * half * din_local * low_rank,
            bytes_accessed=half * din_local * 2 + din_local * low_rank * 2 + 2 * half * low_rank * 4,
            transcendentals=0,
        ),
        name="sketch",
    )(*args)


def project_kernel(n, *refs):
    send_ref, keep_ref = refs[-2:]
    count, _, part = refs[n].shape
    sketch = jnp.concatenate([ref[...] for ref in refs[:n]], axis=0)
    grads = jnp.concatenate(
        [
            jnp.concatenate([ref[j] for j in range(count)], axis=1)
            for ref in refs[n : 2 * n]
        ],
        axis=0,
    )
    total = contract(grads, sketch)
    for j in range(count):
        out_ref = send_ref if j < count // 2 else keep_ref
        out_ref[j % (count // 2)] = total[j * part : (j + 1) * part]


def project(sketches, grads, offsets, count):
    rows, low_rank = sketches[0].shape
    part = grads[0].shape[2]
    n = len(sketches)

    def block_at(offset):
        return pl.BlockSpec((count, rows, part), lambda i: (offset // count, 0, 0))

    out = jax.ShapeDtypeStruct((count // 2, part, low_rank), jnp.float32)
    return pl.pallas_call(
        functools.partial(project_kernel, n),
        grid=(1,),
        in_specs=[pl.BlockSpec((rows, low_rank), lambda i: (0, 0))] * n
        + [block_at(offset) for offset in offsets],
        out_specs=[pl.BlockSpec((count // 2, part, low_rank), lambda i: (0, 0, 0))] * 2,
        out_shape=[out] * 2,
        compiler_params=params(10 * 1024 * 1024),
        cost_estimate=pl.CostEstimate(
            flops=2 * n * count * rows * part * low_rank,
            bytes_accessed=n * (rows * low_rank + count * rows * part) * 2
            + count * low_rank * part * 4,
            transcendentals=0,
        ),
        name="project",
    )(*sketches, *grads)


def prefetch_kernel(*refs):
    n = (len(refs) - 1) // 2
    sources, targets, sem = refs[:n], refs[n : 2 * n], refs[-1]
    pieces = sem.shape[1]
    copies = []
    for at in range(pieces):
        for k, (source, target) in enumerate(zip(sources, targets)):
            rows = source.shape[0] // pieces
            window = pl.ds(at * rows, rows)
            copy = pltpu.make_async_copy(source.at[window], target.at[window], sem.at[k, at])
            copy.start()
            copies.append(copy)
    for copy in copies:
        copy.wait()


def prefetch(*arrays):
    n = len(arrays)
    size = sum(array.size * array.dtype.itemsize for array in arrays)
    return pl.pallas_call(
        prefetch_kernel,
        in_specs=[pl.BlockSpec(memory_space=pl.ANY)] * n,
        out_specs=[pl.BlockSpec(memory_space=pltpu.VMEM)] * n,
        out_shape=[jax.ShapeDtypeStruct(array.shape, array.dtype) for array in arrays],
        scratch_shapes=[pltpu.SemaphoreType.DMA((n, 4))],
        compiler_params=pltpu.CompilerParams(vmem_limit_bytes=size + 2 * 1024 * 1024),
        cost_estimate=pl.CostEstimate(flops=0, bytes_accessed=size, transcendentals=0),
        name="prefetch",
    )(*[pltpu.with_memory_space_constraint(array, pltpu.HBM) for array in arrays])


def update_kernel(where, keep, slabs, tile, *refs):
    n = len(where)
    rows_refs = refs[:n]
    signs_ref, weight_ref, second_ref = refs[n : n + 3]
    new_weight_ref, new_second_ref, new_momentum_ref = refs[-7:-4]
    nw_buf, ns_buf, out_sem, keep_sem = refs[-4:]
    part, low_rank = rows_refs[0].shape
    width = signs_ref.shape[0]
    slab = width // slabs
    gain = math.sqrt(0.05) / math.sqrt(low_rank)
    back = 0.5 / math.sqrt(0.05)
    nt = (((1,), (1,)), ((), ()))
    col = lax.axis_index("col")
    firsts = [pl.multiple_of(((col ^ rel) * 2 + half) * part, part) for rel, half in where]
    stores = []
    if keep:
        half = where[0][1]
        store = pltpu.make_async_copy(
            rows_refs[0], new_momentum_ref.at[pl.ds(half * part, part)], keep_sem.at[0]
        )
        store.start()
        stores.append(store)
    rows = jnp.concatenate([ref[...] for ref in rows_refs], axis=0) * gain
    high = rows.astype(jnp.bfloat16)
    low = (rows - high.astype(jnp.float32)).astype(jnp.bfloat16)
    for k in range(slabs):
        for at in range(k * slab, (k + 1) * slab, tile):
            signs = signs_ref[at : at + tile, :]
            dense = lax.dot_general(high, signs, nt, preferred_element_type=jnp.float32)
            dense += lax.dot_general(low, signs, nt, preferred_element_type=jnp.float32)
            columns = slice(at - k * slab, at - k * slab + tile)
            for b in range(n):
                mine = dense[b * part : (b + 1) * part]
                here = (pl.ds(firsts[b], part), slice(at, at + tile))
                new_second = 0.95 * second_ref[here] + mine * mine
                bottom = new_second * lax.rsqrt(new_second) + 1e-08
                inverse = pl.reciprocal(bottom, approx=True)
                inverse = inverse * (2.0 - bottom * inverse)
                ns_buf[k * n + b, :, columns] = new_second
                nw_buf[k * n + b, :, columns] = weight_ref[here] - (mine * back) * inverse
        for b in range(n):
            slot = k * n + b
            window = (pl.ds(firsts[b], part), pl.ds(k * slab, slab))
            for kind, (buf, ref) in enumerate(
                ((nw_buf, new_weight_ref), (ns_buf, new_second_ref))
            ):
                store = pltpu.make_async_copy(
                    buf.at[slot], ref.at[window], out_sem.at[kind, slot]
                )
                store.start()
                stores.append(store)
    for store in stores:
        store.wait()


def update(row_blocks, where, keep, signs, weight, second, onto):
    part, low_rank = row_blocks[0].shape
    din_local = weight.shape[1]
    n = len(row_blocks)
    slabs = 4
    slab = din_local // slabs
    hbm = pl.BlockSpec(memory_space=pl.ANY)
    vmem = pl.BlockSpec(memory_space=pltpu.VMEM)
    in_specs = [vmem] * (n + 3)
    aliases = {}
    if onto:
        in_specs += [hbm] * 3
        aliases = {n + 3 + k: k for k in range(3)}
    size = n * part * din_local
    buf = pltpu.VMEM((slabs * n, part, slab), jnp.float32)
    return pl.pallas_call(
        functools.partial(update_kernel, where, keep, slabs, min(slab, 256)),
        in_specs=in_specs,
        out_specs=[hbm] * 3,
        out_shape=[
            jax.ShapeDtypeStruct(weight.shape, jnp.float32),
            jax.ShapeDtypeStruct(second.shape, jnp.float32),
            jax.ShapeDtypeStruct((2 * part, low_rank), jnp.float32),
        ],
        scratch_shapes=[
            buf,
            buf,
            pltpu.SemaphoreType.DMA((2, slabs * n)),
            pltpu.SemaphoreType.DMA((1,)),
        ],
        input_output_aliases=aliases,
        compiler_params=pltpu.CompilerParams(
            vmem_limit_bytes=8 * size + 8 * 1024 * 1024
        ),
        cost_estimate=pl.CostEstimate(
            flops=4 * size * low_rank, bytes_accessed=8 * size, transcendentals=2 * size
        ),
        name="update",
    )(*row_blocks, signs, weight, second, *onto)


CORE, X, Y, Z0, Z1 = 1, 2, 4, 8, 16


def exchange(value, mask):
    size = lax.axis_size("dp") * lax.axis_size("col")
    return lax.ppermute(value, AXES, [(i, i ^ mask) for i in range(size)])


def stepped(tokens, out_grad, weight, second, momentum, sign_seed, step_number):
    low_rank = momentum.shape[1]
    owner_rows = momentum.shape[0]
    total_tokens = lax.axis_size("dp") * tokens.shape[0]
    inv_root = 1.0 / jnp.sqrt(jnp.float32(low_rank))
    far0 = [(Z1 | X | Z0, 0), (Z1 | X, 0), (Z1 | Z0, 0), (Z1, 0)]
    near0 = [(Z0 | X, 0), (Z0, 0), (X, 0), (0, 0)]
    far1 = [(Z1 | Y | X, 1), (Z1 | Y, 1), (Z1 | X, 1), (Z1, 1)]
    near1 = [(Y | X, 1), (Y, 1), (X, 1), (0, 1)]

    def toward(mask, pieces):
        return [(rel ^ mask, half) for rel, half in pieces]

    part = owner_rows // 2
    over_y, over_z = far0 + near0, far1 + near1
    og_y, og_z = pack(out_grad, [toward(Y, over_y), toward(Z0, over_z)], owner_rows, part)
    og_y = exchange(og_y, Y)
    og_z = exchange(og_z, Z0)
    seeds = (sign_seed.reshape(1, 1), step_number.reshape(1, 1))
    signs, send_a, keep_a = sketch_parts(tokens, low_rank, None, seeds)
    got_a = exchange(send_a, CORE)
    og_yc, og_zc = pack(
        out_grad, [toward(Y | CORE, over_y), toward(Z0 | CORE, over_z)], owner_rows, part
    )
    og_c, og_own = pack(
        out_grad,
        [toward(CORE, over_y + over_z), over_y + over_z],
        owner_rows,
        part,
    )
    across = exchange(keep_a + got_a, X)
    og_yc = exchange(og_yc, Y | CORE)
    og_zc = exchange(og_zc, Z0 | CORE)
    og_c = exchange(og_c, CORE)
    send_b, keep_b = sketch_parts(tokens, low_rank, signs, None)
    got_b = exchange(send_b, CORE)
    weight_v, second_v = prefetch(weight, second)
    sketch = (((keep_b + got_b) + across) * inv_root).astype(jnp.bfloat16)

    sk_y = exchange(sketch, Y)
    sk_z = exchange(sketch, Z0)
    sk_c = exchange(sketch, CORE)
    sk_yc = exchange(sk_y, CORE)
    sk_zc = exchange(sk_z, CORE)

    scale = jnp.float32(1.0 / total_tokens)

    def packed(value, extra):
        return (value * (scale * extra)).astype(jnp.float16)

    def unpacked(value, extra):
        return value.astype(jnp.float32) * (1.0 / (scale * extra))

    y_side = (sketch, sk_c, sk_y, sk_yc), (og_own, og_c, og_y, og_yc)
    z_side = (sketch, sk_c, sk_z, sk_zc), (og_own, og_c, og_z, og_zc)

    def begin(terms, offsets, axis):
        send, keep = project(*terms, offsets, 4)
        return exchange(packed(send, 8.0), axis), keep

    def middle(state, axis):
        got, keep = state
        ahead = packed(keep[0] + unpacked(got[0], 8.0), 4.0)
        return exchange(ahead, axis), keep[1] + unpacked(got[1], 8.0)

    def finish(state):
        got, keep = state
        return keep + unpacked(got, 4.0)

    far0_state = begin(y_side, (0, 0, 0, 0), X)
    far1_state = begin(z_side, (8, 8, 0, 0), Y)
    near0_state = begin(y_side, (4, 4, 4, 4), Z0)
    near1_state = begin(z_side, (12, 12, 4, 4), Y)
    far0_state = middle(far0_state, Z0)
    far1_state = middle(far1_state, X)
    last0 = exchange(packed(finish(far0_state), 2.0), Z1)
    last1 = exchange(packed(finish(far1_state), 2.0), Z1)
    near0_state = middle(near0_state, X)
    near1_state = middle(near1_state, X)

    def momentum_half(half, near, last):
        projected = (near + unpacked(last, 2.0)) * scale
        return 0.8 * momentum[half * part : (half + 1) * part] + 0.2 * projected

    halves, others = [], []
    small = None
    for half, near_state, last in ((0, near0_state, last0), (1, near1_state, last1)):
        if small is not None:
            last, _ = lax.optimization_barrier((last, small))
        mine = momentum_half(half, finish(near_state), last)
        small = mine.astype(jnp.float16)
        from_core = exchange(small, CORE)
        from_x = exchange(small, X)
        from_xc = exchange(from_x, CORE)
        halves.append(mine)
        others.append([v.astype(jnp.float32) for v in (from_core, from_x, from_xc)])
    done = ()
    for half, rows, relatives in (
        (0, (halves[0], others[0][0]), (0, CORE)),
        (0, others[0][1:], (X, X | CORE)),
        (1, (halves[1], others[1][0]), (0, CORE)),
        (1, others[1][1:], (X, X | CORE)),
    ):
        where = tuple((rel, half) for rel in relatives)
        keep = 0 in relatives
        done = update(rows, where, keep, signs, weight_v, second_v, tuple(done))
    return tuple(done)


def solution(mesh):
    placed = (
        P("dp", "col"),
        P(AXES, None),
        P("dp", "col"),
        P("dp", "col"),
        P(AXES, None),
        P(),
        P(),
    )

    def per_device(tokens, out_grad, weight, second, momentum, sign_seed, step_number):
        args = (tokens, out_grad, weight, second, momentum, sign_seed, step_number)
        cube = mesh.shape["dp"] == Z1 * 2 // (X * 2) and mesh.shape["col"] == X * 2
        if cube and momentum.shape[0] % (2 * LANES) == 0:
            return stepped(*args)
        return general(*args)

    return jax.shard_map(
        per_device,
        mesh=mesh,
        in_specs=placed,
        out_specs=(P("dp", "col"), P("dp", "col"), P(AXES, None)),
        check_vma=False,
    )
```

```python
import functools
import math

import jax
import jax.numpy as jnp
from jax import lax
from jax.experimental import pallas as pl
from jax.experimental.pallas import tpu as pltpu
from jax.sharding import PartitionSpec as P


AXES = ("dp", "col")
LANES = 128


def low_bits(mixed):
    mixed = mixed ^ lax.shift_right_logical(mixed, 16)
    mixed = mixed * 2127912213
    mixed = mixed ^ lax.shift_right_logical(mixed, 13)
    mixed = mixed * 1103515245
    mixed = mixed ^ lax.shift_right_logical(mixed, 16)
    return mixed & (1 << 20)


def sign_table(sign_seed, step_number, first_row, row_count, low_rank):
    row_ids = first_row + lax.iota(jnp.int32, row_count)
    col_ids = lax.iota(jnp.int32, low_rank)
    flat_index = row_ids[:, None] * low_rank + col_ids[None, :]
    seeded = sign_seed[0] * 1664525 + step_number[0] * 1013904223
    return jnp.where(low_bits(flat_index * 747796405 + seeded) == 0, 1.0, -1.0)


def contract(left_rows, right_rows):
    return lax.dot_general(
        left_rows, right_rows, (((0,), (0,)), ((), ())), preferred_element_type=jnp.float32
    )


def general(tokens, out_grad, weight, second, momentum, sign_seed, step_number):
    local_tokens, din_local = tokens.shape
    low_rank = momentum.shape[1]
    owner_rows = momentum.shape[0]
    inv_root = 1.0 / jnp.sqrt(jnp.float32(low_rank))
    col_position = lax.axis_index("col")
    sign_block = sign_table(sign_seed, step_number, col_position * din_local, din_local, low_rank)
    partial_sketch = (
        jnp.dot(tokens, sign_block.astype(jnp.bfloat16), preferred_element_type=jnp.float32)
        * inv_root
    )
    quarter = lax.psum_scatter(partial_sketch, "col", scatter_dimension=0, tiled=True)
    sketch = quarter.astype(jnp.bfloat16)
    total_tokens = lax.axis_size("dp") * local_tokens
    data_count = lax.axis_size("dp")
    col_count = lax.axis_size("col")
    quarter_rows = out_grad.shape[0]
    grouped = out_grad.reshape(quarter_rows, data_count, col_count, owner_rows)
    grouped = jnp.transpose(grouped, (0, 2, 1, 3)).reshape(
        quarter_rows, col_count, data_count * owner_rows
    )
    regrouped = lax.all_to_all(grouped, "col", split_axis=1, concat_axis=0, tiled=True)
    regrouped = regrouped.reshape(quarter_rows * col_count, data_count * owner_rows)
    shard_sketch = lax.all_gather(sketch, "col", axis=0, tiled=True)
    projected = lax.psum_scatter(
        contract(regrouped, shard_sketch), "dp", scatter_dimension=0, tiled=True
    )
    projected = projected / jnp.float32(total_tokens)
    new_momentum = 0.8 * momentum + 0.2 * projected
    row_block = lax.all_gather(new_momentum, "col", axis=0, tiled=True)
    dense_grad = (
        lax.dot_general(
            row_block,
            sign_block,
            (((1,), (1,)), ((), ())),
            precision=lax.Precision.HIGHEST,
            preferred_element_type=jnp.float32,
        )
        * inv_root
    )
    new_second = 0.95 * second + 0.05 * dense_grad * dense_grad
    new_weight = weight - 0.5 * dense_grad / (jnp.sqrt(new_second) + 1e-08)
    return (new_weight, new_second, new_momentum)


def params(vmem=56 * 1024 * 1024, axes=1):
    return pltpu.CompilerParams(
        dimension_semantics=("arbitrary",) * axes, vmem_limit_bytes=vmem
    )


def pack_kernel(groups, width, part, og_ref, *refs):
    n_out = len(groups)
    outs = refs[:n_out]
    stage, in_sem, out_sem = refs[n_out:]
    me = lax.axis_index("dp") * lax.axis_size("col") + lax.axis_index("col")
    loads = []
    slot = 0
    for group in groups:
        mine = []
        for rel, half in group:
            first = pl.multiple_of((me ^ rel) * width + half * part, part)
            copy = pltpu.make_async_copy(
                og_ref.at[:, pl.ds(first, part)], stage.at[slot], in_sem.at[slot]
            )
            copy.start()
            mine.append(copy)
            slot += 1
        loads.append(mine)
    stores = []
    slot = 0
    for index, group in enumerate(groups):
        for copy in loads[index]:
            copy.wait()
        store = pltpu.make_async_copy(
            stage.at[pl.ds(slot, len(group))], outs[index], out_sem.at[index]
        )
        store.start()
        stores.append(store)
        slot += len(group)
    for store in stores:
        store.wait()


def pack(out_grad, groups, width, part):
    rows = out_grad.shape[0]
    count = sum(len(group) for group in groups)
    hbm = pl.BlockSpec(memory_space=pl.ANY)
    return pl.pallas_call(
        functools.partial(pack_kernel, groups, width, part),
        in_specs=[hbm],
        out_specs=[hbm] * len(groups),
        out_shape=[
            jax.ShapeDtypeStruct((len(group), rows, part), out_grad.dtype) for group in groups
        ],
        scratch_shapes=[
            pltpu.VMEM((count, rows, part), out_grad.dtype),
            pltpu.SemaphoreType.DMA((count,)),
            pltpu.SemaphoreType.DMA((len(groups),)),
        ],
        compiler_params=pltpu.CompilerParams(vmem_limit_bytes=8 * 1024 * 1024),
        cost_estimate=pl.CostEstimate(
            flops=0, bytes_accessed=4 * count * rows * part, transcendentals=0
        ),
        name="pack",
    )(pltpu.with_memory_space_constraint(out_grad, pltpu.HBM))


CHUNKS = 4
STRIP = 32


def sketch_kernel(first, din_local, *refs):
    if first:
        seed_ref, step_ref, *refs, seed, step, seed_sem = refs
        seed_copies = [
            pltpu.make_async_copy(seed_ref, seed, seed_sem.at[0]),
            pltpu.make_async_copy(step_ref, step, seed_sem.at[1]),
        ]
        for copy in seed_copies:
            copy.start()
        tok_ref, signs_ref, send_ref, keep_ref, tok, acc, sem = refs
    else:
        tok_ref, signs_ref, send_ref, keep_ref, tok, acc, sem = refs
    quarter, low_rank = keep_ref.shape
    chunk = din_local // CHUNKS
    col = lax.axis_index("col")
    group = col ^ (X if first else 0)
    loads = []
    for part in range(CHUNKS):
        at = pl.ds(part * chunk, chunk)
        mine = []
        for slot, rel in enumerate((CORE, 0)):
            rows = pl.ds(pl.multiple_of((group ^ rel) * quarter, quarter), quarter)
            copy = pltpu.make_async_copy(
                tok_ref.at[rows, at],
                tok.at[pl.ds(slot * quarter, quarter), at],
                sem.at[part, slot],
            )
            copy.start()
            mine.append(copy)
        loads.append(mine)
    if first:
        row_factor = low_rank * 747796405
        row_factor = (row_factor + (1 << 31)) % (1 << 32) - (1 << 31)
        local = lax.broadcasted_iota(jnp.int32, (STRIP, low_rank), 0) * row_factor
        columns = lax.broadcasted_iota(jnp.int32, (1, low_rank), 1) * 747796405
        for copy in seed_copies:
            copy.wait()
        columns = columns + (seed[...] * 1664525 + step[...] * 1013904223)
        local = local + columns
    for part in range(CHUNKS):
        at = slice(part * chunk, (part + 1) * chunk)
        if first:
            for row in range(part * chunk, (part + 1) * chunk, STRIP):
                mixed = local + (col * din_local + row) * row_factor
                strip = jnp.where(low_bits(mixed) == 0, 1.0, -1.0)
                signs_ref[row : row + STRIP, :] = strip.astype(jnp.bfloat16)
        for copy in loads[part]:
            copy.wait()
        product = jnp.dot(tok[:, at], signs_ref[at, :], preferred_element_type=jnp.float32)
        if part > 0:
            product += acc[...]
        if part < CHUNKS - 1:
            acc[...] = product
        else:
            send_ref[...] = product[:quarter]
            keep_ref[...] = product[quarter:]


def sketch_parts(tokens, low_rank, signs, seeds):
    local_tokens, din_local = tokens.shape
    half = local_tokens // 2
    quarter = half // 2
    first = signs is None
    vmem = pl.BlockSpec(memory_space=pltpu.VMEM)
    hbm = pl.BlockSpec(memory_space=pl.ANY)
    parts = [jax.ShapeDtypeStruct((quarter, low_rank), jnp.float32)] * 2
    tokens = pltpu.with_memory_space_constraint(tokens, pltpu.HBM)
    if first:
        in_specs, args = [hbm, hbm, hbm], (*seeds, tokens)
        out_shape = [jax.ShapeDtypeStruct((din_local, low_rank), jnp.bfloat16)] + parts
    else:
        in_specs, args = [hbm, vmem], (tokens, signs)
        out_shape = parts
    return pl.pallas_call(
        functools.partial(sketch_kernel, first, din_local),
        in_specs=in_specs,
        out_specs=[vmem] * len(out_shape),
        out_shape=out_shape,
        scratch_shapes=[
            pltpu.VMEM((half, din_local), tokens.dtype),
            pltpu.VMEM((half, low_rank), jnp.float32),
            pltpu.SemaphoreType.DMA((CHUNKS, 2)),
        ]
        + ([pltpu.VMEM((1, 1), jnp.int32)] * 2 + [pltpu.SemaphoreType.DMA((2,))]) * first,
        compiler_params=pltpu.CompilerParams(vmem_limit_bytes=12 * 1024 * 1024),
        cost_estimate=pl.CostEstimate(
            flops=2 * half * din_local * low_rank,
            bytes_accessed=half * din_local * 2 + din_local * low_rank * 2 + 2 * half * low_rank * 4,
            transcendentals=0,
        ),
        name="sketch",
    )(*args)


def project_kernel(n, *refs):
    send_ref, keep_ref = refs[-2:]
    count, _, part = refs[n].shape
    sketch = jnp.concatenate([ref[...] for ref in refs[:n]], axis=0)
    grads = jnp.concatenate(
        [
            jnp.concatenate([ref[j] for j in range(count)], axis=1)
            for ref in refs[n : 2 * n]
        ],
        axis=0,
    )
    total = contract(grads, sketch)
    away = send_ref.shape[0]
    for j in range(count):
        out_ref, at = (send_ref, j) if j < away else (keep_ref, j - away)
        out_ref[at] = total[j * part : (j + 1) * part]


def project(sketches, grads, offsets, count, away):
    rows, low_rank = sketches[0].shape
    part = grads[0].shape[2]
    n = len(sketches)

    def block_at(offset):
        return pl.BlockSpec((count, rows, part), lambda i: (offset // count, 0, 0))

    shapes = [(away, part, low_rank), (count - away, part, low_rank)]
    return pl.pallas_call(
        functools.partial(project_kernel, n),
        grid=(1,),
        in_specs=[pl.BlockSpec((rows, low_rank), lambda i: (0, 0))] * n
        + [block_at(offset) for offset in offsets],
        out_specs=[pl.BlockSpec(shape, lambda i: (0, 0, 0)) for shape in shapes],
        out_shape=[jax.ShapeDtypeStruct(shape, jnp.float32) for shape in shapes],
        compiler_params=params(10 * 1024 * 1024),
        cost_estimate=pl.CostEstimate(
            flops=2 * n * count * rows * part * low_rank,
            bytes_accessed=n * (rows * low_rank + count * rows * part) * 2
            + count * low_rank * part * 4,
            transcendentals=0,
        ),
        name="project",
    )(*sketches, *grads)


def prefetch_kernel(*refs):
    n = (len(refs) - 1) // 2
    sources, targets, sem = refs[:n], refs[n : 2 * n], refs[-1]
    pieces = sem.shape[1]
    copies = []
    for at in range(pieces):
        for k, (source, target) in enumerate(zip(sources, targets)):
            rows = source.shape[0] // pieces
            window = pl.ds(at * rows, rows)
            copy = pltpu.make_async_copy(source.at[window], target.at[window], sem.at[k, at])
            copy.start()
            copies.append(copy)
    for copy in copies:
        copy.wait()


def prefetch(*arrays):
    n = len(arrays)
    size = sum(array.size * array.dtype.itemsize for array in arrays)
    return pl.pallas_call(
        prefetch_kernel,
        in_specs=[pl.BlockSpec(memory_space=pl.ANY)] * n,
        out_specs=[pl.BlockSpec(memory_space=pltpu.VMEM)] * n,
        out_shape=[jax.ShapeDtypeStruct(array.shape, array.dtype) for array in arrays],
        scratch_shapes=[pltpu.SemaphoreType.DMA((n, 4))],
        compiler_params=pltpu.CompilerParams(vmem_limit_bytes=size + 2 * 1024 * 1024),
        cost_estimate=pl.CostEstimate(flops=0, bytes_accessed=size, transcendentals=0),
        name="prefetch",
    )(*[pltpu.with_memory_space_constraint(array, pltpu.HBM) for array in arrays])


def update_kernel(where, keep, slabs, tile, *refs):
    n = len(where)
    rows_refs = refs[:n]
    signs_ref, weight_ref, second_ref = refs[n : n + 3]
    new_weight_ref, new_second_ref, new_momentum_ref = refs[-7:-4]
    nw_buf, ns_buf, out_sem, keep_sem = refs[-4:]
    part, low_rank = rows_refs[0].shape
    width = signs_ref.shape[0]
    slab = width // slabs
    gain = math.sqrt(0.05) / math.sqrt(low_rank)
    back = 0.5 / math.sqrt(0.05)
    nt = (((1,), (1,)), ((), ()))
    col = lax.axis_index("col")
    firsts = [pl.multiple_of(((col ^ rel) * 2 + half) * part, part) for rel, half in where]
    stores = []
    if keep:
        half = where[0][1]
        store = pltpu.make_async_copy(
            rows_refs[0], new_momentum_ref.at[pl.ds(half * part, part)], keep_sem.at[0]
        )
        store.start()
        stores.append(store)
    rows = jnp.concatenate([ref[...] for ref in rows_refs], axis=0) * gain
    high = rows.astype(jnp.bfloat16)
    low = (rows - high.astype(jnp.float32)).astype(jnp.bfloat16)
    for k in range(slabs):
        for at in range(k * slab, (k + 1) * slab, tile):
            signs = signs_ref[at : at + tile, :]
            dense = lax.dot_general(high, signs, nt, preferred_element_type=jnp.float32)
            dense += lax.dot_general(low, signs, nt, preferred_element_type=jnp.float32)
            columns = slice(at - k * slab, at - k * slab + tile)
            for b in range(n):
                mine = dense[b * part : (b + 1) * part]
                here = (pl.ds(firsts[b], part), slice(at, at + tile))
                new_second = 0.95 * second_ref[here] + mine * mine
                bottom = new_second * lax.rsqrt(new_second) + 1e-08
                inverse = pl.reciprocal(bottom, approx=True)
                inverse = inverse * (2.0 - bottom * inverse)
                ns_buf[k * n + b, :, columns] = new_second
                nw_buf[k * n + b, :, columns] = weight_ref[here] - (mine * back) * inverse
        for b in range(n):
            slot = k * n + b
            window = (pl.ds(firsts[b], part), pl.ds(k * slab, slab))
            for kind, (buf, ref) in enumerate(
                ((nw_buf, new_weight_ref), (ns_buf, new_second_ref))
            ):
                store = pltpu.make_async_copy(
                    buf.at[slot], ref.at[window], out_sem.at[kind, slot]
                )
                store.start()
                stores.append(store)
    for store in stores:
        store.wait()


def update(row_blocks, where, keep, signs, weight, second, onto):
    part, low_rank = row_blocks[0].shape
    din_local = weight.shape[1]
    n = len(row_blocks)
    slabs = 4
    slab = din_local // slabs
    hbm = pl.BlockSpec(memory_space=pl.ANY)
    vmem = pl.BlockSpec(memory_space=pltpu.VMEM)
    in_specs = [vmem] * (n + 3)
    aliases = {}
    if onto:
        in_specs += [hbm] * 3
        aliases = {n + 3 + k: k for k in range(3)}
    size = n * part * din_local
    buf = pltpu.VMEM((slabs * n, part, slab), jnp.float32)
    return pl.pallas_call(
        functools.partial(update_kernel, where, keep, slabs, min(slab, 256)),
        in_specs=in_specs,
        out_specs=[hbm] * 3,
        out_shape=[
            jax.ShapeDtypeStruct(weight.shape, jnp.float32),
            jax.ShapeDtypeStruct(second.shape, jnp.float32),
            jax.ShapeDtypeStruct((2 * part, low_rank), jnp.float32),
        ],
        scratch_shapes=[
            buf,
            buf,
            pltpu.SemaphoreType.DMA((2, slabs * n)),
            pltpu.SemaphoreType.DMA((1,)),
        ],
        input_output_aliases=aliases,
        compiler_params=pltpu.CompilerParams(
            vmem_limit_bytes=8 * size + 8 * 1024 * 1024
        ),
        cost_estimate=pl.CostEstimate(
            flops=4 * size * low_rank, bytes_accessed=8 * size, transcendentals=2 * size
        ),
        name="update",
    )(*row_blocks, signs, weight, second, *onto)


CORE, X, Y, Z0, Z1 = 1, 2, 4, 8, 16


def exchange(value, mask):
    size = lax.axis_size("dp") * lax.axis_size("col")
    return lax.ppermute(value, AXES, [(i, i ^ mask) for i in range(size)])


def stepped(tokens, out_grad, weight, second, momentum, sign_seed, step_number):
    low_rank = momentum.shape[1]
    owner_rows = momentum.shape[0]
    total_tokens = lax.axis_size("dp") * tokens.shape[0]
    inv_root = 1.0 / jnp.sqrt(jnp.float32(low_rank))
    far0 = [(Z1 | X | Z0, 0), (Z1 | X, 0), (Z1 | Z0, 0), (Z1, 0)]
    near0 = [(Z0 | X, 0), (Z0, 0), (X, 0), (0, 0)]
    far1 = [(Z1 | Y | X, 1), (Z1 | Y, 1), (Z1 | X, 1), (Z1, 1)]
    near1 = [(Y | X, 1), (Y, 1), (X, 1), (0, 1)]

    def toward(mask, pieces):
        return [(rel ^ mask, half) for rel, half in pieces]

    part = owner_rows // 2
    over_y, over_z = far0 + near0, far1 + near1
    og_y, og_z = pack(out_grad, [toward(Y, over_y), toward(Z0, over_z)], owner_rows, part)
    og_y = exchange(og_y, Y)
    og_z = exchange(og_z, Z0)
    seeds = (sign_seed.reshape(1, 1), step_number.reshape(1, 1))
    signs, send_a, keep_a = sketch_parts(tokens, low_rank, None, seeds)
    got_a = exchange(send_a, CORE)
    og_yc, og_zc = pack(
        out_grad, [toward(Y | CORE, over_y), toward(Z0 | CORE, over_z)], owner_rows, part
    )
    og_c, og_own = pack(
        out_grad,
        [toward(CORE, over_y + over_z), over_y + over_z],
        owner_rows,
        part,
    )
    across = exchange(keep_a + got_a, X)
    og_yc = exchange(og_yc, Y | CORE)
    og_zc = exchange(og_zc, Z0 | CORE)
    og_c = exchange(og_c, CORE)
    send_b, keep_b = sketch_parts(tokens, low_rank, signs, None)
    got_b = exchange(send_b, CORE)
    (weight_v,) = prefetch(weight)
    (second_v,) = prefetch(second)
    sketch = (((keep_b + got_b) + across) * inv_root).astype(jnp.bfloat16)

    sk_y = exchange(sketch, Y)
    sk_z = exchange(sketch, Z0)
    sk_c = exchange(sketch, CORE)
    sk_yc = exchange(sk_y, CORE)
    sk_zc = exchange(sk_z, CORE)

    scale = jnp.float32(1.0 / total_tokens)

    def packed(value, extra):
        return (value * (scale * extra)).astype(jnp.float16)

    def unpacked(value, extra):
        return value.astype(jnp.float32) * (1.0 / (scale * extra))

    y_side = (sketch, sk_c, sk_y, sk_yc), (og_own, og_c, og_y, og_yc)
    z_side = (sketch, sk_c, sk_z, sk_zc), (og_own, og_c, og_z, og_zc)

    def begin(terms, offsets, axis):
        send, keep = project(*terms, offsets, 4, 2)
        return exchange(packed(send, 8.0), axis), keep

    def direct(terms, offsets, masks):
        send, keep = project(*terms, offsets, 4, 3)
        total = keep[0]
        for at, mask in enumerate(masks):
            got = exchange(packed(send[at], 8.0), mask)
            total += unpacked(got, 8.0)
        return total

    def middle(state, axis):
        got, keep = state
        ahead = packed(keep[0] + unpacked(got[0], 8.0), 4.0)
        return exchange(ahead, axis), keep[1] + unpacked(got[1], 8.0)

    def finish(state):
        got, keep = state
        return keep + unpacked(got, 4.0)

    far0_total = direct(y_side, (0, 0, 0, 0), (X | Z0, X, Z0))
    far1_total = direct(z_side, (8, 8, 0, 0), (Y | X, Y, X))
    near0_state = begin(y_side, (4, 4, 4, 4), Z0)
    near1_state = begin(z_side, (12, 12, 4, 4), Y)
    last0 = exchange(packed(far0_total, 2.0), Z1)
    last1 = exchange(packed(far1_total, 2.0), Z1)
    near0_state = middle(near0_state, X)
    near1_state = middle(near1_state, X)

    def momentum_half(half, near, last):
        projected = (near + unpacked(last, 2.0)) * scale
        return 0.8 * momentum[half * part : (half + 1) * part] + 0.2 * projected

    halves, others = [], []
    small = None
    for half, near_state, last in ((0, near0_state, last0), (1, near1_state, last1)):
        if small is not None:
            last, _ = lax.optimization_barrier((last, small))
        mine = momentum_half(half, finish(near_state), last)
        small = mine.astype(jnp.float16)
        from_core = exchange(small, CORE)
        from_x = exchange(small, X)
        from_xc = exchange(from_x, CORE)
        halves.append(mine)
        others.append([v.astype(jnp.float32) for v in (from_core, from_x, from_xc)])
    done = ()
    near, far = (0, CORE), (X, X | CORE)
    for rows, where in (
        ((halves[0], others[0][0]), [(rel, 0) for rel in near]),
        (
            (halves[1], others[1][0], *others[0][1:]),
            [(rel, 1) for rel in near] + [(rel, 0) for rel in far],
        ),
        (others[1][1:], [(rel, 1) for rel in far]),
    ):
        keep = where[0][0] == 0
        done = update(rows, tuple(where), keep, signs, weight_v, second_v, tuple(done))
    return tuple(done)


def solution(mesh):
    placed = (
        P("dp", "col"),
        P(AXES, None),
        P("dp", "col"),
        P("dp", "col"),
        P(AXES, None),
        P(),
        P(),
    )

    def per_device(tokens, out_grad, weight, second, momentum, sign_seed, step_number):
        args = (tokens, out_grad, weight, second, momentum, sign_seed, step_number)
        cube = mesh.shape["dp"] == Z1 * 2 // (X * 2) and mesh.shape["col"] == X * 2
        if cube and momentum.shape[0] % (2 * LANES) == 0:
            return stepped(*args)
        return general(*args)

    return jax.shard_map(
        per_device,
        mesh=mesh,
        in_specs=placed,
        out_specs=(P("dp", "col"), P("dp", "col"), P(AXES, None)),
        check_vma=False,
    )
```

```python
import functools
import math

import jax
import jax.numpy as jnp
from jax import lax
from jax.experimental import pallas as pl
from jax.experimental.pallas import tpu as pltpu
from jax.sharding import PartitionSpec as P


AXES = ("dp", "col")
LANES = 128


def low_bits(mixed):
    mixed = mixed ^ lax.shift_right_logical(mixed, 16)
    mixed = mixed * 2127912213
    mixed = mixed ^ lax.shift_right_logical(mixed, 13)
    mixed = mixed * 1103515245
    mixed = mixed ^ lax.shift_right_logical(mixed, 16)
    return mixed & (1 << 20)


def sign_table(sign_seed, step_number, first_row, row_count, low_rank):
    row_ids = first_row + lax.iota(jnp.int32, row_count)
    col_ids = lax.iota(jnp.int32, low_rank)
    flat_index = row_ids[:, None] * low_rank + col_ids[None, :]
    seeded = sign_seed[0] * 1664525 + step_number[0] * 1013904223
    return jnp.where(low_bits(flat_index * 747796405 + seeded) == 0, 1.0, -1.0)


def contract(left_rows, right_rows):
    return lax.dot_general(
        left_rows, right_rows, (((0,), (0,)), ((), ())), preferred_element_type=jnp.float32
    )


def general(tokens, out_grad, weight, second, momentum, sign_seed, step_number):
    local_tokens, din_local = tokens.shape
    low_rank = momentum.shape[1]
    owner_rows = momentum.shape[0]
    inv_root = 1.0 / jnp.sqrt(jnp.float32(low_rank))
    col_position = lax.axis_index("col")
    sign_block = sign_table(sign_seed, step_number, col_position * din_local, din_local, low_rank)
    partial_sketch = (
        jnp.dot(tokens, sign_block.astype(jnp.bfloat16), preferred_element_type=jnp.float32)
        * inv_root
    )
    quarter = lax.psum_scatter(partial_sketch, "col", scatter_dimension=0, tiled=True)
    sketch = quarter.astype(jnp.bfloat16)
    total_tokens = lax.axis_size("dp") * local_tokens
    data_count = lax.axis_size("dp")
    col_count = lax.axis_size("col")
    quarter_rows = out_grad.shape[0]
    grouped = out_grad.reshape(quarter_rows, data_count, col_count, owner_rows)
    grouped = jnp.transpose(grouped, (0, 2, 1, 3)).reshape(
        quarter_rows, col_count, data_count * owner_rows
    )
    regrouped = lax.all_to_all(grouped, "col", split_axis=1, concat_axis=0, tiled=True)
    regrouped = regrouped.reshape(quarter_rows * col_count, data_count * owner_rows)
    shard_sketch = lax.all_gather(sketch, "col", axis=0, tiled=True)
    projected = lax.psum_scatter(
        contract(regrouped, shard_sketch), "dp", scatter_dimension=0, tiled=True
    )
    projected = projected / jnp.float32(total_tokens)
    new_momentum = 0.8 * momentum + 0.2 * projected
    row_block = lax.all_gather(new_momentum, "col", axis=0, tiled=True)
    dense_grad = (
        lax.dot_general(
            row_block,
            sign_block,
            (((1,), (1,)), ((), ())),
            precision=lax.Precision.HIGHEST,
            preferred_element_type=jnp.float32,
        )
        * inv_root
    )
    new_second = 0.95 * second + 0.05 * dense_grad * dense_grad
    new_weight = weight - 0.5 * dense_grad / (jnp.sqrt(new_second) + 1e-08)
    return (new_weight, new_second, new_momentum)


def params(vmem=56 * 1024 * 1024, axes=1):
    return pltpu.CompilerParams(
        dimension_semantics=("arbitrary",) * axes, vmem_limit_bytes=vmem
    )


def pack_kernel(groups, width, part, og_ref, *refs):
    n_out = len(groups)
    outs = refs[:n_out]
    stage, in_sem, out_sem = refs[n_out:]
    me = lax.axis_index("dp") * lax.axis_size("col") + lax.axis_index("col")
    loads = []
    slot = 0
    for group in groups:
        mine = []
        for rel, half in group:
            first = pl.multiple_of((me ^ rel) * width + half * part, part)
            copy = pltpu.make_async_copy(
                og_ref.at[:, pl.ds(first, part)], stage.at[slot], in_sem.at[slot]
            )
            copy.start()
            mine.append(copy)
            slot += 1
        loads.append(mine)
    stores = []
    slot = 0
    for index, group in enumerate(groups):
        for copy in loads[index]:
            copy.wait()
        store = pltpu.make_async_copy(
            stage.at[pl.ds(slot, len(group))], outs[index], out_sem.at[index]
        )
        store.start()
        stores.append(store)
        slot += len(group)
    for store in stores:
        store.wait()


def pack(out_grad, groups, width, part):
    rows = out_grad.shape[0]
    count = sum(len(group) for group in groups)
    hbm = pl.BlockSpec(memory_space=pl.ANY)
    return pl.pallas_call(
        functools.partial(pack_kernel, groups, width, part),
        in_specs=[hbm],
        out_specs=[hbm] * len(groups),
        out_shape=[
            jax.ShapeDtypeStruct((len(group), rows, part), out_grad.dtype) for group in groups
        ],
        scratch_shapes=[
            pltpu.VMEM((count, rows, part), out_grad.dtype),
            pltpu.SemaphoreType.DMA((count,)),
            pltpu.SemaphoreType.DMA((len(groups),)),
        ],
        compiler_params=pltpu.CompilerParams(vmem_limit_bytes=8 * 1024 * 1024),
        cost_estimate=pl.CostEstimate(
            flops=0, bytes_accessed=4 * count * rows * part, transcendentals=0
        ),
        name="pack",
    )(pltpu.with_memory_space_constraint(out_grad, pltpu.HBM))


CHUNKS = 4
STRIP = 32


def sketch_kernel(first, din_local, *refs):
    if first:
        seed_ref, step_ref, *refs, seed, step, seed_sem = refs
        seed_copies = [
            pltpu.make_async_copy(seed_ref, seed, seed_sem.at[0]),
            pltpu.make_async_copy(step_ref, step, seed_sem.at[1]),
        ]
        for copy in seed_copies:
            copy.start()
        tok_ref, signs_ref, send_ref, keep_ref, tok, acc, sem = refs
    else:
        tok_ref, signs_ref, send_ref, keep_ref, tok, acc, sem = refs
    quarter, low_rank = keep_ref.shape
    chunk = din_local // CHUNKS
    col = lax.axis_index("col")
    group = col ^ (X if first else 0)
    loads = []
    for part in range(CHUNKS):
        at = pl.ds(part * chunk, chunk)
        mine = []
        for slot, rel in enumerate((CORE, 0)):
            rows = pl.ds(pl.multiple_of((group ^ rel) * quarter, quarter), quarter)
            copy = pltpu.make_async_copy(
                tok_ref.at[rows, at],
                tok.at[pl.ds(slot * quarter, quarter), at],
                sem.at[part, slot],
            )
            copy.start()
            mine.append(copy)
        loads.append(mine)
    if first:
        row_factor = low_rank * 747796405
        row_factor = (row_factor + (1 << 31)) % (1 << 32) - (1 << 31)
        local = lax.broadcasted_iota(jnp.int32, (STRIP, low_rank), 0) * row_factor
        columns = lax.broadcasted_iota(jnp.int32, (1, low_rank), 1) * 747796405
        for copy in seed_copies:
            copy.wait()
        columns = columns + (seed[...] * 1664525 + step[...] * 1013904223)
        local = local + columns
    for part in range(CHUNKS):
        at = slice(part * chunk, (part + 1) * chunk)
        if first:
            for row in range(part * chunk, (part + 1) * chunk, STRIP):
                mixed = local + (col * din_local + row) * row_factor
                strip = jnp.where(low_bits(mixed) == 0, 1.0, -1.0)
                signs_ref[row : row + STRIP, :] = strip.astype(jnp.bfloat16)
        for copy in loads[part]:
            copy.wait()
        product = jnp.dot(tok[:, at], signs_ref[at, :], preferred_element_type=jnp.float32)
        if part > 0:
            product += acc[...]
        if part < CHUNKS - 1:
            acc[...] = product
        else:
            send_ref[...] = product[:quarter]
            keep_ref[...] = product[quarter:]


def sketch_parts(tokens, low_rank, signs, seeds):
    local_tokens, din_local = tokens.shape
    half = local_tokens // 2
    quarter = half // 2
    first = signs is None
    vmem = pl.BlockSpec(memory_space=pltpu.VMEM)
    hbm = pl.BlockSpec(memory_space=pl.ANY)
    parts = [jax.ShapeDtypeStruct((quarter, low_rank), jnp.float32)] * 2
    tokens = pltpu.with_memory_space_constraint(tokens, pltpu.HBM)
    if first:
        in_specs, args = [hbm, hbm, hbm], (*seeds, tokens)
        out_shape = [jax.ShapeDtypeStruct((din_local, low_rank), jnp.bfloat16)] + parts
    else:
        in_specs, args = [hbm, vmem], (tokens, signs)
        out_shape = parts
    return pl.pallas_call(
        functools.partial(sketch_kernel, first, din_local),
        in_specs=in_specs,
        out_specs=[vmem] * len(out_shape),
        out_shape=out_shape,
        scratch_shapes=[
            pltpu.VMEM((half, din_local), tokens.dtype),
            pltpu.VMEM((half, low_rank), jnp.float32),
            pltpu.SemaphoreType.DMA((CHUNKS, 2)),
        ]
        + ([pltpu.VMEM((1, 1), jnp.int32)] * 2 + [pltpu.SemaphoreType.DMA((2,))]) * first,
        compiler_params=pltpu.CompilerParams(vmem_limit_bytes=12 * 1024 * 1024),
        cost_estimate=pl.CostEstimate(
            flops=2 * half * din_local * low_rank,
            bytes_accessed=half * din_local * 2 + din_local * low_rank * 2 + 2 * half * low_rank * 4,
            transcendentals=0,
        ),
        name="sketch",
    )(*args)


def project_kernel(n, *refs):
    send_ref, keep_ref = refs[-2:]
    count, _, part = refs[n].shape
    sketch = jnp.concatenate([ref[...] for ref in refs[:n]], axis=0)
    grads = jnp.concatenate(
        [
            jnp.concatenate([ref[j] for j in range(count)], axis=1)
            for ref in refs[n : 2 * n]
        ],
        axis=0,
    )
    total = contract(grads, sketch)
    away = send_ref.shape[0]
    for j in range(count):
        out_ref, at = (send_ref, j) if j < away else (keep_ref, j - away)
        out_ref[at] = total[j * part : (j + 1) * part]


def project(sketches, grads, offsets, count, away):
    rows, low_rank = sketches[0].shape
    part = grads[0].shape[2]
    n = len(sketches)

    def block_at(offset):
        return pl.BlockSpec((count, rows, part), lambda i: (offset // count, 0, 0))

    shapes = [(away, part, low_rank), (count - away, part, low_rank)]
    return pl.pallas_call(
        functools.partial(project_kernel, n),
        grid=(1,),
        in_specs=[pl.BlockSpec((rows, low_rank), lambda i: (0, 0))] * n
        + [block_at(offset) for offset in offsets],
        out_specs=[pl.BlockSpec(shape, lambda i: (0, 0, 0)) for shape in shapes],
        out_shape=[jax.ShapeDtypeStruct(shape, jnp.float32) for shape in shapes],
        compiler_params=params(10 * 1024 * 1024),
        cost_estimate=pl.CostEstimate(
            flops=2 * n * count * rows * part * low_rank,
            bytes_accessed=n * (rows * low_rank + count * rows * part) * 2
            + count * low_rank * part * 4,
            transcendentals=0,
        ),
        name="project",
    )(*sketches, *grads)


def prefetch_kernel(*refs):
    n = (len(refs) - 1) // 2
    sources, targets, sem = refs[:n], refs[n : 2 * n], refs[-1]
    pieces = sem.shape[1]
    copies = []
    for at in range(pieces):
        for k, (source, target) in enumerate(zip(sources, targets)):
            rows = source.shape[0] // pieces
            window = pl.ds(at * rows, rows)
            copy = pltpu.make_async_copy(source.at[window], target.at[window], sem.at[k, at])
            copy.start()
            copies.append(copy)
    for copy in copies:
        copy.wait()


def prefetch(*arrays):
    n = len(arrays)
    size = sum(array.size * array.dtype.itemsize for array in arrays)
    return pl.pallas_call(
        prefetch_kernel,
        in_specs=[pl.BlockSpec(memory_space=pl.ANY)] * n,
        out_specs=[pl.BlockSpec(memory_space=pltpu.VMEM)] * n,
        out_shape=[jax.ShapeDtypeStruct(array.shape, array.dtype) for array in arrays],
        scratch_shapes=[pltpu.SemaphoreType.DMA((n, 4))],
        compiler_params=pltpu.CompilerParams(vmem_limit_bytes=size + 2 * 1024 * 1024),
        cost_estimate=pl.CostEstimate(flops=0, bytes_accessed=size, transcendentals=0),
        name="prefetch",
    )(*[pltpu.with_memory_space_constraint(array, pltpu.HBM) for array in arrays])


def update_kernel(where, keep, slabs, tile, *refs):
    n = len(where)
    rows_refs = refs[:n]
    signs_ref, weight_ref, second_ref = refs[n : n + 3]
    new_weight_ref, new_second_ref, new_momentum_ref = refs[-7:-4]
    nw_buf, ns_buf, out_sem, keep_sem = refs[-4:]
    part, low_rank = rows_refs[0].shape
    width = signs_ref.shape[0]
    slab = width // slabs
    gain = math.sqrt(0.05) / math.sqrt(low_rank)
    back = 0.5 / math.sqrt(0.05)
    nt = (((1,), (1,)), ((), ()))
    col = lax.axis_index("col")
    firsts = [pl.multiple_of(((col ^ rel) * 2 + half) * part, part) for rel, half in where]
    stores = []
    if keep:
        half = where[0][1]
        store = pltpu.make_async_copy(
            rows_refs[0], new_momentum_ref.at[pl.ds(half * part, part)], keep_sem.at[0]
        )
        store.start()
        stores.append(store)
    rows = jnp.concatenate([ref[...] for ref in rows_refs], axis=0) * gain
    high = rows.astype(jnp.bfloat16)
    low = (rows - high.astype(jnp.float32)).astype(jnp.bfloat16)
    for k in range(slabs):
        for at in range(k * slab, (k + 1) * slab, tile):
            signs = signs_ref[at : at + tile, :]
            dense = lax.dot_general(high, signs, nt, preferred_element_type=jnp.float32)
            dense += lax.dot_general(low, signs, nt, preferred_element_type=jnp.float32)
            columns = slice(at - k * slab, at - k * slab + tile)
            for b in range(n):
                mine = dense[b * part : (b + 1) * part]
                here = (pl.ds(firsts[b], part), slice(at, at + tile))
                new_second = 0.95 * second_ref[here] + mine * mine
                bottom = new_second * lax.rsqrt(new_second) + 1e-08
                inverse = pl.reciprocal(bottom, approx=True)
                inverse = inverse * (2.0 - bottom * inverse)
                ns_buf[k * n + b, :, columns] = new_second
                nw_buf[k * n + b, :, columns] = weight_ref[here] - (mine * back) * inverse
        for b in range(n):
            slot = k * n + b
            window = (pl.ds(firsts[b], part), pl.ds(k * slab, slab))
            for kind, (buf, ref) in enumerate(
                ((nw_buf, new_weight_ref), (ns_buf, new_second_ref))
            ):
                store = pltpu.make_async_copy(
                    buf.at[slot], ref.at[window], out_sem.at[kind, slot]
                )
                store.start()
                stores.append(store)
    for store in stores:
        store.wait()


def update(row_blocks, where, keep, signs, weight, second, onto):
    part, low_rank = row_blocks[0].shape
    din_local = weight.shape[1]
    n = len(row_blocks)
    slabs = 4
    slab = din_local // slabs
    hbm = pl.BlockSpec(memory_space=pl.ANY)
    vmem = pl.BlockSpec(memory_space=pltpu.VMEM)
    in_specs = [vmem] * (n + 3)
    aliases = {}
    if onto:
        in_specs += [hbm] * 3
        aliases = {n + 3 + k: k for k in range(3)}
    size = n * part * din_local
    buf = pltpu.VMEM((slabs * n, part, slab), jnp.float32)
    return pl.pallas_call(
        functools.partial(update_kernel, where, keep, slabs, min(slab, 256)),
        in_specs=in_specs,
        out_specs=[hbm] * 3,
        out_shape=[
            jax.ShapeDtypeStruct(weight.shape, jnp.float32),
            jax.ShapeDtypeStruct(second.shape, jnp.float32),
            jax.ShapeDtypeStruct((2 * part, low_rank), jnp.float32),
        ],
        scratch_shapes=[
            buf,
            buf,
            pltpu.SemaphoreType.DMA((2, slabs * n)),
            pltpu.SemaphoreType.DMA((1,)),
        ],
        input_output_aliases=aliases,
        compiler_params=pltpu.CompilerParams(
            vmem_limit_bytes=8 * size + 8 * 1024 * 1024
        ),
        cost_estimate=pl.CostEstimate(
            flops=4 * size * low_rank, bytes_accessed=8 * size, transcendentals=2 * size
        ),
        name="update",
    )(*row_blocks, signs, weight, second, *onto)


CORE, X, Y, Z0, Z1 = 1, 2, 4, 8, 16


def exchange(value, mask):
    size = lax.axis_size("dp") * lax.axis_size("col")
    return lax.ppermute(value, AXES, [(i, i ^ mask) for i in range(size)])


def stepped(tokens, out_grad, weight, second, momentum, sign_seed, step_number):
    low_rank = momentum.shape[1]
    owner_rows = momentum.shape[0]
    total_tokens = lax.axis_size("dp") * tokens.shape[0]
    inv_root = 1.0 / jnp.sqrt(jnp.float32(low_rank))
    far0 = [(Z1 | X | Z0, 0), (Z1 | X, 0), (Z1 | Z0, 0), (Z1, 0)]
    near0 = [(Y | X, 0), (Y, 0), (X, 0), (0, 0)]
    far1 = [(Z1 | Y | X, 1), (Z1 | Y, 1), (Z1 | X, 1), (Z1, 1)]
    near1 = [(Z0 | X, 1), (Z0, 1), (X, 1), (0, 1)]

    def toward(mask, pieces):
        return [(rel ^ mask, half) for rel, half in pieces]

    part = owner_rows // 2
    over_y, over_z = far0 + near1, far1 + near0
    og_y, og_z = pack(out_grad, [toward(Y, over_y), toward(Z0, over_z)], owner_rows, part)
    og_y = exchange(og_y, Y)
    og_z = exchange(og_z, Z0)
    seeds = (sign_seed.reshape(1, 1), step_number.reshape(1, 1))
    signs, send_a, keep_a = sketch_parts(tokens, low_rank, None, seeds)
    got_a = exchange(send_a, CORE)
    og_yc, og_zc = pack(
        out_grad, [toward(Y | CORE, over_y), toward(Z0 | CORE, over_z)], owner_rows, part
    )
    og_c, og_own = pack(
        out_grad,
        [toward(CORE, over_y + over_z), over_y + over_z],
        owner_rows,
        part,
    )
    across = exchange(keep_a + got_a, X)
    og_yc = exchange(og_yc, Y | CORE)
    og_zc = exchange(og_zc, Z0 | CORE)
    og_c = exchange(og_c, CORE)
    send_b, keep_b = sketch_parts(tokens, low_rank, signs, None)
    got_b = exchange(send_b, CORE)
    (weight_v,) = prefetch(weight)
    (second_v,) = prefetch(second)
    sketch = (((keep_b + got_b) + across) * inv_root).astype(jnp.bfloat16)

    sk_y = exchange(sketch, Y)
    sk_z = exchange(sketch, Z0)
    sk_c = exchange(sketch, CORE)
    sk_yc = exchange(sk_y, CORE)
    sk_zc = exchange(sk_z, CORE)

    scale = jnp.float32(1.0 / total_tokens)

    def packed(value, extra):
        return (value * (scale * extra)).astype(jnp.float16)

    def unpacked(value, extra):
        return value.astype(jnp.float32) * (1.0 / (scale * extra))

    y_side = (sketch, sk_c, sk_y, sk_yc), (og_own, og_c, og_y, og_yc)
    z_side = (sketch, sk_c, sk_z, sk_zc), (og_own, og_c, og_z, og_zc)

    def begin(terms, offsets, axis):
        send, keep = project(*terms, offsets, 4, 2)
        return exchange(packed(send, 8.0), axis), keep

    def direct(terms, offsets, masks):
        send, keep = project(*terms, offsets, 4, 3)
        total = keep[0]
        for at, mask in enumerate(masks):
            got = exchange(packed(send[at], 8.0), mask)
            total += unpacked(got, 8.0)
        return total

    def middle(state, axis):
        got, keep = state
        ahead = packed(keep[0] + unpacked(got[0], 8.0), 4.0)
        return exchange(ahead, axis), keep[1] + unpacked(got[1], 8.0)

    def finish(state):
        got, keep = state
        return keep + unpacked(got, 4.0)

    far0_total = direct(y_side, (0, 0, 0, 0), (X | Z0, X, Z0))
    far1_total = direct(z_side, (8, 8, 0, 0), (Y | X, Y, X))
    near0_state = begin(z_side, (12, 12, 4, 4), Y)
    near1_state = begin(y_side, (4, 4, 4, 4), Z0)
    last0 = exchange(packed(far0_total, 2.0), Z1)
    last1 = exchange(packed(far1_total, 2.0), Z1)
    near0_state = middle(near0_state, X)
    near1_state = middle(near1_state, X)

    def momentum_half(half, near, last):
        projected = (near + unpacked(last, 2.0)) * scale
        return 0.8 * momentum[half * part : (half + 1) * part] + 0.2 * projected

    halves, others = [], []
    small = None
    for half, near_state, last in ((0, near0_state, last0), (1, near1_state, last1)):
        if small is not None:
            last, _ = lax.optimization_barrier((last, small))
        mine = momentum_half(half, finish(near_state), last)
        small = mine.astype(jnp.float16)
        from_core = exchange(small, CORE)
        from_x = exchange(small, X)
        from_xc = exchange(from_x, CORE)
        halves.append(mine)
        others.append([v.astype(jnp.float32) for v in (from_core, from_x, from_xc)])
    done = ()
    near, far = (0, CORE), (X, X | CORE)
    for rows, where in (
        ((halves[0], others[0][0]), [(rel, 0) for rel in near]),
        (
            (halves[1], others[1][0], *others[0][1:]),
            [(rel, 1) for rel in near] + [(rel, 0) for rel in far],
        ),
        (others[1][1:], [(rel, 1) for rel in far]),
    ):
        keep = where[0][0] == 0
        done = update(rows, tuple(where), keep, signs, weight_v, second_v, tuple(done))
    return tuple(done)


def solution(mesh):
    placed = (
        P("dp", "col"),
        P(AXES, None),
        P("dp", "col"),
        P("dp", "col"),
        P(AXES, None),
        P(),
        P(),
    )

    def per_device(tokens, out_grad, weight, second, momentum, sign_seed, step_number):
        args = (tokens, out_grad, weight, second, momentum, sign_seed, step_number)
        cube = mesh.shape["dp"] == Z1 * 2 // (X * 2) and mesh.shape["col"] == X * 2
        if cube and momentum.shape[0] % (2 * LANES) == 0:
            return stepped(*args)
        return general(*args)

    return jax.shard_map(
        per_device,
        mesh=mesh,
        in_specs=placed,
        out_specs=(P("dp", "col"), P("dp", "col"), P(AXES, None)),
        check_vma=False,
    )
```

```python
import functools
import math

import jax
import jax.numpy as jnp
from jax import lax
from jax.experimental import pallas as pl
from jax.experimental.pallas import tpu as pltpu
from jax.sharding import PartitionSpec as P


AXES = ("dp", "col")
LANES = 128


def low_bits(mixed):
    mixed = mixed ^ lax.shift_right_logical(mixed, 16)
    mixed = mixed * 2127912213
    mixed = mixed ^ lax.shift_right_logical(mixed, 13)
    mixed = mixed * 1103515245
    mixed = mixed ^ lax.shift_right_logical(mixed, 16)
    return mixed & (1 << 20)


def sign_table(sign_seed, step_number, first_row, row_count, low_rank):
    row_ids = first_row + lax.iota(jnp.int32, row_count)
    col_ids = lax.iota(jnp.int32, low_rank)
    flat_index = row_ids[:, None] * low_rank + col_ids[None, :]
    seeded = sign_seed[0] * 1664525 + step_number[0] * 1013904223
    return jnp.where(low_bits(flat_index * 747796405 + seeded) == 0, 1.0, -1.0)


def contract(left_rows, right_rows):
    return lax.dot_general(
        left_rows, right_rows, (((0,), (0,)), ((), ())), preferred_element_type=jnp.float32
    )


def general(tokens, out_grad, weight, second, momentum, sign_seed, step_number):
    local_tokens, din_local = tokens.shape
    low_rank = momentum.shape[1]
    owner_rows = momentum.shape[0]
    inv_root = 1.0 / jnp.sqrt(jnp.float32(low_rank))
    col_position = lax.axis_index("col")
    sign_block = sign_table(sign_seed, step_number, col_position * din_local, din_local, low_rank)
    partial_sketch = (
        jnp.dot(tokens, sign_block.astype(jnp.bfloat16), preferred_element_type=jnp.float32)
        * inv_root
    )
    quarter = lax.psum_scatter(partial_sketch, "col", scatter_dimension=0, tiled=True)
    sketch = quarter.astype(jnp.bfloat16)
    total_tokens = lax.axis_size("dp") * local_tokens
    data_count = lax.axis_size("dp")
    col_count = lax.axis_size("col")
    quarter_rows = out_grad.shape[0]
    grouped = out_grad.reshape(quarter_rows, data_count, col_count, owner_rows)
    grouped = jnp.transpose(grouped, (0, 2, 1, 3)).reshape(
        quarter_rows, col_count, data_count * owner_rows
    )
    regrouped = lax.all_to_all(grouped, "col", split_axis=1, concat_axis=0, tiled=True)
    regrouped = regrouped.reshape(quarter_rows * col_count, data_count * owner_rows)
    shard_sketch = lax.all_gather(sketch, "col", axis=0, tiled=True)
    projected = lax.psum_scatter(
        contract(regrouped, shard_sketch), "dp", scatter_dimension=0, tiled=True
    )
    projected = projected / jnp.float32(total_tokens)
    new_momentum = 0.8 * momentum + 0.2 * projected
    row_block = lax.all_gather(new_momentum, "col", axis=0, tiled=True)
    dense_grad = (
        lax.dot_general(
            row_block,
            sign_block,
            (((1,), (1,)), ((), ())),
            precision=lax.Precision.HIGHEST,
            preferred_element_type=jnp.float32,
        )
        * inv_root
    )
    new_second = 0.95 * second + 0.05 * dense_grad * dense_grad
    new_weight = weight - 0.5 * dense_grad / (jnp.sqrt(new_second) + 1e-08)
    return (new_weight, new_second, new_momentum)


def params(vmem=56 * 1024 * 1024, axes=1):
    return pltpu.CompilerParams(
        dimension_semantics=("arbitrary",) * axes, vmem_limit_bytes=vmem
    )


def pack_kernel(groups, width, part, og_ref, *refs):
    n_out = len(groups)
    outs = refs[:n_out]
    stage, in_sem, out_sem = refs[n_out:]
    me = lax.axis_index("dp") * lax.axis_size("col") + lax.axis_index("col")
    loads = []
    slot = 0
    for group in groups:
        mine = []
        for rel, half in group:
            first = pl.multiple_of((me ^ rel) * width + half * part, part)
            copy = pltpu.make_async_copy(
                og_ref.at[:, pl.ds(first, part)], stage.at[slot], in_sem.at[slot]
            )
            copy.start()
            mine.append(copy)
            slot += 1
        loads.append(mine)
    stores = []
    slot = 0
    for index, group in enumerate(groups):
        for copy in loads[index]:
            copy.wait()
        store = pltpu.make_async_copy(
            stage.at[pl.ds(slot, len(group))], outs[index], out_sem.at[index]
        )
        store.start()
        stores.append(store)
        slot += len(group)
    for store in stores:
        store.wait()


def pack(out_grad, groups, width, part):
    rows = out_grad.shape[0]
    count = sum(len(group) for group in groups)
    hbm = pl.BlockSpec(memory_space=pl.ANY)
    return pl.pallas_call(
        functools.partial(pack_kernel, groups, width, part),
        in_specs=[hbm],
        out_specs=[hbm] * len(groups),
        out_shape=[
            jax.ShapeDtypeStruct((len(group), rows, part), out_grad.dtype) for group in groups
        ],
        scratch_shapes=[
            pltpu.VMEM((count, rows, part), out_grad.dtype),
            pltpu.SemaphoreType.DMA((count,)),
            pltpu.SemaphoreType.DMA((len(groups),)),
        ],
        compiler_params=pltpu.CompilerParams(vmem_limit_bytes=8 * 1024 * 1024),
        cost_estimate=pl.CostEstimate(
            flops=0, bytes_accessed=4 * count * rows * part, transcendentals=0
        ),
        name="pack",
    )(pltpu.with_memory_space_constraint(out_grad, pltpu.HBM))


CHUNKS = 4
STRIP = 32


def sketch_kernel(first, din_local, *refs):
    if first:
        seed_ref, step_ref, *refs, seed, step, seed_sem = refs
        seed_copies = [
            pltpu.make_async_copy(seed_ref, seed, seed_sem.at[0]),
            pltpu.make_async_copy(step_ref, step, seed_sem.at[1]),
        ]
        for copy in seed_copies:
            copy.start()
        tok_ref, signs_ref, send_ref, keep_ref, tok, acc, sem = refs
    else:
        tok_ref, signs_ref, send_ref, keep_ref, tok, acc, sem = refs
    quarter, low_rank = keep_ref.shape
    chunk = din_local // CHUNKS
    col = lax.axis_index("col")
    group = col ^ (X if first else 0)
    loads = []
    for part in range(CHUNKS):
        at = pl.ds(part * chunk, chunk)
        mine = []
        for slot, rel in enumerate((CORE, 0)):
            rows = pl.ds(pl.multiple_of((group ^ rel) * quarter, quarter), quarter)
            copy = pltpu.make_async_copy(
                tok_ref.at[rows, at],
                tok.at[pl.ds(slot * quarter, quarter), at],
                sem.at[part, slot],
            )
            copy.start()
            mine.append(copy)
        loads.append(mine)
    if first:
        row_factor = low_rank * 747796405
        row_factor = (row_factor + (1 << 31)) % (1 << 32) - (1 << 31)
        local = lax.broadcasted_iota(jnp.int32, (STRIP, low_rank), 0) * row_factor
        columns = lax.broadcasted_iota(jnp.int32, (1, low_rank), 1) * 747796405
        for copy in seed_copies:
            copy.wait()
        columns = columns + (seed[...] * 1664525 + step[...] * 1013904223)
        local = local + columns
    for part in range(CHUNKS):
        at = slice(part * chunk, (part + 1) * chunk)
        if first:
            for row in range(part * chunk, (part + 1) * chunk, STRIP):
                mixed = local + (col * din_local + row) * row_factor
                strip = jnp.where(low_bits(mixed) == 0, 1.0, -1.0)
                signs_ref[row : row + STRIP, :] = strip.astype(jnp.bfloat16)
        for copy in loads[part]:
            copy.wait()
        product = jnp.dot(tok[:, at], signs_ref[at, :], preferred_element_type=jnp.float32)
        if part > 0:
            product += acc[...]
        if part < CHUNKS - 1:
            acc[...] = product
        else:
            send_ref[...] = product[:quarter]
            keep_ref[...] = product[quarter:]


def sketch_parts(tokens, low_rank, signs, seeds):
    local_tokens, din_local = tokens.shape
    half = local_tokens // 2
    quarter = half // 2
    first = signs is None
    vmem = pl.BlockSpec(memory_space=pltpu.VMEM)
    hbm = pl.BlockSpec(memory_space=pl.ANY)
    parts = [jax.ShapeDtypeStruct((quarter, low_rank), jnp.float32)] * 2
    tokens = pltpu.with_memory_space_constraint(tokens, pltpu.HBM)
    if first:
        in_specs, args = [hbm, hbm, hbm], (*seeds, tokens)
        out_shape = [jax.ShapeDtypeStruct((din_local, low_rank), jnp.bfloat16)] + parts
    else:
        in_specs, args = [hbm, vmem], (tokens, signs)
        out_shape = parts
    return pl.pallas_call(
        functools.partial(sketch_kernel, first, din_local),
        in_specs=in_specs,
        out_specs=[vmem] * len(out_shape),
        out_shape=out_shape,
        scratch_shapes=[
            pltpu.VMEM((half, din_local), tokens.dtype),
            pltpu.VMEM((half, low_rank), jnp.float32),
            pltpu.SemaphoreType.DMA((CHUNKS, 2)),
        ]
        + ([pltpu.VMEM((1, 1), jnp.int32)] * 2 + [pltpu.SemaphoreType.DMA((2,))]) * first,
        compiler_params=pltpu.CompilerParams(vmem_limit_bytes=12 * 1024 * 1024),
        cost_estimate=pl.CostEstimate(
            flops=2 * half * din_local * low_rank,
            bytes_accessed=half * din_local * 2 + din_local * low_rank * 2 + 2 * half * low_rank * 4,
            transcendentals=0,
        ),
        name="sketch",
    )(*args)


def project_kernel(n, *refs):
    send_ref, keep_ref = refs[-2:]
    count, _, part = refs[n].shape
    sketch = jnp.concatenate([ref[...] for ref in refs[:n]], axis=0)
    grads = jnp.concatenate(
        [
            jnp.concatenate([ref[j] for j in range(count)], axis=1)
            for ref in refs[n : 2 * n]
        ],
        axis=0,
    )
    total = contract(grads, sketch)
    away = send_ref.shape[0]
    for j in range(count):
        out_ref, at = (send_ref, j) if j < away else (keep_ref, j - away)
        out_ref[at] = total[j * part : (j + 1) * part]


def project(sketches, grads, offsets, count, away):
    rows, low_rank = sketches[0].shape
    part = grads[0].shape[2]
    n = len(sketches)

    def block_at(offset):
        return pl.BlockSpec((count, rows, part), lambda i: (offset // count, 0, 0))

    shapes = [(away, part, low_rank), (count - away, part, low_rank)]
    return pl.pallas_call(
        functools.partial(project_kernel, n),
        grid=(1,),
        in_specs=[pl.BlockSpec((rows, low_rank), lambda i: (0, 0))] * n
        + [block_at(offset) for offset in offsets],
        out_specs=[pl.BlockSpec(shape, lambda i: (0, 0, 0)) for shape in shapes],
        out_shape=[jax.ShapeDtypeStruct(shape, jnp.float32) for shape in shapes],
        compiler_params=params(10 * 1024 * 1024),
        cost_estimate=pl.CostEstimate(
            flops=2 * n * count * rows * part * low_rank,
            bytes_accessed=n * (rows * low_rank + count * rows * part) * 2
            + count * low_rank * part * 4,
            transcendentals=0,
        ),
        name="project",
    )(*sketches, *grads)


def prefetch_kernel(*refs):
    n = (len(refs) - 1) // 2
    sources, targets, sem = refs[:n], refs[n : 2 * n], refs[-1]
    pieces = sem.shape[1]
    copies = []
    for at in range(pieces):
        for k, (source, target) in enumerate(zip(sources, targets)):
            rows = source.shape[0] // pieces
            window = pl.ds(at * rows, rows)
            copy = pltpu.make_async_copy(source.at[window], target.at[window], sem.at[k, at])
            copy.start()
            copies.append(copy)
    for copy in copies:
        copy.wait()


def prefetch(*arrays):
    n = len(arrays)
    size = sum(array.size * array.dtype.itemsize for array in arrays)
    return pl.pallas_call(
        prefetch_kernel,
        in_specs=[pl.BlockSpec(memory_space=pl.ANY)] * n,
        out_specs=[pl.BlockSpec(memory_space=pltpu.VMEM)] * n,
        out_shape=[jax.ShapeDtypeStruct(array.shape, array.dtype) for array in arrays],
        scratch_shapes=[pltpu.SemaphoreType.DMA((n, 4))],
        compiler_params=pltpu.CompilerParams(vmem_limit_bytes=size + 2 * 1024 * 1024),
        cost_estimate=pl.CostEstimate(flops=0, bytes_accessed=size, transcendentals=0),
        name="prefetch",
    )(*[pltpu.with_memory_space_constraint(array, pltpu.HBM) for array in arrays])


def update_kernel(where, keep, slabs, tile, *refs):
    n = len(where)
    rows_refs = refs[:n]
    signs_ref, weight_ref, second_ref = refs[n : n + 3]
    new_weight_ref, new_second_ref, new_momentum_ref = refs[-7:-4]
    nw_buf, ns_buf, out_sem, keep_sem = refs[-4:]
    part, low_rank = rows_refs[0].shape
    width = signs_ref.shape[0]
    slab = width // slabs
    gain = math.sqrt(0.05) / math.sqrt(low_rank)
    back = 0.5 / math.sqrt(0.05)
    nt = (((1,), (1,)), ((), ()))
    col = lax.axis_index("col")
    firsts = [pl.multiple_of(((col ^ rel) * 2 + half) * part, part) for rel, half in where]
    stores = []
    if keep:
        half = where[0][1]
        store = pltpu.make_async_copy(
            rows_refs[0], new_momentum_ref.at[pl.ds(half * part, part)], keep_sem.at[0]
        )
        store.start()
        stores.append(store)
    rows = jnp.concatenate([ref[...] for ref in rows_refs], axis=0) * gain
    high = rows.astype(jnp.bfloat16)
    low = (rows - high.astype(jnp.float32)).astype(jnp.bfloat16)
    for k in range(slabs):
        for at in range(k * slab, (k + 1) * slab, tile):
            signs = signs_ref[at : at + tile, :]
            dense = lax.dot_general(high, signs, nt, preferred_element_type=jnp.float32)
            dense += lax.dot_general(low, signs, nt, preferred_element_type=jnp.float32)
            columns = slice(at - k * slab, at - k * slab + tile)
            for b in range(n):
                mine = dense[b * part : (b + 1) * part]
                here = (pl.ds(firsts[b], part), slice(at, at + tile))
                new_second = 0.95 * second_ref[here] + mine * mine
                bottom = new_second * lax.rsqrt(new_second) + 1e-08
                inverse = pl.reciprocal(bottom, approx=True)
                inverse = inverse * (2.0 - bottom * inverse)
                ns_buf[k * n + b, :, columns] = new_second
                nw_buf[k * n + b, :, columns] = weight_ref[here] - (mine * back) * inverse
        for b in range(n):
            slot = k * n + b
            window = (pl.ds(firsts[b], part), pl.ds(k * slab, slab))
            for kind, (buf, ref) in enumerate(
                ((nw_buf, new_weight_ref), (ns_buf, new_second_ref))
            ):
                store = pltpu.make_async_copy(
                    buf.at[slot], ref.at[window], out_sem.at[kind, slot]
                )
                store.start()
                stores.append(store)
    for store in stores:
        store.wait()


def update(row_blocks, where, keep, signs, weight, second, onto):
    part, low_rank = row_blocks[0].shape
    din_local = weight.shape[1]
    n = len(row_blocks)
    slabs = 4
    slab = din_local // slabs
    hbm = pl.BlockSpec(memory_space=pl.ANY)
    vmem = pl.BlockSpec(memory_space=pltpu.VMEM)
    in_specs = [vmem] * (n + 3)
    aliases = {}
    if onto:
        in_specs += [hbm] * 3
        aliases = {n + 3 + k: k for k in range(3)}
    size = n * part * din_local
    buf = pltpu.VMEM((slabs * n, part, slab), jnp.float32)
    return pl.pallas_call(
        functools.partial(update_kernel, where, keep, slabs, min(slab, 256)),
        in_specs=in_specs,
        out_specs=[hbm] * 3,
        out_shape=[
            jax.ShapeDtypeStruct(weight.shape, jnp.float32),
            jax.ShapeDtypeStruct(second.shape, jnp.float32),
            jax.ShapeDtypeStruct((2 * part, low_rank), jnp.float32),
        ],
        scratch_shapes=[
            buf,
            buf,
            pltpu.SemaphoreType.DMA((2, slabs * n)),
            pltpu.SemaphoreType.DMA((1,)),
        ],
        input_output_aliases=aliases,
        compiler_params=pltpu.CompilerParams(
            vmem_limit_bytes=8 * size + 8 * 1024 * 1024
        ),
        cost_estimate=pl.CostEstimate(
            flops=4 * size * low_rank, bytes_accessed=8 * size, transcendentals=2 * size
        ),
        name="update",
    )(*row_blocks, signs, weight, second, *onto)


CORE, X, Y, Z0, Z1 = 1, 2, 4, 8, 16


def exchange(value, mask):
    size = lax.axis_size("dp") * lax.axis_size("col")
    return lax.ppermute(value, AXES, [(i, i ^ mask) for i in range(size)])


def stepped(tokens, out_grad, weight, second, momentum, sign_seed, step_number):
    low_rank = momentum.shape[1]
    owner_rows = momentum.shape[0]
    total_tokens = lax.axis_size("dp") * tokens.shape[0]
    inv_root = 1.0 / jnp.sqrt(jnp.float32(low_rank))
    far0 = [(Z1 | X | Z0, 0), (Z1 | X, 0), (Z1 | Z0, 0), (Z1, 0)]
    near0 = [(Z0 | X, 0), (X, 0), (Z0, 0), (0, 0)]
    far1 = [(Z1 | Y | X, 1), (Z1 | Y, 1), (Z1 | X, 1), (Z1, 1)]
    near1 = [(Y | X, 1), (Y, 1), (X, 1), (0, 1)]

    def toward(mask, pieces):
        return [(rel ^ mask, half) for rel, half in pieces]

    part = owner_rows // 2
    over_y, over_z = far0 + near0, far1 + near1
    og_y, og_z = pack(out_grad, [toward(Y, over_y), toward(Z0, over_z)], owner_rows, part)
    og_y = exchange(og_y, Y)
    og_z = exchange(og_z, Z0)
    seeds = (sign_seed.reshape(1, 1), step_number.reshape(1, 1))
    signs, send_a, keep_a = sketch_parts(tokens, low_rank, None, seeds)
    got_a = exchange(send_a, CORE)
    og_yc, og_zc = pack(
        out_grad, [toward(Y | CORE, over_y), toward(Z0 | CORE, over_z)], owner_rows, part
    )
    og_c, og_own = pack(
        out_grad,
        [toward(CORE, over_y + over_z), over_y + over_z],
        owner_rows,
        part,
    )
    across = exchange(keep_a + got_a, X)
    og_yc = exchange(og_yc, Y | CORE)
    og_zc = exchange(og_zc, Z0 | CORE)
    og_c = exchange(og_c, CORE)
    send_b, keep_b = sketch_parts(tokens, low_rank, signs, None)
    got_b = exchange(send_b, CORE)
    (weight_v,) = prefetch(weight)
    (second_v,) = prefetch(second)
    sketch = (((keep_b + got_b) + across) * inv_root).astype(jnp.bfloat16)

    sk_y = exchange(sketch, Y)
    sk_z = exchange(sketch, Z0)
    sk_c = exchange(sketch, CORE)
    sk_yc = exchange(sk_y, CORE)
    sk_zc = exchange(sk_z, CORE)

    scale = jnp.float32(1.0 / total_tokens)

    def packed(value, extra):
        return (value * (scale * extra)).astype(jnp.float16)

    def unpacked(value, extra):
        return value.astype(jnp.float32) * (1.0 / (scale * extra))

    y_side = (sketch, sk_c, sk_y, sk_yc), (og_own, og_c, og_y, og_yc)
    z_side = (sketch, sk_c, sk_z, sk_zc), (og_own, og_c, og_z, og_zc)

    def begin(terms, offsets, axis):
        send, keep = project(*terms, offsets, 4, 2)
        return exchange(packed(send, 8.0), axis), keep

    def direct(terms, offsets, masks):
        send, keep = project(*terms, offsets, 4, 3)
        total = keep[0]
        for at, mask in enumerate(masks):
            got = exchange(packed(send[at], 8.0), mask)
            total += unpacked(got, 8.0)
        return total

    def middle(state, axis):
        got, keep = state
        ahead = packed(keep[0] + unpacked(got[0], 8.0), 4.0)
        return exchange(ahead, axis), keep[1] + unpacked(got[1], 8.0)

    def finish(state):
        got, keep = state
        return keep + unpacked(got, 4.0)

    far0_total = direct(y_side, (0, 0, 0, 0), (X | Z0, X, Z0))
    far1_total = direct(z_side, (8, 8, 0, 0), (Y | X, Y, X))
    near0_state = begin(y_side, (4, 4, 4, 4), X)
    near1_state = begin(z_side, (12, 12, 4, 4), Y)
    last0 = exchange(packed(far0_total, 2.0), Z1)
    far1_small = packed(far1_total, 2.0)
    last1 = exchange(far1_small, Z1)
    near0_state = middle(near0_state, Z0)
    near1_state = middle(near1_state, X)

    def momentum_half(half, near, last):
        projected = (near + unpacked(last, 2.0)) * scale
        return 0.8 * momentum[half * part : (half + 1) * part] + 0.2 * projected

    halves, others = [], []
    small = None
    for half, near_state, last in ((0, near0_state, last0), (1, near1_state, last1)):
        if small is not None:
            last, _ = lax.optimization_barrier((last, small))
        mine = momentum_half(half, finish(near_state), last)
        small = mine.astype(jnp.float16)
        from_core = exchange(small, CORE)
        from_x = exchange(small, X)
        from_xc = exchange(from_x, CORE)
        halves.append(mine)
        others.append([v.astype(jnp.float32) for v in (from_core, from_x, from_xc)])
    done = ()
    near, far = (0, CORE), (X, X | CORE)
    for half, rows, relatives in (
        (0, (halves[0], others[0][0]), near),
        (0, others[0][1:], far),
        (1, (halves[1], others[1][0]), near),
        (1, others[1][1:], far),
    ):
        where = [(rel, half) for rel in relatives]
        keep = where[0][0] == 0
        done = update(rows, tuple(where), keep, signs, weight_v, second_v, tuple(done))
    return tuple(done)


def solution(mesh):
    placed = (
        P("dp", "col"),
        P(AXES, None),
        P("dp", "col"),
        P("dp", "col"),
        P(AXES, None),
        P(),
        P(),
    )

    def per_device(tokens, out_grad, weight, second, momentum, sign_seed, step_number):
        args = (tokens, out_grad, weight, second, momentum, sign_seed, step_number)
        cube = mesh.shape["dp"] == Z1 * 2 // (X * 2) and mesh.shape["col"] == X * 2
        if cube and momentum.shape[0] % (2 * LANES) == 0:
            return stepped(*args)
        return general(*args)

    return jax.shard_map(
        per_device,
        mesh=mesh,
        in_specs=placed,
        out_specs=(P("dp", "col"), P("dp", "col"), P(AXES, None)),
        check_vma=False,
    )
```

```python
import functools
import math

import jax
import jax.numpy as jnp
from jax import lax
from jax.experimental import pallas as pl
from jax.experimental.pallas import tpu as pltpu
from jax.sharding import PartitionSpec as P


AXES = ("dp", "col")
LANES = 128


def low_bits(mixed):
    mixed = mixed ^ lax.shift_right_logical(mixed, 16)
    mixed = mixed * 2127912213
    mixed = mixed ^ lax.shift_right_logical(mixed, 13)
    mixed = mixed * 1103515245
    mixed = mixed ^ lax.shift_right_logical(mixed, 16)
    return mixed & (1 << 20)


def sign_table(sign_seed, step_number, first_row, row_count, low_rank):
    row_ids = first_row + lax.iota(jnp.int32, row_count)
    col_ids = lax.iota(jnp.int32, low_rank)
    flat_index = row_ids[:, None] * low_rank + col_ids[None, :]
    seeded = sign_seed[0] * 1664525 + step_number[0] * 1013904223
    return jnp.where(low_bits(flat_index * 747796405 + seeded) == 0, 1.0, -1.0)


def contract(left_rows, right_rows):
    return lax.dot_general(
        left_rows, right_rows, (((0,), (0,)), ((), ())), preferred_element_type=jnp.float32
    )


def general(tokens, out_grad, weight, second, momentum, sign_seed, step_number):
    local_tokens, din_local = tokens.shape
    low_rank = momentum.shape[1]
    owner_rows = momentum.shape[0]
    inv_root = 1.0 / jnp.sqrt(jnp.float32(low_rank))
    col_position = lax.axis_index("col")
    sign_block = sign_table(sign_seed, step_number, col_position * din_local, din_local, low_rank)
    partial_sketch = (
        jnp.dot(tokens, sign_block.astype(jnp.bfloat16), preferred_element_type=jnp.float32)
        * inv_root
    )
    quarter = lax.psum_scatter(partial_sketch, "col", scatter_dimension=0, tiled=True)
    sketch = quarter.astype(jnp.bfloat16)
    total_tokens = lax.axis_size("dp") * local_tokens
    data_count = lax.axis_size("dp")
    col_count = lax.axis_size("col")
    quarter_rows = out_grad.shape[0]
    grouped = out_grad.reshape(quarter_rows, data_count, col_count, owner_rows)
    grouped = jnp.transpose(grouped, (0, 2, 1, 3)).reshape(
        quarter_rows, col_count, data_count * owner_rows
    )
    regrouped = lax.all_to_all(grouped, "col", split_axis=1, concat_axis=0, tiled=True)
    regrouped = regrouped.reshape(quarter_rows * col_count, data_count * owner_rows)
    shard_sketch = lax.all_gather(sketch, "col", axis=0, tiled=True)
    projected = lax.psum_scatter(
        contract(regrouped, shard_sketch), "dp", scatter_dimension=0, tiled=True
    )
    projected = projected / jnp.float32(total_tokens)
    new_momentum = 0.8 * momentum + 0.2 * projected
    row_block = lax.all_gather(new_momentum, "col", axis=0, tiled=True)
    dense_grad = (
        lax.dot_general(
            row_block,
            sign_block,
            (((1,), (1,)), ((), ())),
            precision=lax.Precision.HIGHEST,
            preferred_element_type=jnp.float32,
        )
        * inv_root
    )
    new_second = 0.95 * second + 0.05 * dense_grad * dense_grad
    new_weight = weight - 0.5 * dense_grad / (jnp.sqrt(new_second) + 1e-08)
    return (new_weight, new_second, new_momentum)


def params(vmem=56 * 1024 * 1024, axes=1):
    return pltpu.CompilerParams(
        dimension_semantics=("arbitrary",) * axes, vmem_limit_bytes=vmem
    )


def pack_kernel(groups, width, part, og_ref, *refs):
    n_out = len(groups)
    outs = refs[:n_out]
    stage, in_sem, out_sem = refs[n_out:]
    me = lax.axis_index("dp") * lax.axis_size("col") + lax.axis_index("col")
    loads = []
    slot = 0
    for group in groups:
        mine = []
        for rel, half in group:
            first = pl.multiple_of((me ^ rel) * width + half * part, part)
            copy = pltpu.make_async_copy(
                og_ref.at[:, pl.ds(first, part)], stage.at[slot], in_sem.at[slot]
            )
            copy.start()
            mine.append(copy)
            slot += 1
        loads.append(mine)
    stores = []
    slot = 0
    for index, group in enumerate(groups):
        for copy in loads[index]:
            copy.wait()
        store = pltpu.make_async_copy(
            stage.at[pl.ds(slot, len(group))], outs[index], out_sem.at[index]
        )
        store.start()
        stores.append(store)
        slot += len(group)
    for store in stores:
        store.wait()


def pack(out_grad, groups, width, part):
    rows = out_grad.shape[0]
    count = sum(len(group) for group in groups)
    hbm = pl.BlockSpec(memory_space=pl.ANY)
    return pl.pallas_call(
        functools.partial(pack_kernel, groups, width, part),
        in_specs=[hbm],
        out_specs=[hbm] * len(groups),
        out_shape=[
            jax.ShapeDtypeStruct((len(group), rows, part), out_grad.dtype) for group in groups
        ],
        scratch_shapes=[
            pltpu.VMEM((count, rows, part), out_grad.dtype),
            pltpu.SemaphoreType.DMA((count,)),
            pltpu.SemaphoreType.DMA((len(groups),)),
        ],
        compiler_params=pltpu.CompilerParams(vmem_limit_bytes=8 * 1024 * 1024),
        cost_estimate=pl.CostEstimate(
            flops=0, bytes_accessed=4 * count * rows * part, transcendentals=0
        ),
        name="pack",
    )(pltpu.with_memory_space_constraint(out_grad, pltpu.HBM))


CHUNKS = 4
STRIP = 32


def sketch_kernel(first, din_local, *refs):
    if first:
        seed_ref, step_ref, *refs, seed, step, seed_sem = refs
        seed_copies = [
            pltpu.make_async_copy(seed_ref, seed, seed_sem.at[0]),
            pltpu.make_async_copy(step_ref, step, seed_sem.at[1]),
        ]
        for copy in seed_copies:
            copy.start()
        tok_ref, signs_ref, send_ref, keep_ref, tok, acc, sem = refs
    else:
        tok_ref, signs_ref, send_ref, keep_ref, tok, acc, sem = refs
    quarter, low_rank = keep_ref.shape
    chunk = din_local // CHUNKS
    col = lax.axis_index("col")
    group = col ^ (X if first else 0)
    loads = []
    for part in range(CHUNKS):
        at = pl.ds(part * chunk, chunk)
        mine = []
        for slot, rel in enumerate((CORE, 0)):
            rows = pl.ds(pl.multiple_of((group ^ rel) * quarter, quarter), quarter)
            copy = pltpu.make_async_copy(
                tok_ref.at[rows, at],
                tok.at[pl.ds(slot * quarter, quarter), at],
                sem.at[part, slot],
            )
            copy.start()
            mine.append(copy)
        loads.append(mine)
    if first:
        row_factor = low_rank * 747796405
        row_factor = (row_factor + (1 << 31)) % (1 << 32) - (1 << 31)
        local = lax.broadcasted_iota(jnp.int32, (STRIP, low_rank), 0) * row_factor
        columns = lax.broadcasted_iota(jnp.int32, (1, low_rank), 1) * 747796405
        for copy in seed_copies:
            copy.wait()
        columns = columns + (seed[...] * 1664525 + step[...] * 1013904223)
        local = local + columns
    for part in range(CHUNKS):
        at = slice(part * chunk, (part + 1) * chunk)
        if first:
            for row in range(part * chunk, (part + 1) * chunk, STRIP):
                mixed = local + (col * din_local + row) * row_factor
                strip = jnp.where(low_bits(mixed) == 0, 1.0, -1.0)
                signs_ref[row : row + STRIP, :] = strip.astype(jnp.bfloat16)
        for copy in loads[part]:
            copy.wait()
        product = jnp.dot(tok[:, at], signs_ref[at, :], preferred_element_type=jnp.float32)
        if part > 0:
            product += acc[...]
        if part < CHUNKS - 1:
            acc[...] = product
        else:
            send_ref[...] = product[:quarter]
            keep_ref[...] = product[quarter:]


def sketch_parts(tokens, low_rank, signs, seeds):
    local_tokens, din_local = tokens.shape
    half = local_tokens // 2
    quarter = half // 2
    first = signs is None
    vmem = pl.BlockSpec(memory_space=pltpu.VMEM)
    hbm = pl.BlockSpec(memory_space=pl.ANY)
    parts = [jax.ShapeDtypeStruct((quarter, low_rank), jnp.float32)] * 2
    tokens = pltpu.with_memory_space_constraint(tokens, pltpu.HBM)
    if first:
        in_specs, args = [hbm, hbm, hbm], (*seeds, tokens)
        out_shape = [jax.ShapeDtypeStruct((din_local, low_rank), jnp.bfloat16)] + parts
    else:
        in_specs, args = [hbm, vmem], (tokens, signs)
        out_shape = parts
    return pl.pallas_call(
        functools.partial(sketch_kernel, first, din_local),
        in_specs=in_specs,
        out_specs=[vmem] * len(out_shape),
        out_shape=out_shape,
        scratch_shapes=[
            pltpu.VMEM((half, din_local), tokens.dtype),
            pltpu.VMEM((half, low_rank), jnp.float32),
            pltpu.SemaphoreType.DMA((CHUNKS, 2)),
        ]
        + ([pltpu.VMEM((1, 1), jnp.int32)] * 2 + [pltpu.SemaphoreType.DMA((2,))]) * first,
        compiler_params=pltpu.CompilerParams(vmem_limit_bytes=12 * 1024 * 1024),
        cost_estimate=pl.CostEstimate(
            flops=2 * half * din_local * low_rank,
            bytes_accessed=half * din_local * 2 + din_local * low_rank * 2 + 2 * half * low_rank * 4,
            transcendentals=0,
        ),
        name="sketch",
    )(*args)


def project_kernel(n, *refs):
    send_ref, keep_ref = refs[-2:]
    count, _, part = refs[n].shape
    sketch = jnp.concatenate([ref[...] for ref in refs[:n]], axis=0)
    grads = jnp.concatenate(
        [
            jnp.concatenate([ref[j] for j in range(count)], axis=1)
            for ref in refs[n : 2 * n]
        ],
        axis=0,
    )
    total = contract(grads, sketch)
    away = send_ref.shape[0]
    for j in range(count):
        out_ref, at = (send_ref, j) if j < away else (keep_ref, j - away)
        out_ref[at] = total[j * part : (j + 1) * part]


def project(sketches, grads, offsets, count, away):
    rows, low_rank = sketches[0].shape
    part = grads[0].shape[2]
    n = len(sketches)

    def block_at(offset):
        return pl.BlockSpec((count, rows, part), lambda i: (offset // count, 0, 0))

    shapes = [(away, part, low_rank), (count - away, part, low_rank)]
    return pl.pallas_call(
        functools.partial(project_kernel, n),
        grid=(1,),
        in_specs=[pl.BlockSpec((rows, low_rank), lambda i: (0, 0))] * n
        + [block_at(offset) for offset in offsets],
        out_specs=[pl.BlockSpec(shape, lambda i: (0, 0, 0)) for shape in shapes],
        out_shape=[jax.ShapeDtypeStruct(shape, jnp.float32) for shape in shapes],
        compiler_params=params(10 * 1024 * 1024),
        cost_estimate=pl.CostEstimate(
            flops=2 * n * count * rows * part * low_rank,
            bytes_accessed=n * (rows * low_rank + count * rows * part) * 2
            + count * low_rank * part * 4,
            transcendentals=0,
        ),
        name="project",
    )(*sketches, *grads)


def prefetch_kernel(*refs):
    n = (len(refs) - 1) // 2
    sources, targets, sem = refs[:n], refs[n : 2 * n], refs[-1]
    pieces = sem.shape[1]
    copies = []
    for at in range(pieces):
        for k, (source, target) in enumerate(zip(sources, targets)):
            rows = source.shape[0] // pieces
            window = pl.ds(at * rows, rows)
            copy = pltpu.make_async_copy(source.at[window], target.at[window], sem.at[k, at])
            copy.start()
            copies.append(copy)
    for copy in copies:
        copy.wait()


def prefetch(*arrays):
    n = len(arrays)
    size = sum(array.size * array.dtype.itemsize for array in arrays)
    return pl.pallas_call(
        prefetch_kernel,
        in_specs=[pl.BlockSpec(memory_space=pl.ANY)] * n,
        out_specs=[pl.BlockSpec(memory_space=pltpu.VMEM)] * n,
        out_shape=[jax.ShapeDtypeStruct(array.shape, array.dtype) for array in arrays],
        scratch_shapes=[pltpu.SemaphoreType.DMA((n, 4))],
        compiler_params=pltpu.CompilerParams(vmem_limit_bytes=size + 2 * 1024 * 1024),
        cost_estimate=pl.CostEstimate(flops=0, bytes_accessed=size, transcendentals=0),
        name="prefetch",
    )(*[pltpu.with_memory_space_constraint(array, pltpu.HBM) for array in arrays])


def update_kernel(where, keep, slabs, tile, *refs):
    n = len(where)
    rows_refs = refs[:n]
    signs_ref, weight_ref, second_ref = refs[n : n + 3]
    new_weight_ref, new_second_ref, new_momentum_ref = refs[-7:-4]
    nw_buf, ns_buf, out_sem, keep_sem = refs[-4:]
    part, low_rank = rows_refs[0].shape
    width = signs_ref.shape[0]
    slab = width // slabs
    gain = math.sqrt(0.05) / math.sqrt(low_rank)
    back = 0.5 / math.sqrt(0.05)
    nt = (((1,), (1,)), ((), ()))
    col = lax.axis_index("col")
    firsts = [pl.multiple_of(((col ^ rel) * 2 + half) * part, part) for rel, half in where]
    stores = []
    if keep:
        half = where[0][1]
        store = pltpu.make_async_copy(
            rows_refs[0], new_momentum_ref.at[pl.ds(half * part, part)], keep_sem.at[0]
        )
        store.start()
        stores.append(store)
    rows = jnp.concatenate([ref[...] for ref in rows_refs], axis=0) * gain
    high = rows.astype(jnp.bfloat16)
    low = (rows - high.astype(jnp.float32)).astype(jnp.bfloat16)
    for k in range(slabs):
        for at in range(k * slab, (k + 1) * slab, tile):
            signs = signs_ref[at : at + tile, :]
            dense = lax.dot_general(high, signs, nt, preferred_element_type=jnp.float32)
            dense += lax.dot_general(low, signs, nt, preferred_element_type=jnp.float32)
            columns = slice(at - k * slab, at - k * slab + tile)
            for b in range(n):
                mine = dense[b * part : (b + 1) * part]
                here = (pl.ds(firsts[b], part), slice(at, at + tile))
                new_second = 0.95 * second_ref[here] + mine * mine
                bottom = new_second * lax.rsqrt(new_second) + 1e-08
                inverse = pl.reciprocal(bottom, approx=True)
                inverse = inverse * (2.0 - bottom * inverse)
                ns_buf[k * n + b, :, columns] = new_second
                nw_buf[k * n + b, :, columns] = weight_ref[here] - (mine * back) * inverse
        for b in range(n):
            slot = k * n + b
            window = (pl.ds(firsts[b], part), pl.ds(k * slab, slab))
            for kind, (buf, ref) in enumerate(
                ((nw_buf, new_weight_ref), (ns_buf, new_second_ref))
            ):
                store = pltpu.make_async_copy(
                    buf.at[slot], ref.at[window], out_sem.at[kind, slot]
                )
                store.start()
                stores.append(store)
    for store in stores:
        store.wait()


def update(row_blocks, where, keep, signs, weight, second, onto):
    part, low_rank = row_blocks[0].shape
    din_local = weight.shape[1]
    n = len(row_blocks)
    slabs = 4
    slab = din_local // slabs
    hbm = pl.BlockSpec(memory_space=pl.ANY)
    vmem = pl.BlockSpec(memory_space=pltpu.VMEM)
    in_specs = [vmem] * (n + 3)
    aliases = {}
    if onto:
        in_specs += [hbm] * 3
        aliases = {n + 3 + k: k for k in range(3)}
    size = n * part * din_local
    buf = pltpu.VMEM((slabs * n, part, slab), jnp.float32)
    return pl.pallas_call(
        functools.partial(update_kernel, where, keep, slabs, min(slab, 256)),
        in_specs=in_specs,
        out_specs=[hbm] * 3,
        out_shape=[
            jax.ShapeDtypeStruct(weight.shape, jnp.float32),
            jax.ShapeDtypeStruct(second.shape, jnp.float32),
            jax.ShapeDtypeStruct((2 * part, low_rank), jnp.float32),
        ],
        scratch_shapes=[
            buf,
            buf,
            pltpu.SemaphoreType.DMA((2, slabs * n)),
            pltpu.SemaphoreType.DMA((1,)),
        ],
        input_output_aliases=aliases,
        compiler_params=pltpu.CompilerParams(
            vmem_limit_bytes=8 * size + 8 * 1024 * 1024
        ),
        cost_estimate=pl.CostEstimate(
            flops=4 * size * low_rank, bytes_accessed=8 * size, transcendentals=2 * size
        ),
        name="update",
    )(*row_blocks, signs, weight, second, *onto)


CORE, X, Y, Z0, Z1 = 1, 2, 4, 8, 16


def exchange(value, mask):
    size = lax.axis_size("dp") * lax.axis_size("col")
    return lax.ppermute(value, AXES, [(i, i ^ mask) for i in range(size)])


def stepped(tokens, out_grad, weight, second, momentum, sign_seed, step_number):
    low_rank = momentum.shape[1]
    owner_rows = momentum.shape[0]
    total_tokens = lax.axis_size("dp") * tokens.shape[0]
    inv_root = 1.0 / jnp.sqrt(jnp.float32(low_rank))
    far0 = [(Z1 | X | Z0, 0), (Z1 | X, 0), (Z1 | Z0, 0), (Z1, 0)]
    near0 = [(Z0 | X, 0), (Z0, 0), (X, 0), (0, 0)]
    far1 = [(Z1 | Y | X, 1), (Z1 | Y, 1), (Z1 | X, 1), (Z1, 1)]
    near1 = [(Y | X, 1), (Y, 1), (X, 1), (0, 1)]

    def toward(mask, pieces):
        return [(rel ^ mask, half) for rel, half in pieces]

    part = owner_rows // 2
    over_y, over_z = far0 + near0, far1 + near1
    og_y, og_z = pack(out_grad, [toward(Y, over_y), toward(Z0, over_z)], owner_rows, part)
    og_y = exchange(og_y, Y)
    og_z = exchange(og_z, Z0)
    seeds = (sign_seed.reshape(1, 1), step_number.reshape(1, 1))
    signs, send_a, keep_a = sketch_parts(tokens, low_rank, None, seeds)
    got_a = exchange(send_a, CORE)
    og_yc, og_zc = pack(
        out_grad, [toward(Y | CORE, over_y), toward(Z0 | CORE, over_z)], owner_rows, part
    )
    og_c, og_own = pack(
        out_grad,
        [toward(CORE, over_y + over_z), over_y + over_z],
        owner_rows,
        part,
    )
    across = exchange(keep_a + got_a, X)
    og_yc = exchange(og_yc, Y | CORE)
    og_zc = exchange(og_zc, Z0 | CORE)
    og_c = exchange(og_c, CORE)
    send_b, keep_b = sketch_parts(tokens, low_rank, signs, None)
    got_b = exchange(send_b, CORE)
    (weight_v,) = prefetch(weight)
    (second_v,) = prefetch(second)
    sketch = (((keep_b + got_b) + across) * inv_root).astype(jnp.bfloat16)

    sk_y = exchange(sketch, Y)
    sk_z = exchange(sketch, Z0)
    sk_c = exchange(sketch, CORE)
    sk_yc = exchange(sk_y, CORE)
    sk_zc = exchange(sk_z, CORE)

    scale = jnp.float32(1.0 / total_tokens)

    def packed(value, extra):
        return (value * (scale * extra)).astype(jnp.float16)

    def unpacked(value, extra):
        return value.astype(jnp.float32) * (1.0 / (scale * extra))

    y_side = (sketch, sk_c, sk_y, sk_yc), (og_own, og_c, og_y, og_yc)
    z_side = (sketch, sk_c, sk_z, sk_zc), (og_own, og_c, og_z, og_zc)

    def begin(terms, offsets, axis):
        send, keep = project(*terms, offsets, 4, 2)
        return exchange(packed(send, 8.0), axis), keep

    def direct(terms, offsets, masks):
        send, keep = project(*terms, offsets, 4, 3)
        total = keep[0]
        for at, mask in enumerate(masks):
            got = exchange(packed(send[at], 8.0), mask)
            total += unpacked(got, 8.0)
        return total

    def middle(state, axis):
        got, keep = state
        ahead = packed(keep[0] + unpacked(got[0], 8.0), 4.0)
        return exchange(ahead, axis), keep[1] + unpacked(got[1], 8.0)

    def finish(state):
        got, keep = state
        return keep + unpacked(got, 4.0)

    far0_total = direct(y_side, (0, 0, 0, 0), (X | Z0, X, Z0))
    far1_total = direct(z_side, (8, 8, 0, 0), (Y | X, Y, X))
    near0_state = begin(y_side, (4, 4, 4, 4), Z0)
    near1_state = begin(z_side, (12, 12, 4, 4), Y)
    last0 = exchange(packed(far0_total, 2.0), Z1)
    last1 = exchange(packed(far1_total, 2.0), Z1)
    near0_state = middle(near0_state, X)
    near1_state = middle(near1_state, X)

    def momentum_half(half, near, last):
        projected = (near + unpacked(last, 2.0)) * scale
        return 0.8 * momentum[half * part : (half + 1) * part] + 0.2 * projected

    halves, others = [], []
    small = None
    for half, near_state, last in ((0, near0_state, last0), (1, near1_state, last1)):
        if small is not None:
            last, _ = lax.optimization_barrier((last, small))
        mine = momentum_half(half, finish(near_state), last)
        small = mine.astype(jnp.float16)
        from_core = exchange(small, CORE)
        from_x = exchange(small, X)
        from_xc = exchange(from_x, CORE)
        halves.append(mine)
        others.append([v.astype(jnp.float32) for v in (from_core, from_x, from_xc)])
    done = ()
    near, far = (0, CORE), (X, X | CORE)
    for half, rows, relatives in (
        (0, (halves[0], others[0][0]), near),
        (1, (halves[1], others[1][0]), near),
        (0, others[0][1:], far),
        (1, others[1][1:], far),
    ):
        where = [(rel, half) for rel in relatives]
        keep = where[0][0] == 0
        done = update(rows, tuple(where), keep, signs, weight_v, second_v, tuple(done))
    return tuple(done)


def solution(mesh):
    placed = (
        P("dp", "col"),
        P(AXES, None),
        P("dp", "col"),
        P("dp", "col"),
        P(AXES, None),
        P(),
        P(),
    )

    def per_device(tokens, out_grad, weight, second, momentum, sign_seed, step_number):
        args = (tokens, out_grad, weight, second, momentum, sign_seed, step_number)
        cube = mesh.shape["dp"] == Z1 * 2 // (X * 2) and mesh.shape["col"] == X * 2
        if cube and momentum.shape[0] % (2 * LANES) == 0:
            return stepped(*args)
        return general(*args)

    return jax.shard_map(
        per_device,
        mesh=mesh,
        in_specs=placed,
        out_specs=(P("dp", "col"), P("dp", "col"), P(AXES, None)),
        check_vma=False,
    )
```

```python
import functools
import math

import jax
import jax.numpy as jnp
from jax import lax
from jax.experimental import pallas as pl
from jax.experimental.pallas import tpu as pltpu
from jax.sharding import PartitionSpec as P


AXES = ("dp", "col")
LANES = 128


def low_bits(mixed):
    mixed = mixed ^ lax.shift_right_logical(mixed, 16)
    mixed = mixed * 2127912213
    mixed = mixed ^ lax.shift_right_logical(mixed, 13)
    mixed = mixed * 1103515245
    mixed = mixed ^ lax.shift_right_logical(mixed, 16)
    return mixed & (1 << 20)


def sign_table(sign_seed, step_number, first_row, row_count, low_rank):
    row_ids = first_row + lax.iota(jnp.int32, row_count)
    col_ids = lax.iota(jnp.int32, low_rank)
    flat_index = row_ids[:, None] * low_rank + col_ids[None, :]
    seeded = sign_seed[0] * 1664525 + step_number[0] * 1013904223
    return jnp.where(low_bits(flat_index * 747796405 + seeded) == 0, 1.0, -1.0)


def contract(left_rows, right_rows):
    return lax.dot_general(
        left_rows, right_rows, (((0,), (0,)), ((), ())), preferred_element_type=jnp.float32
    )


def general(tokens, out_grad, weight, second, momentum, sign_seed, step_number):
    local_tokens, din_local = tokens.shape
    low_rank = momentum.shape[1]
    owner_rows = momentum.shape[0]
    inv_root = 1.0 / jnp.sqrt(jnp.float32(low_rank))
    col_position = lax.axis_index("col")
    sign_block = sign_table(sign_seed, step_number, col_position * din_local, din_local, low_rank)
    partial_sketch = (
        jnp.dot(tokens, sign_block.astype(jnp.bfloat16), preferred_element_type=jnp.float32)
        * inv_root
    )
    quarter = lax.psum_scatter(partial_sketch, "col", scatter_dimension=0, tiled=True)
    sketch = quarter.astype(jnp.bfloat16)
    total_tokens = lax.axis_size("dp") * local_tokens
    data_count = lax.axis_size("dp")
    col_count = lax.axis_size("col")
    quarter_rows = out_grad.shape[0]
    grouped = out_grad.reshape(quarter_rows, data_count, col_count, owner_rows)
    grouped = jnp.transpose(grouped, (0, 2, 1, 3)).reshape(
        quarter_rows, col_count, data_count * owner_rows
    )
    regrouped = lax.all_to_all(grouped, "col", split_axis=1, concat_axis=0, tiled=True)
    regrouped = regrouped.reshape(quarter_rows * col_count, data_count * owner_rows)
    shard_sketch = lax.all_gather(sketch, "col", axis=0, tiled=True)
    projected = lax.psum_scatter(
        contract(regrouped, shard_sketch), "dp", scatter_dimension=0, tiled=True
    )
    projected = projected / jnp.float32(total_tokens)
    new_momentum = 0.8 * momentum + 0.2 * projected
    row_block = lax.all_gather(new_momentum, "col", axis=0, tiled=True)
    dense_grad = (
        lax.dot_general(
            row_block,
            sign_block,
            (((1,), (1,)), ((), ())),
            precision=lax.Precision.HIGHEST,
            preferred_element_type=jnp.float32,
        )
        * inv_root
    )
    new_second = 0.95 * second + 0.05 * dense_grad * dense_grad
    new_weight = weight - 0.5 * dense_grad / (jnp.sqrt(new_second) + 1e-08)
    return (new_weight, new_second, new_momentum)


def params(vmem=56 * 1024 * 1024, axes=1):
    return pltpu.CompilerParams(
        dimension_semantics=("arbitrary",) * axes, vmem_limit_bytes=vmem
    )


def pack_kernel(groups, width, part, og_ref, *refs):
    n_out = len(groups)
    outs = refs[:n_out]
    stage, in_sem, out_sem = refs[n_out:]
    me = lax.axis_index("dp") * lax.axis_size("col") + lax.axis_index("col")
    loads = []
    slot = 0
    for group in groups:
        mine = []
        for rel, half in group:
            first = pl.multiple_of((me ^ rel) * width + half * part, part)
            copy = pltpu.make_async_copy(
                og_ref.at[:, pl.ds(first, part)], stage.at[slot], in_sem.at[slot]
            )
            copy.start()
            mine.append(copy)
            slot += 1
        loads.append(mine)
    stores = []
    slot = 0
    for index, group in enumerate(groups):
        for copy in loads[index]:
            copy.wait()
        store = pltpu.make_async_copy(
            stage.at[pl.ds(slot, len(group))], outs[index], out_sem.at[index]
        )
        store.start()
        stores.append(store)
        slot += len(group)
    for store in stores:
        store.wait()


def pack(out_grad, groups, width, part):
    rows = out_grad.shape[0]
    count = sum(len(group) for group in groups)
    hbm = pl.BlockSpec(memory_space=pl.ANY)
    return pl.pallas_call(
        functools.partial(pack_kernel, groups, width, part),
        in_specs=[hbm],
        out_specs=[hbm] * len(groups),
        out_shape=[
            jax.ShapeDtypeStruct((len(group), rows, part), out_grad.dtype) for group in groups
        ],
        scratch_shapes=[
            pltpu.VMEM((count, rows, part), out_grad.dtype),
            pltpu.SemaphoreType.DMA((count,)),
            pltpu.SemaphoreType.DMA((len(groups),)),
        ],
        compiler_params=pltpu.CompilerParams(vmem_limit_bytes=8 * 1024 * 1024),
        cost_estimate=pl.CostEstimate(
            flops=0, bytes_accessed=4 * count * rows * part, transcendentals=0
        ),
        name="pack",
    )(pltpu.with_memory_space_constraint(out_grad, pltpu.HBM))


CHUNKS = 4
STRIP = 32


def sketch_kernel(first, din_local, *refs):
    if first:
        seed_ref, step_ref, *refs, seed, step, seed_sem = refs
        seed_copies = [
            pltpu.make_async_copy(seed_ref, seed, seed_sem.at[0]),
            pltpu.make_async_copy(step_ref, step, seed_sem.at[1]),
        ]
        for copy in seed_copies:
            copy.start()
        tok_ref, signs_ref, send_ref, keep_ref, tok, acc, sem = refs
    else:
        tok_ref, signs_ref, send_ref, keep_ref, tok, acc, sem = refs
    quarter, low_rank = keep_ref.shape
    chunk = din_local // CHUNKS
    col = lax.axis_index("col")
    group = col ^ (X if first else 0)
    loads = []
    for part in range(CHUNKS):
        at = pl.ds(part * chunk, chunk)
        mine = []
        for slot, rel in enumerate((CORE, 0)):
            rows = pl.ds(pl.multiple_of((group ^ rel) * quarter, quarter), quarter)
            copy = pltpu.make_async_copy(
                tok_ref.at[rows, at],
                tok.at[pl.ds(slot * quarter, quarter), at],
                sem.at[part, slot],
            )
            copy.start()
            mine.append(copy)
        loads.append(mine)
    if first:
        row_factor = low_rank * 747796405
        row_factor = (row_factor + (1 << 31)) % (1 << 32) - (1 << 31)
        local = lax.broadcasted_iota(jnp.int32, (STRIP, low_rank), 0) * row_factor
        columns = lax.broadcasted_iota(jnp.int32, (1, low_rank), 1) * 747796405
        for copy in seed_copies:
            copy.wait()
        columns = columns + (seed[...] * 1664525 + step[...] * 1013904223)
        local = local + columns
    for part in range(CHUNKS):
        at = slice(part * chunk, (part + 1) * chunk)
        if first:
            for row in range(part * chunk, (part + 1) * chunk, STRIP):
                mixed = local + (col * din_local + row) * row_factor
                strip = jnp.where(low_bits(mixed) == 0, 1.0, -1.0)
                signs_ref[row : row + STRIP, :] = strip.astype(jnp.bfloat16)
        for copy in loads[part]:
            copy.wait()
        product = jnp.dot(tok[:, at], signs_ref[at, :], preferred_element_type=jnp.float32)
        if part > 0:
            product += acc[...]
        if part < CHUNKS - 1:
            acc[...] = product
        else:
            send_ref[...] = product[:quarter]
            keep_ref[...] = product[quarter:]


def sketch_parts(tokens, low_rank, signs, seeds):
    local_tokens, din_local = tokens.shape
    half = local_tokens // 2
    quarter = half // 2
    first = signs is None
    vmem = pl.BlockSpec(memory_space=pltpu.VMEM)
    hbm = pl.BlockSpec(memory_space=pl.ANY)
    parts = [jax.ShapeDtypeStruct((quarter, low_rank), jnp.float32)] * 2
    tokens = pltpu.with_memory_space_constraint(tokens, pltpu.HBM)
    if first:
        in_specs, args = [hbm, hbm, hbm], (*seeds, tokens)
        out_shape = [jax.ShapeDtypeStruct((din_local, low_rank), jnp.bfloat16)] + parts
    else:
        in_specs, args = [hbm, vmem], (tokens, signs)
        out_shape = parts
    return pl.pallas_call(
        functools.partial(sketch_kernel, first, din_local),
        in_specs=in_specs,
        out_specs=[vmem] * len(out_shape),
        out_shape=out_shape,
        scratch_shapes=[
            pltpu.VMEM((half, din_local), tokens.dtype),
            pltpu.VMEM((half, low_rank), jnp.float32),
            pltpu.SemaphoreType.DMA((CHUNKS, 2)),
        ]
        + ([pltpu.VMEM((1, 1), jnp.int32)] * 2 + [pltpu.SemaphoreType.DMA((2,))]) * first,
        compiler_params=pltpu.CompilerParams(vmem_limit_bytes=12 * 1024 * 1024),
        cost_estimate=pl.CostEstimate(
            flops=2 * half * din_local * low_rank,
            bytes_accessed=half * din_local * 2 + din_local * low_rank * 2 + 2 * half * low_rank * 4,
            transcendentals=0,
        ),
        name="sketch",
    )(*args)


def project_kernel(n, *refs):
    send_ref, keep_ref = refs[-2:]
    count, _, part = refs[n].shape
    sketch = jnp.concatenate([ref[...] for ref in refs[:n]], axis=0)
    grads = jnp.concatenate(
        [
            jnp.concatenate([ref[j] for j in range(count)], axis=1)
            for ref in refs[n : 2 * n]
        ],
        axis=0,
    )
    total = contract(grads, sketch)
    away = send_ref.shape[0]
    for j in range(count):
        out_ref, at = (send_ref, j) if j < away else (keep_ref, j - away)
        out_ref[at] = total[j * part : (j + 1) * part]


def project(sketches, grads, offsets, count, away):
    rows, low_rank = sketches[0].shape
    part = grads[0].shape[2]
    n = len(sketches)

    def block_at(offset):
        return pl.BlockSpec((count, rows, part), lambda i: (offset // count, 0, 0))

    shapes = [(away, part, low_rank), (count - away, part, low_rank)]
    return pl.pallas_call(
        functools.partial(project_kernel, n),
        grid=(1,),
        in_specs=[pl.BlockSpec((rows, low_rank), lambda i: (0, 0))] * n
        + [block_at(offset) for offset in offsets],
        out_specs=[pl.BlockSpec(shape, lambda i: (0, 0, 0)) for shape in shapes],
        out_shape=[jax.ShapeDtypeStruct(shape, jnp.float32) for shape in shapes],
        compiler_params=params(10 * 1024 * 1024),
        cost_estimate=pl.CostEstimate(
            flops=2 * n * count * rows * part * low_rank,
            bytes_accessed=n * (rows * low_rank + count * rows * part) * 2
            + count * low_rank * part * 4,
            transcendentals=0,
        ),
        name="project",
    )(*sketches, *grads)


def prefetch_kernel(*refs):
    n = (len(refs) - 1) // 2
    sources, targets, sem = refs[:n], refs[n : 2 * n], refs[-1]
    pieces = sem.shape[1]
    copies = []
    for at in range(pieces):
        for k, (source, target) in enumerate(zip(sources, targets)):
            rows = source.shape[0] // pieces
            window = pl.ds(at * rows, rows)
            copy = pltpu.make_async_copy(source.at[window], target.at[window], sem.at[k, at])
            copy.start()
            copies.append(copy)
    for copy in copies:
        copy.wait()


def prefetch(*arrays):
    n = len(arrays)
    size = sum(array.size * array.dtype.itemsize for array in arrays)
    return pl.pallas_call(
        prefetch_kernel,
        in_specs=[pl.BlockSpec(memory_space=pl.ANY)] * n,
        out_specs=[pl.BlockSpec(memory_space=pltpu.VMEM)] * n,
        out_shape=[jax.ShapeDtypeStruct(array.shape, array.dtype) for array in arrays],
        scratch_shapes=[pltpu.SemaphoreType.DMA((n, 4))],
        compiler_params=pltpu.CompilerParams(vmem_limit_bytes=size + 2 * 1024 * 1024),
        cost_estimate=pl.CostEstimate(flops=0, bytes_accessed=size, transcendentals=0),
        name="prefetch",
    )(*[pltpu.with_memory_space_constraint(array, pltpu.HBM) for array in arrays])


def update_kernel(where, keep, slabs, tile, *refs):
    n = len(where)
    rows_refs = refs[:n]
    signs_ref, weight_ref, second_ref = refs[n : n + 3]
    new_weight_ref, new_second_ref, new_momentum_ref = refs[-7:-4]
    nw_buf, ns_buf, out_sem, keep_sem = refs[-4:]
    part, low_rank = rows_refs[0].shape
    width = signs_ref.shape[0]
    slab = width // slabs
    gain = math.sqrt(0.05) / math.sqrt(low_rank)
    back = 0.5 / math.sqrt(0.05)
    nt = (((1,), (1,)), ((), ()))
    col = lax.axis_index("col")
    firsts = [pl.multiple_of(((col ^ rel) * 2 + half) * part, part) for rel, half in where]
    stores = []
    if keep:
        half = where[0][1]
        store = pltpu.make_async_copy(
            rows_refs[0], new_momentum_ref.at[pl.ds(half * part, part)], keep_sem.at[0]
        )
        store.start()
        stores.append(store)
    rows = jnp.concatenate([ref[...] for ref in rows_refs], axis=0) * gain
    high = rows.astype(jnp.bfloat16)
    low = (rows - high.astype(jnp.float32)).astype(jnp.bfloat16)
    for k in range(slabs):
        for at in range(k * slab, (k + 1) * slab, tile):
            signs = signs_ref[at : at + tile, :]
            dense = lax.dot_general(high, signs, nt, preferred_element_type=jnp.float32)
            dense += lax.dot_general(low, signs, nt, preferred_element_type=jnp.float32)
            columns = slice(at - k * slab, at - k * slab + tile)
            for b in range(n):
                mine = dense[b * part : (b + 1) * part]
                here = (pl.ds(firsts[b], part), slice(at, at + tile))
                new_second = 0.95 * second_ref[here] + mine * mine
                bottom = new_second * lax.rsqrt(new_second) + 1e-08
                inverse = pl.reciprocal(bottom, approx=True)
                inverse = inverse * (2.0 - bottom * inverse)
                ns_buf[k * n + b, :, columns] = new_second
                nw_buf[k * n + b, :, columns] = weight_ref[here] - (mine * back) * inverse
        for b in range(n):
            slot = k * n + b
            window = (pl.ds(firsts[b], part), pl.ds(k * slab, slab))
            for kind, (buf, ref) in enumerate(
                ((nw_buf, new_weight_ref), (ns_buf, new_second_ref))
            ):
                store = pltpu.make_async_copy(
                    buf.at[slot], ref.at[window], out_sem.at[kind, slot]
                )
                store.start()
                stores.append(store)
    for store in stores:
        store.wait()


def update(row_blocks, where, keep, signs, weight, second, onto):
    part, low_rank = row_blocks[0].shape
    din_local = weight.shape[1]
    n = len(row_blocks)
    slabs = 4
    slab = din_local // slabs
    hbm = pl.BlockSpec(memory_space=pl.ANY)
    vmem = pl.BlockSpec(memory_space=pltpu.VMEM)
    in_specs = [vmem] * (n + 3)
    aliases = {}
    if onto:
        in_specs += [hbm] * 3
        aliases = {n + 3 + k: k for k in range(3)}
    size = n * part * din_local
    buf = pltpu.VMEM((slabs * n, part, slab), jnp.float32)
    return pl.pallas_call(
        functools.partial(update_kernel, where, keep, slabs, min(slab, 256)),
        in_specs=in_specs,
        out_specs=[hbm] * 3,
        out_shape=[
            jax.ShapeDtypeStruct(weight.shape, jnp.float32),
            jax.ShapeDtypeStruct(second.shape, jnp.float32),
            jax.ShapeDtypeStruct((2 * part, low_rank), jnp.float32),
        ],
        scratch_shapes=[
            buf,
            buf,
            pltpu.SemaphoreType.DMA((2, slabs * n)),
            pltpu.SemaphoreType.DMA((1,)),
        ],
        input_output_aliases=aliases,
        compiler_params=pltpu.CompilerParams(
            vmem_limit_bytes=8 * size + 8 * 1024 * 1024
        ),
        cost_estimate=pl.CostEstimate(
            flops=4 * size * low_rank, bytes_accessed=8 * size, transcendentals=2 * size
        ),
        name="update",
    )(*row_blocks, signs, weight, second, *onto)


CORE, X, Y, Z0, Z1 = 1, 2, 4, 8, 16


def exchange(value, mask):
    size = lax.axis_size("dp") * lax.axis_size("col")
    return lax.ppermute(value, AXES, [(i, i ^ mask) for i in range(size)])


def stepped(tokens, out_grad, weight, second, momentum, sign_seed, step_number):
    low_rank = momentum.shape[1]
    owner_rows = momentum.shape[0]
    total_tokens = lax.axis_size("dp") * tokens.shape[0]
    inv_root = 1.0 / jnp.sqrt(jnp.float32(low_rank))
    far0 = [(Z1 | X | Z0, 0), (Z1 | X, 0), (Z1 | Z0, 0), (Z1, 0)]
    near0 = [(Z0 | X, 0), (X, 0), (Z0, 0), (0, 0)]
    far1 = [(Z1 | Y | X, 1), (Z1 | Y, 1), (Z1 | X, 1), (Z1, 1)]
    near1 = [(Y | X, 1), (Y, 1), (X, 1), (0, 1)]

    def toward(mask, pieces):
        return [(rel ^ mask, half) for rel, half in pieces]

    part = owner_rows // 2
    over_y, over_z = far0 + near0, far1 + near1
    og_y, og_z = pack(out_grad, [toward(Y, over_y), toward(Z0, over_z)], owner_rows, part)
    og_y = exchange(og_y, Y)
    og_z = exchange(og_z, Z0)
    seeds = (sign_seed.reshape(1, 1), step_number.reshape(1, 1))
    signs, send_a, keep_a = sketch_parts(tokens, low_rank, None, seeds)
    got_a = exchange(send_a, CORE)
    og_yc, og_zc = pack(
        out_grad, [toward(Y | CORE, over_y), toward(Z0 | CORE, over_z)], owner_rows, part
    )
    og_c, og_own = pack(
        out_grad,
        [toward(CORE, over_y + over_z), over_y + over_z],
        owner_rows,
        part,
    )
    across = exchange(keep_a + got_a, X)
    og_yc = exchange(og_yc, Y | CORE)
    og_zc = exchange(og_zc, Z0 | CORE)
    og_c = exchange(og_c, CORE)
    send_b, keep_b = sketch_parts(tokens, low_rank, signs, None)
    got_b = exchange(send_b, CORE)
    (weight_v,) = prefetch(weight)
    (second_v,) = prefetch(second)
    sketch = (((keep_b + got_b) + across) * inv_root).astype(jnp.bfloat16)

    sk_y = exchange(sketch, Y)
    sk_z = exchange(sketch, Z0)
    sk_c = exchange(sketch, CORE)
    sk_yc = exchange(sk_y, CORE)
    sk_zc = exchange(sk_z, CORE)

    scale = jnp.float32(1.0 / total_tokens)

    def packed(value, extra):
        return (value * (scale * extra)).astype(jnp.float16)

    def unpacked(value, extra):
        return value.astype(jnp.float32) * (1.0 / (scale * extra))

    y_side = (sketch, sk_c, sk_y, sk_yc), (og_own, og_c, og_y, og_yc)
    z_side = (sketch, sk_c, sk_z, sk_zc), (og_own, og_c, og_z, og_zc)

    def direct(terms, offsets, masks):
        send, keep = project(*terms, offsets, 4, 3)
        total = keep[0]
        for at, mask in enumerate(masks):
            got = exchange(packed(send[at], 8.0), mask)
            total += unpacked(got, 8.0)
        return total

    far0_total = direct(y_side, (0, 0, 0, 0), (X | Z0, X, Z0))
    far1_total = direct(z_side, (8, 8, 0, 0), (Y | X, Y, X))
    near0_total = direct(y_side, (4, 4, 4, 4), (X | Z0, X, Z0))
    near1_total = direct(z_side, (12, 12, 4, 4), (Y | X, Y, X))
    last0 = exchange(packed(far0_total, 2.0), Z1)
    far1_small = packed(far1_total, 2.0)
    last1 = exchange(far1_small, Z1)

    def momentum_half(half, near, last):
        projected = (near + unpacked(last, 2.0)) * scale
        return 0.8 * momentum[half * part : (half + 1) * part] + 0.2 * projected

    halves, others = [], []
    small = None
    for half, near, last in ((0, near0_total, last0), (1, near1_total, last1)):
        if small is not None:
            last, _ = lax.optimization_barrier((last, small))
        mine = momentum_half(half, near, last)
        small = mine.astype(jnp.float16)
        from_core = exchange(small, CORE)
        from_x = exchange(small, X)
        from_xc = exchange(from_x, CORE)
        halves.append(mine)
        others.append([v.astype(jnp.float32) for v in (from_core, from_x, from_xc)])
    done = ()
    near, far = (0, CORE), (X, X | CORE)
    for half, rows, relatives in (
        (0, (halves[0], others[0][0]), near),
        (1, (halves[1], others[1][0]), near),
        (0, others[0][1:], far),
        (1, others[1][1:], far),
    ):
        where = [(rel, half) for rel in relatives]
        keep = where[0][0] == 0
        done = update(rows, tuple(where), keep, signs, weight_v, second_v, tuple(done))
    return tuple(done)


def solution(mesh):
    placed = (
        P("dp", "col"),
        P(AXES, None),
        P("dp", "col"),
        P("dp", "col"),
        P(AXES, None),
        P(),
        P(),
    )

    def per_device(tokens, out_grad, weight, second, momentum, sign_seed, step_number):
        args = (tokens, out_grad, weight, second, momentum, sign_seed, step_number)
        cube = mesh.shape["dp"] == Z1 * 2 // (X * 2) and mesh.shape["col"] == X * 2
        if cube and momentum.shape[0] % (2 * LANES) == 0:
            return stepped(*args)
        return general(*args)

    return jax.shard_map(
        per_device,
        mesh=mesh,
        in_specs=placed,
        out_specs=(P("dp", "col"), P("dp", "col"), P(AXES, None)),
        check_vma=False,
    )
```

```python
import functools
import math

import jax
import jax.numpy as jnp
from jax import lax
from jax.experimental import pallas as pl
from jax.experimental.pallas import tpu as pltpu
from jax.sharding import PartitionSpec as P


AXES = ("dp", "col")
LANES = 128


def low_bits(mixed):
    mixed = mixed ^ lax.shift_right_logical(mixed, 16)
    mixed = mixed * 2127912213
    mixed = mixed ^ lax.shift_right_logical(mixed, 13)
    mixed = mixed * 1103515245
    mixed = mixed ^ lax.shift_right_logical(mixed, 16)
    return mixed & (1 << 20)


def sign_table(sign_seed, step_number, first_row, row_count, low_rank):
    row_ids = first_row + lax.iota(jnp.int32, row_count)
    col_ids = lax.iota(jnp.int32, low_rank)
    flat_index = row_ids[:, None] * low_rank + col_ids[None, :]
    seeded = sign_seed[0] * 1664525 + step_number[0] * 1013904223
    return jnp.where(low_bits(flat_index * 747796405 + seeded) == 0, 1.0, -1.0)


def contract(left_rows, right_rows):
    return lax.dot_general(
        left_rows, right_rows, (((0,), (0,)), ((), ())), preferred_element_type=jnp.float32
    )


def general(tokens, out_grad, weight, second, momentum, sign_seed, step_number):
    local_tokens, din_local = tokens.shape
    low_rank = momentum.shape[1]
    owner_rows = momentum.shape[0]
    inv_root = 1.0 / jnp.sqrt(jnp.float32(low_rank))
    col_position = lax.axis_index("col")
    sign_block = sign_table(sign_seed, step_number, col_position * din_local, din_local, low_rank)
    partial_sketch = (
        jnp.dot(tokens, sign_block.astype(jnp.bfloat16), preferred_element_type=jnp.float32)
        * inv_root
    )
    quarter = lax.psum_scatter(partial_sketch, "col", scatter_dimension=0, tiled=True)
    sketch = quarter.astype(jnp.bfloat16)
    total_tokens = lax.axis_size("dp") * local_tokens
    data_count = lax.axis_size("dp")
    col_count = lax.axis_size("col")
    quarter_rows = out_grad.shape[0]
    grouped = out_grad.reshape(quarter_rows, data_count, col_count, owner_rows)
    grouped = jnp.transpose(grouped, (0, 2, 1, 3)).reshape(
        quarter_rows, col_count, data_count * owner_rows
    )
    regrouped = lax.all_to_all(grouped, "col", split_axis=1, concat_axis=0, tiled=True)
    regrouped = regrouped.reshape(quarter_rows * col_count, data_count * owner_rows)
    shard_sketch = lax.all_gather(sketch, "col", axis=0, tiled=True)
    projected = lax.psum_scatter(
        contract(regrouped, shard_sketch), "dp", scatter_dimension=0, tiled=True
    )
    projected = projected / jnp.float32(total_tokens)
    new_momentum = 0.8 * momentum + 0.2 * projected
    row_block = lax.all_gather(new_momentum, "col", axis=0, tiled=True)
    dense_grad = (
        lax.dot_general(
            row_block,
            sign_block,
            (((1,), (1,)), ((), ())),
            precision=lax.Precision.HIGHEST,
            preferred_element_type=jnp.float32,
        )
        * inv_root
    )
    new_second = 0.95 * second + 0.05 * dense_grad * dense_grad
    new_weight = weight - 0.5 * dense_grad / (jnp.sqrt(new_second) + 1e-08)
    return (new_weight, new_second, new_momentum)


def params(vmem=56 * 1024 * 1024, axes=1):
    return pltpu.CompilerParams(
        dimension_semantics=("arbitrary",) * axes, vmem_limit_bytes=vmem
    )


def pack_kernel(groups, width, part, og_ref, *refs):
    n_out = len(groups)
    outs = refs[:n_out]
    stage, in_sem, out_sem = refs[n_out:]
    me = lax.axis_index("dp") * lax.axis_size("col") + lax.axis_index("col")
    loads = []
    slot = 0
    for group in groups:
        mine = []
        for rel, half in group:
            first = pl.multiple_of((me ^ rel) * width + half * part, part)
            copy = pltpu.make_async_copy(
                og_ref.at[:, pl.ds(first, part)], stage.at[slot], in_sem.at[slot]
            )
            copy.start()
            mine.append(copy)
            slot += 1
        loads.append(mine)
    stores = []
    slot = 0
    for index, group in enumerate(groups):
        for copy in loads[index]:
            copy.wait()
        store = pltpu.make_async_copy(
            stage.at[pl.ds(slot, len(group))], outs[index], out_sem.at[index]
        )
        store.start()
        stores.append(store)
        slot += len(group)
    for store in stores:
        store.wait()


def pack(out_grad, groups, width, part):
    rows = out_grad.shape[0]
    count = sum(len(group) for group in groups)
    hbm = pl.BlockSpec(memory_space=pl.ANY)
    return pl.pallas_call(
        functools.partial(pack_kernel, groups, width, part),
        in_specs=[hbm],
        out_specs=[hbm] * len(groups),
        out_shape=[
            jax.ShapeDtypeStruct((len(group), rows, part), out_grad.dtype) for group in groups
        ],
        scratch_shapes=[
            pltpu.VMEM((count, rows, part), out_grad.dtype),
            pltpu.SemaphoreType.DMA((count,)),
            pltpu.SemaphoreType.DMA((len(groups),)),
        ],
        compiler_params=pltpu.CompilerParams(vmem_limit_bytes=8 * 1024 * 1024),
        cost_estimate=pl.CostEstimate(
            flops=0, bytes_accessed=4 * count * rows * part, transcendentals=0
        ),
        name="pack",
    )(pltpu.with_memory_space_constraint(out_grad, pltpu.HBM))


CHUNKS = 4
STRIP = 32


def sketch_kernel(first, din_local, *refs):
    if first:
        seed_ref, step_ref, *refs, seed, step, seed_sem = refs
        seed_copies = [
            pltpu.make_async_copy(seed_ref, seed, seed_sem.at[0]),
            pltpu.make_async_copy(step_ref, step, seed_sem.at[1]),
        ]
        for copy in seed_copies:
            copy.start()
        tok_ref, signs_ref, send_ref, keep_ref, tok, acc, sem = refs
    else:
        tok_ref, signs_ref, send_ref, keep_ref, tok, acc, sem = refs
    quarter, low_rank = keep_ref.shape
    chunk = din_local // CHUNKS
    col = lax.axis_index("col")
    group = col ^ (X if first else 0)
    loads = []
    for part in range(CHUNKS):
        at = pl.ds(part * chunk, chunk)
        mine = []
        for slot, rel in enumerate((CORE, 0)):
            rows = pl.ds(pl.multiple_of((group ^ rel) * quarter, quarter), quarter)
            copy = pltpu.make_async_copy(
                tok_ref.at[rows, at],
                tok.at[pl.ds(slot * quarter, quarter), at],
                sem.at[part, slot],
            )
            copy.start()
            mine.append(copy)
        loads.append(mine)
    if first:
        row_factor = low_rank * 747796405
        row_factor = (row_factor + (1 << 31)) % (1 << 32) - (1 << 31)
        local = lax.broadcasted_iota(jnp.int32, (STRIP, low_rank), 0) * row_factor
        columns = lax.broadcasted_iota(jnp.int32, (1, low_rank), 1) * 747796405
        for copy in seed_copies:
            copy.wait()
        columns = columns + (seed[...] * 1664525 + step[...] * 1013904223)
        local = local + columns
    for part in range(CHUNKS):
        at = slice(part * chunk, (part + 1) * chunk)
        if first:
            for row in range(part * chunk, (part + 1) * chunk, STRIP):
                mixed = local + (col * din_local + row) * row_factor
                strip = jnp.where(low_bits(mixed) == 0, 1.0, -1.0)
                signs_ref[row : row + STRIP, :] = strip.astype(jnp.bfloat16)
        for copy in loads[part]:
            copy.wait()
        product = jnp.dot(tok[:, at], signs_ref[at, :], preferred_element_type=jnp.float32)
        if part > 0:
            product += acc[...]
        if part < CHUNKS - 1:
            acc[...] = product
        else:
            send_ref[...] = product[:quarter]
            keep_ref[...] = product[quarter:]


def sketch_parts(tokens, low_rank, signs, seeds):
    local_tokens, din_local = tokens.shape
    half = local_tokens // 2
    quarter = half // 2
    first = signs is None
    vmem = pl.BlockSpec(memory_space=pltpu.VMEM)
    hbm = pl.BlockSpec(memory_space=pl.ANY)
    parts = [jax.ShapeDtypeStruct((quarter, low_rank), jnp.float32)] * 2
    tokens = pltpu.with_memory_space_constraint(tokens, pltpu.HBM)
    if first:
        in_specs, args = [hbm, hbm, hbm], (*seeds, tokens)
        out_shape = [jax.ShapeDtypeStruct((din_local, low_rank), jnp.bfloat16)] + parts
    else:
        in_specs, args = [hbm, vmem], (tokens, signs)
        out_shape = parts
    return pl.pallas_call(
        functools.partial(sketch_kernel, first, din_local),
        in_specs=in_specs,
        out_specs=[vmem] * len(out_shape),
        out_shape=out_shape,
        scratch_shapes=[
            pltpu.VMEM((half, din_local), tokens.dtype),
            pltpu.VMEM((half, low_rank), jnp.float32),
            pltpu.SemaphoreType.DMA((CHUNKS, 2)),
        ]
        + ([pltpu.VMEM((1, 1), jnp.int32)] * 2 + [pltpu.SemaphoreType.DMA((2,))]) * first,
        compiler_params=pltpu.CompilerParams(vmem_limit_bytes=12 * 1024 * 1024),
        cost_estimate=pl.CostEstimate(
            flops=2 * half * din_local * low_rank,
            bytes_accessed=half * din_local * 2 + din_local * low_rank * 2 + 2 * half * low_rank * 4,
            transcendentals=0,
        ),
        name="sketch",
    )(*args)


def project_kernel(n, *refs):
    send_ref, keep_ref = refs[-2:]
    count, _, part = refs[n].shape
    sketch = jnp.concatenate([ref[...] for ref in refs[:n]], axis=0)
    grads = jnp.concatenate(
        [
            jnp.concatenate([ref[j] for j in range(count)], axis=1)
            for ref in refs[n : 2 * n]
        ],
        axis=0,
    )
    total = contract(grads, sketch)
    for j in range(count):
        out_ref = send_ref if j < count // 2 else keep_ref
        out_ref[j % (count // 2)] = total[j * part : (j + 1) * part]


def project(sketches, grads, offsets, count):
    rows, low_rank = sketches[0].shape
    part = grads[0].shape[2]
    n = len(sketches)

    def block_at(offset):
        return pl.BlockSpec((count, rows, part), lambda i: (offset // count, 0, 0))

    out = jax.ShapeDtypeStruct((count // 2, part, low_rank), jnp.float32)
    return pl.pallas_call(
        functools.partial(project_kernel, n),
        grid=(1,),
        in_specs=[pl.BlockSpec((rows, low_rank), lambda i: (0, 0))] * n
        + [block_at(offset) for offset in offsets],
        out_specs=[pl.BlockSpec((count // 2, part, low_rank), lambda i: (0, 0, 0))] * 2,
        out_shape=[out] * 2,
        compiler_params=params(10 * 1024 * 1024),
        cost_estimate=pl.CostEstimate(
            flops=2 * n * count * rows * part * low_rank,
            bytes_accessed=n * (rows * low_rank + count * rows * part) * 2
            + count * low_rank * part * 4,
            transcendentals=0,
        ),
        name="project",
    )(*sketches, *grads)


def prefetch_kernel(*refs):
    n = (len(refs) - 1) // 2
    sources, targets, sem = refs[:n], refs[n : 2 * n], refs[-1]
    pieces = sem.shape[1]
    copies = []
    for at in range(pieces):
        for k, (source, target) in enumerate(zip(sources, targets)):
            rows = source.shape[0] // pieces
            window = pl.ds(at * rows, rows)
            copy = pltpu.make_async_copy(source.at[window], target.at[window], sem.at[k, at])
            copy.start()
            copies.append(copy)
    for copy in copies:
        copy.wait()


def prefetch(*arrays):
    n = len(arrays)
    size = sum(array.size * array.dtype.itemsize for array in arrays)
    return pl.pallas_call(
        prefetch_kernel,
        in_specs=[pl.BlockSpec(memory_space=pl.ANY)] * n,
        out_specs=[pl.BlockSpec(memory_space=pltpu.VMEM)] * n,
        out_shape=[jax.ShapeDtypeStruct(array.shape, array.dtype) for array in arrays],
        scratch_shapes=[pltpu.SemaphoreType.DMA((n, 4))],
        compiler_params=pltpu.CompilerParams(vmem_limit_bytes=size + 2 * 1024 * 1024),
        cost_estimate=pl.CostEstimate(flops=0, bytes_accessed=size, transcendentals=0),
        name="prefetch",
    )(*[pltpu.with_memory_space_constraint(array, pltpu.HBM) for array in arrays])


def update_kernel(where, keep, slabs, tile, *refs):
    n = len(where)
    rows_refs = refs[:n]
    signs_ref, weight_ref, second_ref = refs[n : n + 3]
    new_weight_ref, new_second_ref, new_momentum_ref = refs[-7:-4]
    nw_buf, ns_buf, out_sem, keep_sem = refs[-4:]
    part, low_rank = rows_refs[0].shape
    width = signs_ref.shape[0]
    slab = width // slabs
    gain = math.sqrt(0.05) / math.sqrt(low_rank)
    back = 0.5 / math.sqrt(0.05)
    nt = (((1,), (1,)), ((), ()))
    col = lax.axis_index("col")
    firsts = [pl.multiple_of(((col ^ rel) * 2 + half) * part, part) for rel, half in where]
    stores = []
    if keep:
        half = where[0][1]
        store = pltpu.make_async_copy(
            rows_refs[0], new_momentum_ref.at[pl.ds(half * part, part)], keep_sem.at[0]
        )
        store.start()
        stores.append(store)
    rows = jnp.concatenate([ref[...] for ref in rows_refs], axis=0) * gain
    high = rows.astype(jnp.bfloat16)
    low = (rows - high.astype(jnp.float32)).astype(jnp.bfloat16)
    for k in range(slabs):
        for at in range(k * slab, (k + 1) * slab, tile):
            signs = signs_ref[at : at + tile, :]
            dense = lax.dot_general(high, signs, nt, preferred_element_type=jnp.float32)
            dense += lax.dot_general(low, signs, nt, preferred_element_type=jnp.float32)
            columns = slice(at - k * slab, at - k * slab + tile)
            for b in range(n):
                mine = dense[b * part : (b + 1) * part]
                here = (pl.ds(firsts[b], part), slice(at, at + tile))
                new_second = 0.95 * second_ref[here] + mine * mine
                bottom = new_second * lax.rsqrt(new_second) + 1e-08
                inverse = pl.reciprocal(bottom, approx=True)
                inverse = inverse * (2.0 - bottom * inverse)
                ns_buf[k * n + b, :, columns] = new_second
                nw_buf[k * n + b, :, columns] = weight_ref[here] - (mine * back) * inverse
        for b in range(n):
            slot = k * n + b
            window = (pl.ds(firsts[b], part), pl.ds(k * slab, slab))
            for kind, (buf, ref) in enumerate(
                ((nw_buf, new_weight_ref), (ns_buf, new_second_ref))
            ):
                store = pltpu.make_async_copy(
                    buf.at[slot], ref.at[window], out_sem.at[kind, slot]
                )
                store.start()
                stores.append(store)
    for store in stores:
        store.wait()


def update(row_blocks, where, keep, signs, weight, second, onto):
    part, low_rank = row_blocks[0].shape
    din_local = weight.shape[1]
    n = len(row_blocks)
    slabs = 4
    slab = din_local // slabs
    hbm = pl.BlockSpec(memory_space=pl.ANY)
    vmem = pl.BlockSpec(memory_space=pltpu.VMEM)
    in_specs = [vmem] * (n + 3)
    aliases = {}
    if onto:
        in_specs += [hbm] * 3
        aliases = {n + 3 + k: k for k in range(3)}
    size = n * part * din_local
    buf = pltpu.VMEM((slabs * n, part, slab), jnp.float32)
    return pl.pallas_call(
        functools.partial(update_kernel, where, keep, slabs, min(slab, 256)),
        in_specs=in_specs,
        out_specs=[hbm] * 3,
        out_shape=[
            jax.ShapeDtypeStruct(weight.shape, jnp.float32),
            jax.ShapeDtypeStruct(second.shape, jnp.float32),
            jax.ShapeDtypeStruct((2 * part, low_rank), jnp.float32),
        ],
        scratch_shapes=[
            buf,
            buf,
            pltpu.SemaphoreType.DMA((2, slabs * n)),
            pltpu.SemaphoreType.DMA((1,)),
        ],
        input_output_aliases=aliases,
        compiler_params=pltpu.CompilerParams(
            vmem_limit_bytes=8 * size + 8 * 1024 * 1024
        ),
        cost_estimate=pl.CostEstimate(
            flops=4 * size * low_rank, bytes_accessed=8 * size, transcendentals=2 * size
        ),
        name="update",
    )(*row_blocks, signs, weight, second, *onto)


CORE, X, Y, Z0, Z1 = 1, 2, 4, 8, 16


def exchange(value, mask):
    size = lax.axis_size("dp") * lax.axis_size("col")
    return lax.ppermute(value, AXES, [(i, i ^ mask) for i in range(size)])


def stepped(tokens, out_grad, weight, second, momentum, sign_seed, step_number):
    low_rank = momentum.shape[1]
    owner_rows = momentum.shape[0]
    total_tokens = lax.axis_size("dp") * tokens.shape[0]
    inv_root = 1.0 / jnp.sqrt(jnp.float32(low_rank))
    far0 = [(Z1 | X | Z0, 0), (Z1 | X, 0), (Z1 | Z0, 0), (Z1, 0)]
    near0 = [(Z0 | X, 0), (Z0, 0), (X, 0), (0, 0)]
    far1 = [(Z1 | Y | X, 1), (Z1 | Y, 1), (Z1 | X, 1), (Z1, 1)]
    near1 = [(Y | X, 1), (Y, 1), (X, 1), (0, 1)]

    def toward(mask, pieces):
        return [(rel ^ mask, half) for rel, half in pieces]

    part = owner_rows // 2
    over_y, over_z = far0 + near0, far1 + near1
    og_y, og_z = pack(out_grad, [toward(Y, over_y), toward(Z0, over_z)], owner_rows, part)
    og_y = exchange(og_y, Y)
    og_z = exchange(og_z, Z0)
    seeds = (sign_seed.reshape(1, 1), step_number.reshape(1, 1))
    signs, send_a, keep_a = sketch_parts(tokens, low_rank, None, seeds)
    got_a = exchange(send_a, CORE)
    og_yc, og_zc = pack(
        out_grad, [toward(Y | CORE, over_y), toward(Z0 | CORE, over_z)], owner_rows, part
    )
    og_c, og_own = pack(
        out_grad,
        [toward(CORE, over_y + over_z), over_y + over_z],
        owner_rows,
        part,
    )
    across = exchange(keep_a + got_a, X)
    og_yc = exchange(og_yc, Y | CORE)
    og_zc = exchange(og_zc, Z0 | CORE)
    og_c = exchange(og_c, CORE)
    send_b, keep_b = sketch_parts(tokens, low_rank, signs, None)
    got_b = exchange(send_b, CORE)
    (weight_v,) = prefetch(weight)
    (second_v,) = prefetch(second)
    sketch = (((keep_b + got_b) + across) * inv_root).astype(jnp.bfloat16)

    sk_y = exchange(sketch, Y)
    sk_z = exchange(sketch, Z0)
    sk_c = exchange(sketch, CORE)
    sk_yc = exchange(sk_y, CORE)
    sk_zc = exchange(sk_z, CORE)

    scale = jnp.float32(1.0 / total_tokens)

    def packed(value, extra):
        return (value * (scale * extra)).astype(jnp.float16)

    def unpacked(value, extra):
        return value.astype(jnp.float32) * (1.0 / (scale * extra))

    y_side = (sketch, sk_c, sk_y, sk_yc), (og_own, og_c, og_y, og_yc)
    z_side = (sketch, sk_c, sk_z, sk_zc), (og_own, og_c, og_z, og_zc)

    def begin(terms, offsets, axis):
        send, keep = project(*terms, offsets, 4)
        return exchange(packed(send, 8.0), axis), keep

    def middle(state, axis):
        got, keep = state
        ahead = packed(keep[0] + unpacked(got[0], 8.0), 4.0)
        return exchange(ahead, axis), keep[1] + unpacked(got[1], 8.0)

    def finish(state):
        got, keep = state
        return keep + unpacked(got, 4.0)

    far0_state = begin(y_side, (0, 0, 0, 0), X)
    far1_state = begin(z_side, (8, 8, 0, 0), Y)
    near0_state = begin(y_side, (4, 4, 4, 4), Z0)
    near1_state = begin(z_side, (12, 12, 4, 4), Y)
    far0_state = middle(far0_state, Z0)
    far1_state = middle(far1_state, X)
    last0 = exchange(packed(finish(far0_state), 2.0), Z1)
    last1 = exchange(packed(finish(far1_state), 2.0), Z1)
    near0_state = middle(near0_state, X)
    near1_state = middle(near1_state, X)

    def momentum_half(half, near, last):
        projected = (near + unpacked(last, 2.0)) * scale
        return 0.8 * momentum[half * part : (half + 1) * part] + 0.2 * projected

    halves, others = [], []
    small = None
    for half, near_state, last in ((0, near0_state, last0), (1, near1_state, last1)):
        if small is not None:
            last, _ = lax.optimization_barrier((last, small))
        mine = momentum_half(half, finish(near_state), last)
        small = mine.astype(jnp.float16)
        from_core = exchange(small, CORE)
        from_x = exchange(small, X)
        from_xc = exchange(from_x, CORE)
        halves.append(mine)
        others.append([v.astype(jnp.float32) for v in (from_core, from_x, from_xc)])
    done = ()
    near, far = (0, CORE), (X, X | CORE)
    for half, rows, relatives in (
        (0, (halves[0], others[0][0]), near),
        (1, (halves[1], others[1][0]), near),
        (0, others[0][1:], far),
        (1, others[1][1:], far),
    ):
        where = tuple((rel, half) for rel in relatives)
        keep = where[0][0] == 0
        done = update(rows, where, keep, signs, weight_v, second_v, tuple(done))
    return tuple(done)


def solution(mesh):
    placed = (
        P("dp", "col"),
        P(AXES, None),
        P("dp", "col"),
        P("dp", "col"),
        P(AXES, None),
        P(),
        P(),
    )

    def per_device(tokens, out_grad, weight, second, momentum, sign_seed, step_number):
        args = (tokens, out_grad, weight, second, momentum, sign_seed, step_number)
        cube = mesh.shape["dp"] == Z1 * 2 // (X * 2) and mesh.shape["col"] == X * 2
        if cube and momentum.shape[0] % (2 * LANES) == 0:
            return stepped(*args)
        return general(*args)

    return jax.shard_map(
        per_device,
        mesh=mesh,
        in_specs=placed,
        out_specs=(P("dp", "col"), P("dp", "col"), P(AXES, None)),
        check_vma=False,
    )
```
